512 devices in a mesh: wide: 32 (over y, x), narrow: 16 (over z, core).
Axes of the slice: x: 4, y: 8, z: 8, core: 2. Of those that a mesh axis runs over, the one named last changes fastest.
Arguments:
- pops_in: float32 [2560, 19, 512], P(('wide', 'narrow')), may hold values from 0 to 1, as said below
- keep_slot: int32 [1536], P(('wide', 'narrow')), may hold values from -1 to 4, as said below
- send_slot: int32 [1024], P(('wide', 'narrow')), may hold values from -1 to 4, as said below
- send_dest: int32 [1024], P(('wide', 'narrow')), may hold values from -1 to 47, as said below
- neighbours: int32 [1536, 18], P(('wide', 'narrow')), may hold values from -1 to 143, as said below
- fluid: int32 [1536, 512], P(('wide', 'narrow')), may hold values 0 or 1
Outputs:
- populations: float32 [1536, 19, 512], P(('wide', 'narrow'))
The draws below stay inside these ranges and needn't reach their ends.
Inputs may be any that keep to these rules, and one draw needn't show every extreme that they name: Every block stays within its wide index. The blocks of one device that stay keep their populations; each slot after migration is filled at most once, by keep_slot or by one leaving block. Half of the devices of each wide index end with 3 blocks and half with one; empty slots get no neighbours. `send_slot`: A quarter of the devices of each wide index send exactly 2 blocks each, the others none; every sent block fills a slot that keep_slot leaves empty. Destinations lie on the same wide index as the sender and differ from it in narrow index; send_dest is -1 exactly where send_slot is. `neighbours`: direction j points along c_(j+1); a neighbour in a direction with first component o - 1 lies on wide index w + o - 1, none lies outside the wide range; the relation is symmetric and consistent with the slots after migration; each wide index holds 32 blocks. `pops_in`: positive populations near an equilibrium of density about one and small velocity.
All inputs are finite; a program needn't handle non-finite values. No bound on the sum of `fluid` on one device may be relied on, other than what follows from the above.
Results may differ from the reference program's by a relative error of at most 0.0003.
Values sent between devices are 32-bit elements; how exact they have to be, the bound alone decides.
No kernel may reach another device: no remote copies, remote signals or barrier semaphores. Data moves between devices by JAX's collectives and lax.ppermute only.
A program may use at most 128 MiB of HBM per device.

```python
import jax
import jax.numpy as jnp
import numpy as np
from jax import lax

EDGE = 8
CELLS = 512
HELD = 3
OUT_CAP = 2
SLOTS = 5
STEPS = 4
SLABS = 32
GROUP = 16
DEVICES = 512


VELOCITY_TABLE = np.array([[0, 0, 0], [1, 0, 0], [-1, 0, 0], [0, 1, 0], [0, -1, 0], [0, 0, 1], [0, 0, -1], [1, 1, 0], [-1, -1, 0], [1, -1, 0], [-1, 1, 0], [1, 0, 1], [-1, 0, -1], [1, 0, -1], [-1, 0, 1], [0, 1, 1], [0, -1, -1], [0, 1, -1], [0, -1, 1]])


WEIGHT_TABLE = np.array([1.0 / 3.0] + [1.0 / 18.0] * 6 + [1.0 / 36.0] * 12)


def shuffle_rows(key, row_count, length):
    return jax.vmap(lambda sub_key: jax.random.permutation(sub_key, length))(jax.random.split(key, row_count))


def layout_plan(key):
    base_key = jax.random.fold_in(key, 4242)
    keys = jax.random.split(base_key, 4)
    group_size = GROUP
    positions = 4 * group_size
    block_count = 2 * group_size
    occupied = shuffle_rows(keys[0], SLABS, positions)[:, :block_count].astype(jnp.int32)
    order = shuffle_rows(keys[1], SLABS, group_size).astype(jnp.int32)
    post_perm = shuffle_rows(keys[2], SLABS * group_size, HELD).reshape(SLABS, group_size, HELD).astype(jnp.int32)
    pre_perm = shuffle_rows(keys[3], SLABS * group_size, SLOTS).reshape(SLABS, group_size, SLOTS).astype(jnp.int32)
    block_ids = jnp.arange(block_count, dtype=jnp.int32)
    full_part = group_size // 2 * HELD
    stays_row = block_ids < full_part
    rank = jnp.where(stays_row, block_ids // HELD, group_size // 2 + block_ids - full_part)
    place_pos = jnp.where(stays_row, block_ids % HELD, 0)
    slab_ids = jnp.broadcast_to(jnp.arange(SLABS, dtype=jnp.int32)[:, None], (SLABS, block_count))
    stays = jnp.broadcast_to(stays_row[None, :], (SLABS, block_count))
    owner = order[slab_ids, jnp.broadcast_to(rank[None, :], (SLABS, block_count))]
    place_all = jnp.broadcast_to(place_pos[None, :], (SLABS, block_count))
    post_slot = post_perm[slab_ids, owner, place_all]
    single = jnp.maximum(block_ids - full_part, 0)
    holder = order[slab_ids, jnp.broadcast_to((single // OUT_CAP)[None, :], (SLABS, block_count))]
    send_pos = jnp.broadcast_to((single % OUT_CAP)[None, :], (SLABS, block_count))
    pre_stay = pre_perm[slab_ids, owner, place_all]
    pre_move = pre_perm[slab_ids, holder, HELD + send_pos]
    keep_table = jnp.full((SLABS, group_size, HELD), -1, jnp.int32)
    keep_table = keep_table.at[slab_ids, owner, post_slot].set(jnp.where(stays, pre_stay, -1))
    holder_index = jnp.where(stays, group_size, holder)
    slot_table = jnp.full((SLABS, group_size, OUT_CAP), -1, jnp.int32)
    slot_table = slot_table.at[slab_ids, holder_index, send_pos].set(pre_move, mode='drop')
    dest_table = jnp.full((SLABS, group_size, OUT_CAP), -1, jnp.int32)
    dest_table = dest_table.at[slab_ids, holder_index, send_pos].set(owner * HELD + post_slot, mode='drop')
    occ_y = occupied // group_size
    occ_z = occupied % group_size
    grid = jnp.full((SLABS, 4, group_size), -1, jnp.int32)
    grid = grid.at[slab_ids, occ_y, occ_z].set(owner * HELD + post_slot)
    padded = jnp.pad(grid, 1, constant_values=-1)
    code_list = []
    for direction in range(18):
        shift_x = int(VELOCITY_TABLE[direction + 1][0])
        shift_y = int(VELOCITY_TABLE[direction + 1][1])
        shift_z = int(VELOCITY_TABLE[direction + 1][2])
        found = padded[slab_ids + 1 + shift_x, occ_y + 1 + shift_y, occ_z + 1 + shift_z]
        code_list.append(jnp.where(found >= 0, (shift_x + 1) * group_size * HELD + found, -1))
    codes = jnp.stack(code_list, axis=-1).astype(jnp.int32)
    neighbour_table = jnp.full((SLABS, group_size, HELD, 18), -1, jnp.int32)
    neighbour_table = neighbour_table.at[slab_ids, owner, post_slot].set(codes)
    return (keep_table.reshape(-1), slot_table.reshape(-1), dest_table.reshape(-1), neighbour_table.reshape(-1, 18))


def draw_keep_slot(key, part):
    return layout_plan(key)[0]


def draw_send_slot(key, part):
    return layout_plan(key)[1]


def draw_send_dest(key, part):
    return layout_plan(key)[2]


def draw_neighbours(key, part):
    return layout_plan(key)[3]


def draw_pops_in(key, part):
    row_count = SLABS * GROUP * SLOTS
    cell_count = EDGE * EDGE * EDGE
    keys = jax.random.split(jax.random.fold_in(key, 99), 3)
    density = 1.0 + 0.1 * jnp.clip(jax.random.normal(keys[0], (row_count, 1, cell_count), jnp.float32), -3.0, 3.0)
    flow = 0.04 * jnp.clip(jax.random.normal(keys[1], (row_count, 3, cell_count), jnp.float32), -2.5, 2.5)
    spread = 0.35
    vel_table = jnp.asarray(VELOCITY_TABLE, jnp.float32)
    weights = jnp.asarray(WEIGHT_TABLE, jnp.float32)
    projected = jnp.einsum('pa,rac->rpc', vel_table, flow)
    square = jnp.sum(flow * flow, axis=1, keepdims=True)
    equilibrium = weights[None, :, None] * density * (1.0 + 3.0 * projected + 4.5 * projected * projected - 1.5 * square)
    noise = jax.random.uniform(keys[2], (row_count, 19, cell_count), jnp.float32, -1.0, 1.0)
    return (equilibrium * (1.0 + spread * noise)).astype(jnp.float32)


def touch_ends(values, own_key, least, top_value):
    place = [jax.random.randint(jax.random.fold_in(own_key, axis), (), 0, length) for axis, length in enumerate(values.shape)]
    widest = values.shape.index(max(values.shape))
    neighbour = place[:widest] + [(place[widest] + 1) % values.shape[widest]] + place[widest + 1:]
    return values.at[tuple(place)].set(least).at[tuple(neighbour)].set(top_value)


def setup_inputs(seed: int = 0) -> dict:
    key_of = jax.random.split(jax.random.key(seed), 7)
    return {
        "pops_in": draw_pops_in(jax.random.fold_in(key_of[6], 71), 0),
        "keep_slot": draw_keep_slot(jax.random.fold_in(key_of[6], 71), 0),
        "send_slot": draw_send_slot(jax.random.fold_in(key_of[6], 71), 0),
        "send_dest": draw_send_dest(jax.random.fold_in(key_of[6], 71), 0),
        "neighbours": draw_neighbours(jax.random.fold_in(key_of[6], 71), 0),
        "fluid": touch_ends((jax.random.randint(key_of[5], (DEVICES * HELD, CELLS), 0, 20) < 17).astype(jnp.int32), jax.random.fold_in(key_of[5], 1), 0, 1),
    }


VELOCITY = np.array([[0, 0, 0], [1, 0, 0], [-1, 0, 0], [0, 1, 0], [0, -1, 0], [0, 0, 1], [0, 0, -1], [1, 1, 0], [-1, -1, 0], [1, -1, 0], [-1, 1, 0], [1, 0, 1], [-1, 0, -1], [1, 0, -1], [-1, 0, 1], [0, 1, 1], [0, -1, -1], [0, 1, -1], [0, -1, 1]])
WEIGHTS = np.array([1.0 / 3.0] + [1.0 / 18.0] * 6 + [1.0 / 36.0] * 12)
OPPOSITE = [0, 2, 1, 4, 3, 6, 5, 8, 7, 10, 9, 12, 11, 14, 13, 16, 15, 18, 17]
FACE_OPPOSITE = np.array([1, 0, 3, 2, 5, 4])
EDGE_OPPOSITE = np.array([1, 0, 3, 2, 5, 4, 7, 6, 9, 8, 11, 10])
NU_ZERO = 0.1
NU_LIMIT = 0.01
LAMBDA_TIME = 10.0
POWER_INDEX = 0.35
OMEGA_ZERO = 1.0 / (3.0 * NU_ZERO + 0.5)
SHEAR_SCALE = 2.1213203435596424

def find_velocity(target):
    for pop_index in range(19):
        if tuple((int(value) for value in VELOCITY[pop_index])) == tuple((int(value) for value in target)):
            return pop_index
    return -1

def face_members(normal_index):
    normal = VELOCITY[normal_index + 1]
    return [pop_index for pop_index in range(1, 19) if int(np.dot(VELOCITY[pop_index], normal)) == 1]

def face_source(pop_index, dimension):
    target = [0, 0, 0]
    target[dimension] = -int(VELOCITY[pop_index][dimension])
    direction = find_velocity(target) - 1
    members = face_members(direction ^ 1)
    return (direction, members.index(pop_index))

def collide(pops, fluid):
    vel_table = jnp.asarray(VELOCITY, jnp.float32)
    weights = jnp.asarray(WEIGHTS, jnp.float32)
    density = lax.optimization_barrier(jnp.sum(pops, axis=1))
    moment = jnp.einsum('pa,bpc->bac', vel_table, pops, precision=lax.Precision.HIGHEST)
    velocity_field = moment / density[:, None, :]
    projected = jnp.einsum('pa,bac->bpc', vel_table, velocity_field, precision=lax.Precision.HIGHEST)
    square = lax.optimization_barrier(jnp.sum(velocity_field * velocity_field, axis=1))
    equilibrium = weights[None, :, None] * density[:, None, :] * (1.0 + 3.0 * projected + 4.5 * projected * projected - 1.5 * square[:, None, :])
    excess = pops - equilibrium
    stress_total = jnp.zeros_like(density)
    for first_axis in range(3):
        for second_axis in range(3):
            factor = jnp.asarray(VELOCITY[:, first_axis] * VELOCITY[:, second_axis], jnp.float32)
            component = jnp.einsum('p,bpc->bc', factor, excess, precision=lax.Precision.HIGHEST)
            stress_total = stress_total + component * component
    shear_rate = SHEAR_SCALE * OMEGA_ZERO * jnp.sqrt(stress_total) / density
    viscosity = NU_LIMIT + (NU_ZERO - NU_LIMIT) * jnp.power(1.0 + (LAMBDA_TIME * shear_rate) ** 2, (POWER_INDEX - 1.0) / 2.0)
    relax_rate = 1.0 / (3.0 * viscosity + 0.5)
    relaxed = pops - relax_rate[:, None, :] * excess
    flipped = pops[:, OPPOSITE]
    return jnp.where(fluid[:, None, :] == 1, relaxed, flipped)

def make_rims(collided):
    block_count = collided.shape[0]
    edge_cells = collided.shape[-1]
    plane_list = []
    for normal_index in range(6):
        normal = VELOCITY[normal_index + 1]
        main_axis = int(np.argmax(np.abs(normal)))
        layer_index = edge_cells - 1 if normal[main_axis] > 0 else 0
        picked = collided[:, face_members(normal_index)]
        plane_list.append(lax.index_in_dim(picked, layer_index, main_axis + 2, keepdims=False))
    face_rims = jnp.stack(plane_list, 1).reshape(block_count, 30, edge_cells * edge_cells)
    line_list = []
    for edge_index in range(12):
        edge_vec = VELOCITY[edge_index + 7]
        chosen = collided[:, edge_index + 7]
        for dimension in (2, 1, 0):
            if edge_vec[dimension] != 0:
                layer_index = edge_cells - 1 if edge_vec[dimension] > 0 else 0
                chosen = lax.index_in_dim(chosen, layer_index, dimension + 1, keepdims=False)
        line_list.append(chosen)
    edge_rims = jnp.stack(line_list, 1)
    return (face_rims, edge_rims)

def attach_plane(block_data, plane_data, dimension, sign_value):
    expanded = jnp.expand_dims(plane_data, dimension)
    if sign_value > 0:
        return jnp.concatenate([expanded, block_data], axis=dimension)
    return jnp.concatenate([block_data, expanded], axis=dimension)

def trim_block(block_data, dimension, sign_value, edge_cells):
    if sign_value > 0:
        return lax.slice_in_dim(block_data, 0, edge_cells, axis=dimension)
    return lax.slice_in_dim(block_data, 1, edge_cells + 1, axis=dimension)

def stream(collided, face_ghost, edge_ghost, face_here, edge_here):
    block_count = collided.shape[0]
    edge_cells = collided.shape[-1]
    planes = face_ghost.reshape(block_count, 6, 5, edge_cells, edge_cells)
    moved_pops = [collided[:, 0]]
    for pop_index in range(1, 19):
        arrow_vec = VELOCITY[pop_index]
        moving = [dimension for dimension in range(3) if arrow_vec[dimension] != 0]
        values = collided[:, pop_index]
        present_mask = jnp.ones_like(values)
        first_axis = moving[0]
        direction, member = face_source(pop_index, first_axis)
        face_vals = planes[:, direction, member]
        face_mask = jnp.broadcast_to(face_here[:, direction][:, None, None], face_vals.shape)
        values = attach_plane(values, face_vals, first_axis + 1, arrow_vec[first_axis])
        present_mask = attach_plane(present_mask, face_mask, first_axis + 1, arrow_vec[first_axis])
        if len(moving) == 2:
            second = moving[1]
            other_dir, other_member = face_source(pop_index, second)
            side_vals = planes[:, other_dir, other_member]
            side_mask = jnp.broadcast_to(edge_here[:, 0][:, None, None] * 0.0 + face_here[:, other_dir][:, None, None], side_vals.shape)
            line_index = find_velocity(-arrow_vec) - 7
            corner_vals = edge_ghost[:, line_index]
            corner_mask = jnp.broadcast_to(edge_here[:, line_index][:, None], corner_vals.shape)
            others = [dimension for dimension in range(3) if dimension != second]
            first_pos = others.index(first_axis) + 1
            side_vals = attach_plane(side_vals, corner_vals, first_pos, arrow_vec[first_axis])
            side_mask = attach_plane(side_mask, corner_mask, first_pos, arrow_vec[first_axis])
            values = attach_plane(values, side_vals, second + 1, arrow_vec[second])
            present_mask = attach_plane(present_mask, side_mask, second + 1, arrow_vec[second])
        for dimension in moving:
            values = trim_block(values, dimension + 1, arrow_vec[dimension], edge_cells)
            present_mask = trim_block(present_mask, dimension + 1, arrow_vec[dimension], edge_cells)
        moved_pops.append(jnp.where(present_mask > 0.5, values, collided[:, OPPOSITE[pop_index]]))
    return jnp.stack(moved_pops, axis=1)

def reference(pops_in, keep_slot, send_slot, send_dest, neighbours, fluid):
    total = keep_slot.shape[0]
    per_slab = GROUP * HELD
    cell_count = pops_in.shape[2]
    edge_cells = EDGE
    weights = jnp.asarray(WEIGHTS, jnp.float32)
    rest_state = jnp.broadcast_to(weights[None, :, None], (total, 19, cell_count))
    owner = (jnp.arange(total) // HELD).astype(jnp.int32)
    kept = pops_in[jnp.where(keep_slot >= 0, owner * SLOTS + keep_slot, 0).astype(jnp.int32)]
    current = jnp.where((keep_slot >= 0)[:, None, None], kept, rest_state)
    sender = (jnp.arange(send_slot.shape[0]) // OUT_CAP).astype(jnp.int32)
    moved_rows = pops_in[jnp.where(send_slot >= 0, sender * SLOTS + send_slot, 0).astype(jnp.int32)]
    target = jnp.where(send_dest >= 0, sender // GROUP * per_slab + send_dest, total).astype(jnp.int32)
    current = current.at[target].set(moved_rows, mode='drop')
    slab_base = (jnp.arange(total) // per_slab * per_slab).astype(jnp.int32)
    present = neighbours >= 0
    lookup = jnp.where(present, slab_base[:, None] + neighbours - per_slab, 0).astype(jnp.int32)
    face_here = present[:, :6].astype(jnp.float32)
    edge_here = present[:, 6:].astype(jnp.float32)
    for step_index in range(STEPS):
        collided = collide(current, fluid).reshape(total, 19, edge_cells, edge_cells, edge_cells)
        face_rims, edge_rims = make_rims(collided)
        face_table = face_rims.reshape(total, 6, 5, edge_cells * edge_cells)
        face_ghost = face_table[lookup[:, :6], FACE_OPPOSITE[None, :]]
        edge_ghost = edge_rims[lookup[:, 6:], EDGE_OPPOSITE[None, :]]
        current = stream(collided, face_ghost, edge_ghost, face_here, edge_here).reshape(total, 19, cell_count)
    return current
```

```python
import jax
import jax.numpy as jnp
from jax import lax
from jax.experimental import pallas as pl
from jax.experimental.pallas import tpu as pltpu
from jax.sharding import Mesh, PartitionSpec as P

STEPS = 4
HELD = 3
ROWS = 48
PACK = 56
INTERPRET = False

VELOCITY = [
    (0, 0, 0),
    (1, 0, 0), (-1, 0, 0), (0, 1, 0), (0, -1, 0), (0, 0, 1), (0, 0, -1),
    (1, 1, 0), (-1, -1, 0), (1, -1, 0), (-1, 1, 0),
    (1, 0, 1), (-1, 0, -1), (1, 0, -1), (-1, 0, 1),
    (0, 1, 1), (0, -1, -1), (0, 1, -1), (0, -1, 1),
]
WEIGHTS = [1.0 / 3.0] + [1.0 / 18.0] * 6 + [1.0 / 36.0] * 12
OPPOSITE = [0, 2, 1, 4, 3, 6, 5, 8, 7, 10, 9, 12, 11, 14, 13, 16, 15, 18, 17]
UP = [i for i in range(19) if VELOCITY[i][2] == 1]
DOWN = [i for i in range(19) if VELOCITY[i][2] == -1]
NU_ZERO = 0.1
NU_LIMIT = 0.01
LAMBDA_TIME = 10.0
POWER_INDEX = 0.35
OMEGA_ZERO = 1.0 / (3.0 * NU_ZERO + 0.5)
SHEAR_SCALE = 2.1213203435596424
RATE_SCALE = (LAMBDA_TIME * SHEAR_SCALE * OMEGA_ZERO) ** 2
F32 = jnp.float32
BF16 = jnp.bfloat16


def iota(shape, dim):
    return lax.broadcasted_iota(jnp.int32, shape, dim)


def dot(a, b):
    return jnp.dot(a, b, preferred_element_type=F32)


def split(x):
    high = x.astype(BF16)
    rest = x - high.astype(F32)
    middle = rest.astype(BF16)
    low = (rest - middle.astype(F32)).astype(BF16)
    return high, middle, low


def choose(picks, x):
    n = x.shape[1]
    y = dot(picks, jnp.concatenate(split(x), axis=1))
    return y[:, :n] + y[:, n : 2 * n] + y[:, 2 * n :]


def permute_lanes(x, picks):
    m = x.shape[0]
    y = dot(jnp.concatenate(split(x), axis=0), picks)
    return y[:m] + y[m : 2 * m] + y[2 * m :]


def collide(f, fluid):
    def total(indices):
        out = None
        for i in indices:
            out = f[i] if out is None else out + f[i]
        return out

    rho = total(range(19))
    inverse = 1.0 / rho
    u = []
    for a in range(3):
        plus = total([i for i in range(19) if VELOCITY[i][a] == 1])
        minus = total([i for i in range(19) if VELOCITY[i][a] == -1])
        u.append((plus - minus) * inverse)
    base = 1.0 - 1.5 * (u[0] * u[0] + u[1] * u[1] + u[2] * u[2])
    excess = [f[0] - WEIGHTS[0] * rho * base]
    scaled = {}
    for i in range(1, 19, 2):
        c = VELOCITY[i]
        along = None
        for a in range(3):
            if c[a]:
                term = u[a]
                if along is None:
                    along = term if c[a] > 0 else -term
                else:
                    along = along + term if c[a] > 0 else along - term
        if WEIGHTS[i] not in scaled:
            scaled[WEIGHTS[i]] = WEIGHTS[i] * rho
        even = base + 4.5 * along * along
        odd = 3.0 * along
        excess.append(f[i] - scaled[WEIGHTS[i]] * (even + odd))
        excess.append(f[i + 1] - scaled[WEIGHTS[i]] * (even - odd))
    stress = None
    for a in range(3):
        for b in range(a, 3):
            part = None
            for i in range(1, 19):
                sign = VELOCITY[i][a] * VELOCITY[i][b]
                if sign:
                    if part is None:
                        part = excess[i] if sign > 0 else -excess[i]
                    else:
                        part = part + excess[i] if sign > 0 else part - excess[i]
            square = part * part if a == b else 2.0 * (part * part)
            stress = square if stress is None else stress + square
    grown = 1.0 + RATE_SCALE * stress * inverse * inverse
    thinned = jnp.exp(((POWER_INDEX - 1.0) / 2.0) * jnp.log(grown))
    viscosity = NU_LIMIT + (NU_ZERO - NU_LIMIT) * thinned
    rate = 1.0 / (3.0 * viscosity + 0.5)
    wet = fluid == 1.0
    return [jnp.where(wet, f[i] - rate * excess[i], f[OPPOSITE[i]]) for i in range(19)]


def collide_all(f_ref, fluid_ref, fc_ref):
    for g in range(ROWS // 8):
        rows = slice(8 * g, 8 * g + 8)
        done = collide([f_ref[i, rows, :] for i in range(19)], fluid_ref[rows, :])
        for i in range(19):
            fc_ref[i, rows, :] = done[i]


def planes_to_send(fc_ref, zp_ref):
    z = lax.axis_index("z")
    up = ((z + lax.axis_index("core")) % 2) == 0
    for k in range(5):
        @pl.when(up)
        def _():
            zp_ref[ROWS * k : ROWS * (k + 1), :] = fc_ref[UP[k]]

        @pl.when(jnp.logical_not(up))
        def _():
            zp_ref[ROWS * k : ROWS * (k + 1), :] = fc_ref[DOWN[k]]


def pack_kernel(keep, send, dest, nbr, pops, fluid, out, xa, xb):
    xa[...] = jnp.zeros_like(xa)
    xb[...] = jnp.zeros_like(xb)
    for s in range(5):
        slot = jnp.maximum(keep[s] if s < HELD else send[s - HELD], 0)
        for i in range(19):
            rows = slice(10 * s + i // 2, 10 * s + i // 2 + 1)
            (xb if i % 2 else xa)[rows, :] = pops[slot, i : i + 1, :]
    for t in range(HELD):
        xb[10 * t + 9 : 10 * t + 10, :] = fluid[t : t + 1, :].astype(F32)
    k, n = iota((128, 128), 0), iota((128, 128), 1)
    picks = (n == (k % 8) * 16 + k // 8).astype(F32).astype(BF16)
    tiles = [x[:, 128 * q : 128 * q + 128] for x in (xa, xb) for q in range(4)]
    y = permute_lanes(jnp.concatenate(tiles, axis=0), picks)
    lane, row = iota((PACK, 128), 1), iota((PACK, 128), 0)
    values = [keep[t] for t in range(3)] + [dest[j] for j in range(2)]
    values = list(enumerate(values)) + [
        (10 + 18 * t + j, nbr[t, j]) for t in range(3) for j in range(18)
    ]
    line = iota((8, 128), 1)
    table = jnp.zeros((8, 128), jnp.int32)
    for place, value in values:
        table = jnp.where(line == 64 + place, value, table)
    table = jnp.concatenate([table.astype(F32)] * (PACK // 8), axis=0)
    marked = jnp.logical_and(row == 39, lane >= 64)
    for z in range(8):
        acc = table
        for part in range(8):
            piece = y[PACK * part : PACK * part + PACK]
            shift = (16 * part - 16 * z) % 128
            piece = pltpu.roll(piece, shift, 1) if shift else piece
            keep_mask = lane // 16 == part
            if part >= 4:
                keep_mask = jnp.logical_and(keep_mask, row != 39)
            acc = jnp.where(keep_mask, piece, acc)
        out[z] = jnp.where(jnp.logical_or(marked, lane < 128), acc, 0.0)


def place_kernel(got, st, nb, xp):
    tables = got[pl.ds(39, 16, stride=PACK), :]
    row16 = iota((ROWS, 16), 0)
    lane16 = iota((ROWS, 16), 1)
    m16 = row16 // 3
    whose = (m16 % 2) * 8 + m16 // 2
    picks = (lane16 == whose).astype(F32).astype(BF16)
    mine = dot(picks, tables.astype(BF16))
    lane, row = iota((ROWS, 128), 1), iota((ROWS, 128), 0)
    t = row % 3
    kept = jnp.sum(jnp.where(lane == 64 + t, mine, 0.0), axis=1, keepdims=True)
    eye = iota((16, 16), 0) == iota((16, 16), 1)
    lane_t = iota((16, 128), 1)
    found = jnp.full((ROWS, 1), -4096, jnp.int32)
    for j in range(2):
        column = jnp.sum(jnp.where(lane_t == 67 + j, tables, 0.0), axis=1, keepdims=True)
        diagonal = jnp.where(eye, column, 0.0).astype(BF16)
        targets = dot(jnp.ones((ROWS, 16), BF16), diagonal)
        hit = targets == row16.astype(F32)
        where_from = jnp.where(hit, lane16 * PACK + 30 + 10 * j + 4096, 0)
        found = found + jnp.sum(where_from.astype(F32), axis=1, keepdims=True).astype(jnp.int32)
    row1 = iota((ROWS, 1), 0)
    m1 = row1 // 3
    own = ((m1 % 2) * 8 + m1 // 2) * PACK + (row1 % 3) * 10
    source = jnp.where(kept >= 0.0, own, found)
    wide_lane = iota((ROWS, 16 * PACK), 1)
    matrices = [(wide_lane == source + p).astype(F32) for p in range(10)]
    matrices.append((wide_lane == own + 9).astype(F32))
    full = choose(jnp.concatenate(matrices, axis=0).astype(BF16), got[...])
    there = source >= 0
    middle = jnp.logical_and(lane >= 32, lane < 96)
    for i in range(19):
        value = full[ROWS * (i // 2) : ROWS * (i // 2) + ROWS]
        value = pltpu.roll(value, 32 if i % 2 == 0 else 96, 1)
        st[i] = jnp.where(jnp.logical_and(there, middle), value, WEIGHTS[i])
    st[19] = jnp.where(middle, pltpu.roll(full[10 * ROWS : 11 * ROWS], 96, 1), 0.0)
    codes = jnp.zeros((ROWS, 128), F32)
    for k in range(3):
        codes = jnp.where(t == k, pltpu.roll(mine, (128 - 74 - 18 * k) % 128, 1), codes)
    nb[...] = codes
    to_right = ((lax.axis_index("wide") + lax.axis_index("core")) % 2) == 0
    for q in range(5):
        acc = jnp.zeros((ROWS, 128), F32)
        for k in range(4):
            value = st[4 * q + k]
            half = jnp.where(to_right, pltpu.roll(value, 64, 1), pltpu.roll(value, 96, 1))
            half = pltpu.roll(half, 32 * k, 1) if k else half
            acc = jnp.where(lane // 32 == k, half, acc)
        xp[ROWS * q : ROWS * q + ROWS, :] = acc
    xp[ROWS * 5 : ROWS * 6, :] = codes


def start_kernel(st, nb, xg, fc, fluid, nb3, zp, f):
    w = lax.axis_index("wide")
    lane = iota((ROWS, 128), 1)
    left, right = (w + 1) % 2, w % 2
    for i in range(20):
        rows = slice(ROWS * (i // 4), ROWS * (i // 4) + ROWS)
        from_left = xg[left, 0, rows, :]
        from_right = xg[right, 1, rows, :]
        shift = (128 - 32 * (i % 4)) % 128
        from_left = pltpu.roll(from_left, shift, 1) if shift else from_left
        shift = (224 - 32 * (i % 4)) % 128
        from_right = pltpu.roll(from_right, shift, 1) if shift else from_right
        value = jnp.where(lane < 32, from_left, jnp.where(lane < 96, st[i], from_right))
        if i < 19:
            f[i] = value
        else:
            fluid[...] = value
    nb3[0] = xg[left, 0, ROWS * 5 : ROWS * 6, :]
    nb3[1] = nb[...]
    nb3[2] = xg[right, 1, ROWS * 5 : ROWS * 6, :]
    collide_all(f, fluid, fc)
    planes_to_send(fc, zp)


def stream(fc, zg, nb3, f):
    z = lax.axis_index("z")
    planes = 8
    lane = iota((ROWS, 128), 1)
    column, y = lane // 8, lane % 8
    segment = [column < 4, jnp.logical_and(column >= 4, column < 12), column >= 12]
    row1 = iota((ROWS, 1), 0)
    slots = iota((ROWS, ROWS), 1)
    tables = [nb3[g].astype(jnp.int32) for g in range(3)]
    below, above = (z + 1) % 2, z % 2

    def source_rows(g, d):
        if d == (0, 0, 0):
            return row1
        j = VELOCITY.index(d) - 1
        return tables[g][:, j : j + 1] - (1 + d[0]) * ROWS

    f[0] = fc[0]
    for i in range(1, 19):
        cx, cy, cz = VELOCITY[i]
        if cz == 0:
            x = fc[i]
        elif cz == 1:
            k = UP.index(i)
            x = zg[below, 0, ROWS * k : ROWS * (k + 1), :]
        else:
            k = DOWN.index(i)
            x = zg[above, 1, ROWS * k : ROWS * (k + 1), :]
        shift = (8 * cx + cy) % 128
        moved = pltpu.roll(x, shift, 1) if shift else x
        at_y = None
        if cy:
            at_y = y == (0 if cy > 0 else 7)
            moved = jnp.where(at_y, pltpu.roll(x, (8 * cx - 7 * cy) % 128, 1), moved)
        at_x = {}
        if cx > 0:
            at_x = {1: column == 4, 2: column == 12}
            edge = column == 0
        elif cx < 0:
            at_x = {0: column == 3, 1: column == 11}
            edge = column == 15
        if cz:
            at_z = z == (0 if cz > 0 else planes - 1)
        parts = []
        for bx in (0, 1) if cx else (0,):
            for by in (0, 1) if cy else (0,):
                if not (bx or by or cz):
                    continue
                for g in range(3):
                    if bx and g not in at_x:
                        continue
                    d = (-cx * bx, -cy * by, 0)
                    rows = source_rows(g, d)
                    if cz:
                        rows = jnp.where(at_z, source_rows(g, d[:2] + (-cz,)), rows)
                    mask = at_x[g] if bx else segment[g]
                    if by:
                        mask = jnp.logical_and(mask, at_y)
                    parts.append((mask, rows))
        picks = [(rows == slots).astype(F32) for _, rows in parts]
        taken = choose(jnp.concatenate(picks, axis=0).astype(BF16), moved)
        bounced = fc[OPPOSITE[i]]
        out = moved
        for n, (mask, rows) in enumerate(parts):
            value = jnp.where(rows >= 0, taken[ROWS * n : ROWS * n + ROWS], bounced)
            out = jnp.where(mask, value, out)
        if cx:
            out = jnp.where(edge, bounced, out)
        f[i] = out


def step_kernel(fc, zg, nb3, fluid, fc_out, zp, f):
    stream(fc, zg, nb3, f)
    collide_all(f, fluid, fc_out)
    planes_to_send(fc_out, zp)


def last_kernel(fc, zg, nb3, out, f):
    stream(fc, zg, nb3, f)
    first = lax.axis_index("core") == 0
    lane = iota((ROWS, 128), 1)
    out[:, 24:32, :] = jnp.zeros((8, 8, 128), F32)
    for p in range(10):
        value = pltpu.roll(f[2 * p], 96, 1)
        if p < 9:
            value = jnp.where(lane < 64, value, pltpu.roll(f[2 * p + 1], 32, 1))
        for z in range(8):
            a, b = value[6 * z : 6 * z + 3], value[6 * z + 3 : 6 * z + 6]
            out[z, 3 * p : 3 * p + 3, :] = jnp.where(first, a, b)


def unpack_kernel(got, out, y):
    lane = iota((32, 128), 1)
    k, n = iota((128, 128), 0), iota((128, 128), 1)
    picks = (n == (k % 16) * 8 + k // 16).astype(F32).astype(BF16)
    tiles = []
    for part in range(8):
        acc = None
        for z in range(8):
            shift = (16 * z - 16 * part) % 128
            piece = pltpu.roll(got[z], shift, 1) if shift else got[z]
            acc = piece if acc is None else jnp.where(lane // 16 == z, piece, acc)
        tiles.append(acc)
    y[...] = permute_lanes(jnp.concatenate(tiles, axis=0), picks)
    for part in range(8):
        h, q = part // 4, part % 4
        for i in range(h, 19, 2):
            for t in range(HELD):
                row = 32 * part + 3 * (i // 2) + t
                out[t, i : i + 1, 128 * q : 128 * q + 128] = y[row : row + 1, :]


def call(kernel, outs, scratch, *args, smem=0):
    spaces = [pltpu.SMEM] * smem + [pltpu.VMEM] * (len(args) - smem)
    many = isinstance(outs, list)
    shapes = [jax.ShapeDtypeStruct(s, F32) for s in (outs if many else [outs])]
    specs = [pl.BlockSpec(memory_space=pltpu.VMEM) for _ in shapes]
    return pl.pallas_call(
        kernel,
        out_shape=shapes if many else shapes[0],
        in_specs=[pl.BlockSpec(memory_space=s) for s in spaces],
        out_specs=specs if many else specs[0],
        scratch_shapes=[pltpu.VMEM(s, F32) for s in scratch],
        interpret=INTERPRET,
    )(*args)


def solution(mesh):
    slabs, group = mesh.shape["wide"], mesh.shape["narrow"]
    chips = group // 2
    axes = ("wide", "z", "core")
    fine = Mesh(mesh.devices.reshape(slabs, chips, 2), axes)

    def pairs(count, other, index):
        return [
            [index(a, b, c), index((a + 1) % count, b, c)]
            for c in range(2)
            for a in range(c, count, 2)
            for b in range(other)
        ]

    wide_pairs = pairs(slabs, chips, lambda w, z, c: (w * chips + z) * 2 + c)
    z_pairs = pairs(chips, 1, lambda z, _, c: z * 2 + c)

    def both_sides(x, names, groups):
        y = lax.all_gather(x, names, axis_index_groups=groups)
        return lax.all_gather(y, "core")

    def shards(pops_in, keep_slot, send_slot, send_dest, neighbours, fluid):
        packed = call(
            pack_kernel, (8, PACK, 128), [(PACK, 512), (PACK, 512)],
            keep_slot, send_slot, send_dest, neighbours, pops_in, fluid, smem=4,
        )
        planes = lax.all_to_all(packed, "z", 0, 0, tiled=True)
        got = lax.all_gather(planes, "core").reshape(16 * PACK, 128)
        st, nb, xp = call(place_kernel, [(20, ROWS, 128), (ROWS, 128), (6 * ROWS, 128)], [], got)
        xg = both_sides(xp, axes, wide_pairs)
        state = (19, ROWS, 128)
        sent = (5 * ROWS, 128)
        fc, wet, nb3, zp = call(
            start_kernel, [state, (ROWS, 128), (3, ROWS, 128), sent], [state], st, nb, xg
        )
        for step in range(STEPS - 1):
            zg = both_sides(zp, ("z", "core"), z_pairs)
            fc, zp = call(step_kernel, [state, sent], [state], fc, zg, nb3, wet)
        zg = both_sides(zp, ("z", "core"), z_pairs)
        back = call(last_kernel, (8, 32, 128), [state], fc, zg, nb3)
        home = lax.all_to_all(back, "z", 0, 0, tiled=True)
        return call(unpack_kernel, (HELD, 19, 512), [(256, 128)], home)

    placed = (P(axes, None, None), P(axes), P(axes), P(axes), P(axes, None), P(axes, None))
    return jax.shard_map(
        shards, mesh=fine, in_specs=placed, out_specs=P(axes, None, None), check_vma=False
    )
```

```python
import jax
import jax.numpy as jnp
from jax import lax
from jax.experimental import pallas as pl
from jax.experimental.pallas import tpu as pltpu
from jax.sharding import Mesh, PartitionSpec as P

STEPS = 4
HELD = 3
ROWS = 48
PACK = 56
INTERPRET = False

VELOCITY = [
    (0, 0, 0),
    (1, 0, 0), (-1, 0, 0), (0, 1, 0), (0, -1, 0), (0, 0, 1), (0, 0, -1),
    (1, 1, 0), (-1, -1, 0), (1, -1, 0), (-1, 1, 0),
    (1, 0, 1), (-1, 0, -1), (1, 0, -1), (-1, 0, 1),
    (0, 1, 1), (0, -1, -1), (0, 1, -1), (0, -1, 1),
]
WEIGHTS = [1.0 / 3.0] + [1.0 / 18.0] * 6 + [1.0 / 36.0] * 12
OPPOSITE = [0, 2, 1, 4, 3, 6, 5, 8, 7, 10, 9, 12, 11, 14, 13, 16, 15, 18, 17]
UP = [i for i in range(19) if VELOCITY[i][2] == 1]
DOWN = [i for i in range(19) if VELOCITY[i][2] == -1]
NU_ZERO = 0.1
NU_LIMIT = 0.01
LAMBDA_TIME = 10.0
POWER_INDEX = 0.35
OMEGA_ZERO = 1.0 / (3.0 * NU_ZERO + 0.5)
SHEAR_SCALE = 2.1213203435596424
RATE_SCALE = (LAMBDA_TIME * SHEAR_SCALE * OMEGA_ZERO) ** 2
F32 = jnp.float32
BF16 = jnp.bfloat16


def iota(shape, dim):
    return lax.broadcasted_iota(jnp.int32, shape, dim)


def dot(a, b):
    return jnp.dot(a, b, preferred_element_type=F32)


def split(x):
    high = x.astype(BF16)
    rest = x - high.astype(F32)
    middle = rest.astype(BF16)
    low = (rest - middle.astype(F32)).astype(BF16)
    return high, middle, low


def choose(picks, x):
    n = x.shape[1]
    y = dot(picks, jnp.concatenate(split(x), axis=1))
    return y[:, :n] + y[:, n : 2 * n] + y[:, 2 * n :]


def permute_lanes(x, picks):
    m = x.shape[0]
    y = dot(jnp.concatenate(split(x), axis=0), picks)
    return y[:m] + y[m : 2 * m] + y[2 * m :]


def collide(f, fluid):
    def total(indices):
        out = None
        for i in indices:
            out = f[i] if out is None else out + f[i]
        return out

    rho = total(range(19))
    inverse = 1.0 / rho
    u = []
    for a in range(3):
        plus = total([i for i in range(19) if VELOCITY[i][a] == 1])
        minus = total([i for i in range(19) if VELOCITY[i][a] == -1])
        u.append((plus - minus) * inverse)
    base = 1.0 - 1.5 * (u[0] * u[0] + u[1] * u[1] + u[2] * u[2])
    excess = [f[0] - WEIGHTS[0] * rho * base]
    scaled = {}
    for i in range(1, 19, 2):
        c = VELOCITY[i]
        along = None
        for a in range(3):
            if c[a]:
                term = u[a]
                if along is None:
                    along = term if c[a] > 0 else -term
                else:
                    along = along + term if c[a] > 0 else along - term
        if WEIGHTS[i] not in scaled:
            scaled[WEIGHTS[i]] = WEIGHTS[i] * rho
        even = base + 4.5 * along * along
        odd = 3.0 * along
        excess.append(f[i] - scaled[WEIGHTS[i]] * (even + odd))
        excess.append(f[i + 1] - scaled[WEIGHTS[i]] * (even - odd))
    stress = None
    for a in range(3):
        for b in range(a, 3):
            part = None
            for i in range(1, 19):
                sign = VELOCITY[i][a] * VELOCITY[i][b]
                if sign:
                    if part is None:
                        part = excess[i] if sign > 0 else -excess[i]
                    else:
                        part = part + excess[i] if sign > 0 else part - excess[i]
            square = part * part if a == b else 2.0 * (part * part)
            stress = square if stress is None else stress + square
    grown = 1.0 + RATE_SCALE * stress * inverse * inverse
    thinned = jnp.exp(((POWER_INDEX - 1.0) / 2.0) * jnp.log(grown))
    viscosity = NU_LIMIT + (NU_ZERO - NU_LIMIT) * thinned
    rate = 1.0 / (3.0 * viscosity + 0.5)
    wet = fluid == 1.0
    return [jnp.where(wet, f[i] - rate * excess[i], f[OPPOSITE[i]]) for i in range(19)]


def collide_all(f_ref, fluid_ref, fc_ref):
    for g in range(ROWS // 8):
        rows = slice(8 * g, 8 * g + 8)
        done = collide([f_ref[i, rows, :] for i in range(19)], fluid_ref[rows, :])
        for i in range(19):
            fc_ref[i, rows, :] = done[i]


def planes_to_send(fc_ref, zp_ref):
    z = lax.axis_index("z")
    up = ((z + lax.axis_index("core")) % 2) == 0
    for k in range(5):
        @pl.when(up)
        def _():
            zp_ref[ROWS * k : ROWS * (k + 1), :] = fc_ref[UP[k]]

        @pl.when(jnp.logical_not(up))
        def _():
            zp_ref[ROWS * k : ROWS * (k + 1), :] = fc_ref[DOWN[k]]


def pack_kernel(keep, send, dest, nbr, pops, fluid, out, xa, xb):
    xa[...] = jnp.zeros_like(xa)
    xb[...] = jnp.zeros_like(xb)
    for s in range(5):
        slot = jnp.maximum(keep[s] if s < HELD else send[s - HELD], 0)
        for i in range(19):
            rows = slice(10 * s + i // 2, 10 * s + i // 2 + 1)
            (xb if i % 2 else xa)[rows, :] = pops[slot, i : i + 1, :]
    for t in range(HELD):
        xb[10 * t + 9 : 10 * t + 10, :] = fluid[t : t + 1, :].astype(F32)
    k, n = iota((128, 128), 0), iota((128, 128), 1)
    picks = (n == (k % 8) * 16 + k // 8).astype(F32).astype(BF16)
    tiles = [x[:, 128 * q : 128 * q + 128] for x in (xa, xb) for q in range(4)]
    y = permute_lanes(jnp.concatenate(tiles, axis=0), picks)
    lane, row = iota((PACK, 128), 1), iota((PACK, 128), 0)
    values = [keep[t] for t in range(3)] + [dest[j] for j in range(2)]
    values = list(enumerate(values)) + [
        (10 + 18 * t + j, nbr[t, j]) for t in range(3) for j in range(18)
    ]
    line = iota((8, 128), 1)
    table = jnp.zeros((8, 128), jnp.int32)
    for place, value in values:
        table = jnp.where(line == 64 + place, value, table)
    table = jnp.concatenate([table.astype(F32)] * (PACK // 8), axis=0)
    marked = jnp.logical_and(row == 39, lane >= 64)
    for z in range(8):
        acc = table
        for part in range(8):
            piece = y[PACK * part : PACK * part + PACK]
            shift = (16 * part - 16 * z) % 128
            piece = pltpu.roll(piece, shift, 1) if shift else piece
            keep_mask = lane // 16 == part
            if part >= 4:
                keep_mask = jnp.logical_and(keep_mask, row != 39)
            acc = jnp.where(keep_mask, piece, acc)
        out[z] = jnp.where(jnp.logical_or(marked, lane < 128), acc, 0.0)


def place_kernel(got, st, nb, xp):
    tables = got[pl.ds(39, 16, stride=PACK), :]
    row16 = iota((ROWS, 16), 0)
    lane16 = iota((ROWS, 16), 1)
    m16 = row16 // 3
    whose = (m16 % 2) * 8 + m16 // 2
    picks = (lane16 == whose).astype(F32).astype(BF16)
    mine = dot(picks, tables.astype(BF16))
    lane, row = iota((ROWS, 128), 1), iota((ROWS, 128), 0)
    t = row % 3
    kept = jnp.sum(jnp.where(lane == 64 + t, mine, 0.0), axis=1, keepdims=True)
    eye = iota((16, 16), 0) == iota((16, 16), 1)
    lane_t = iota((16, 128), 1)
    found = jnp.full((ROWS, 1), -4096, jnp.int32)
    for j in range(2):
        column = jnp.sum(jnp.where(lane_t == 67 + j, tables, 0.0), axis=1, keepdims=True)
        diagonal = jnp.where(eye, column, 0.0).astype(BF16)
        targets = dot(jnp.ones((ROWS, 16), BF16), diagonal)
        hit = targets == row16.astype(F32)
        where_from = jnp.where(hit, lane16 * PACK + 30 + 10 * j + 4096, 0)
        found = found + jnp.sum(where_from.astype(F32), axis=1, keepdims=True).astype(jnp.int32)
    row1 = iota((ROWS, 1), 0)
    m1 = row1 // 3
    own = ((m1 % 2) * 8 + m1 // 2) * PACK + (row1 % 3) * 10
    source = jnp.where(kept >= 0.0, own, found)
    wide_lane = iota((ROWS, 16 * PACK), 1)
    matrices = [(wide_lane == source + p).astype(F32) for p in range(10)]
    matrices.append((wide_lane == own + 9).astype(F32))
    full = choose(jnp.concatenate(matrices, axis=0).astype(BF16), got[...])
    there = source >= 0
    middle = jnp.logical_and(lane >= 32, lane < 96)
    for i in range(19):
        value = full[ROWS * (i // 2) : ROWS * (i // 2) + ROWS]
        value = pltpu.roll(value, 32 if i % 2 == 0 else 96, 1)
        st[i] = jnp.where(jnp.logical_and(there, middle), value, WEIGHTS[i])
    st[19] = jnp.where(middle, pltpu.roll(full[10 * ROWS : 11 * ROWS], 96, 1), 0.0)
    codes = jnp.zeros((ROWS, 128), F32)
    for k in range(3):
        codes = jnp.where(t == k, pltpu.roll(mine, (128 - 74 - 18 * k) % 128, 1), codes)
    nb[...] = codes
    to_right = ((lax.axis_index("wide") + lax.axis_index("core")) % 2) == 0
    for q in range(5):
        acc = jnp.zeros((ROWS, 128), F32)
        for k in range(4):
            value = st[4 * q + k]
            half = jnp.where(to_right, pltpu.roll(value, 64, 1), pltpu.roll(value, 96, 1))
            half = pltpu.roll(half, 32 * k, 1) if k else half
            acc = jnp.where(lane // 32 == k, half, acc)
        xp[ROWS * q : ROWS * q + ROWS, :] = acc
    xp[ROWS * 5 : ROWS * 6, :] = codes


def start_kernel(st, nb, xg, fc, fluid, nb3, zp, f):
    w = lax.axis_index("wide")
    lane = iota((ROWS, 128), 1)
    left, right = (w + 1) % 2, w % 2
    for i in range(20):
        rows = slice(ROWS * (i // 4), ROWS * (i // 4) + ROWS)
        from_left = xg[left, 0, rows, :]
        from_right = xg[right, 1, rows, :]
        shift = (128 - 32 * (i % 4)) % 128
        from_left = pltpu.roll(from_left, shift, 1) if shift else from_left
        shift = (224 - 32 * (i % 4)) % 128
        from_right = pltpu.roll(from_right, shift, 1) if shift else from_right
        value = jnp.where(lane < 32, from_left, jnp.where(lane < 96, st[i], from_right))
        if i < 19:
            f[i] = value
        else:
            fluid[...] = value
    nb3[0] = xg[left, 0, ROWS * 5 : ROWS * 6, :]
    nb3[1] = nb[...]
    nb3[2] = xg[right, 1, ROWS * 5 : ROWS * 6, :]
    collide_all(f, fluid, fc)
    planes_to_send(fc, zp)


def stream(fc, zg, nb3, f):
    z = lax.axis_index("z")
    planes = 8
    lane = iota((ROWS, 128), 1)
    column, y = lane // 8, lane % 8
    segment = [column < 4, jnp.logical_and(column >= 4, column < 12), column >= 12]
    row1 = iota((ROWS, 1), 0)
    slots = iota((ROWS, ROWS), 1)
    tables = [nb3[g].astype(jnp.int32) for g in range(3)]
    below, above = (z + 1) % 2, z % 2

    def source_rows(g, d):
        if d == (0, 0, 0):
            return row1
        j = VELOCITY.index(d) - 1
        return tables[g][:, j : j + 1] - (1 + d[0]) * ROWS

    f[0] = fc[0]
    for i in range(1, 19):
        cx, cy, cz = VELOCITY[i]
        if cz == 0:
            x = fc[i]
        elif cz == 1:
            k = UP.index(i)
            x = zg[below, 0, ROWS * k : ROWS * (k + 1), :]
        else:
            k = DOWN.index(i)
            x = zg[above, 1, ROWS * k : ROWS * (k + 1), :]
        shift = (8 * cx + cy) % 128
        moved = pltpu.roll(x, shift, 1) if shift else x
        at_y = None
        if cy:
            at_y = y == (0 if cy > 0 else 7)
            moved = jnp.where(at_y, pltpu.roll(x, (8 * cx - 7 * cy) % 128, 1), moved)
        at_x = {}
        if cx > 0:
            at_x = {1: column == 4, 2: column == 12}
            edge = column == 0
        elif cx < 0:
            at_x = {0: column == 3, 1: column == 11}
            edge = column == 15
        if cz:
            at_z = z == (0 if cz > 0 else planes - 1)
        parts = []
        for bx in (0, 1) if cx else (0,):
            for by in (0, 1) if cy else (0,):
                if not (bx or by or cz):
                    continue
                for g in range(3):
                    if bx and g not in at_x:
                        continue
                    d = (-cx * bx, -cy * by, 0)
                    rows = source_rows(g, d)
                    if cz:
                        rows = jnp.where(at_z, source_rows(g, d[:2] + (-cz,)), rows)
                    mask = at_x[g] if bx else segment[g]
                    if by:
                        mask = jnp.logical_and(mask, at_y)
                    parts.append((mask, rows))
        picks = [(rows == slots).astype(F32) for _, rows in parts]
        taken = choose(jnp.concatenate(picks, axis=0).astype(BF16), moved)
        bounced = fc[OPPOSITE[i]]
        out = moved
        for n, (mask, rows) in enumerate(parts):
            value = jnp.where(rows >= 0, taken[ROWS * n : ROWS * n + ROWS], bounced)
            out = jnp.where(mask, value, out)
        if cx:
            out = jnp.where(edge, bounced, out)
        f[i] = out


def step_kernel(fc, zg, nb3, fluid, fc_out, zp, f):
    stream(fc, zg, nb3, f)
    collide_all(f, fluid, fc_out)
    planes_to_send(fc_out, zp)


def last_kernel(fc, zg, nb3, out, f):
    stream(fc, zg, nb3, f)
    first = lax.axis_index("core") == 0
    lane = iota((ROWS, 128), 1)
    out[:, 24:32, :] = jnp.zeros((8, 8, 128), F32)
    for p in range(10):
        value = pltpu.roll(f[2 * p], 96, 1)
        if p < 9:
            value = jnp.where(lane < 64, value, pltpu.roll(f[2 * p + 1], 32, 1))
        for z in range(8):
            a, b = value[6 * z : 6 * z + 3], value[6 * z + 3 : 6 * z + 6]
            out[z, 3 * p : 3 * p + 3, :] = jnp.where(first, a, b)


def unpack_kernel(got, out, y):
    lane = iota((32, 128), 1)
    k, n = iota((128, 128), 0), iota((128, 128), 1)
    picks = (n == (k % 16) * 8 + k // 16).astype(F32).astype(BF16)
    tiles = []
    for part in range(8):
        acc = None
        for z in range(8):
            shift = (16 * z - 16 * part) % 128
            piece = pltpu.roll(got[z], shift, 1) if shift else got[z]
            acc = piece if acc is None else jnp.where(lane // 16 == z, piece, acc)
        tiles.append(acc)
    y[...] = permute_lanes(jnp.concatenate(tiles, axis=0), picks)
    for part in range(8):
        h, q = part // 4, part % 4
        for i in range(h, 19, 2):
            for t in range(HELD):
                row = 32 * part + 3 * (i // 2) + t
                out[t, i : i + 1, 128 * q : 128 * q + 128] = y[row : row + 1, :]


def call(kernel, outs, scratch, *args, smem=0, limit=8 * 1024 * 1024):
    spaces = [pltpu.SMEM] * smem + [pltpu.VMEM] * (len(args) - smem)
    many = isinstance(outs, list)
    shapes = [jax.ShapeDtypeStruct(s, F32) for s in (outs if many else [outs])]
    specs = [pl.BlockSpec(memory_space=pltpu.VMEM) for _ in shapes]
    return pl.pallas_call(
        kernel,
        out_shape=shapes if many else shapes[0],
        in_specs=[pl.BlockSpec(memory_space=s) for s in spaces],
        out_specs=specs if many else specs[0],
        scratch_shapes=[pltpu.VMEM(s, F32) for s in scratch],
        compiler_params=pltpu.CompilerParams(vmem_limit_bytes=limit),
        interpret=INTERPRET,
    )(*args)


def solution(mesh):
    slabs, group = mesh.shape["wide"], mesh.shape["narrow"]
    chips = group // 2
    axes = ("wide", "z", "core")
    fine = Mesh(mesh.devices.reshape(slabs, chips, 2), axes)

    def pairs(count, other, index):
        return [
            [index(a, b, c), index((a + 1) % count, b, c)]
            for c in range(2)
            for a in range(c, count, 2)
            for b in range(other)
        ]

    wide_pairs = pairs(slabs, chips, lambda w, z, c: (w * chips + z) * 2 + c)
    z_pairs = pairs(chips, 1, lambda z, _, c: z * 2 + c)

    def both_sides(x, names, groups):
        y = lax.all_gather(x, names, axis_index_groups=groups)
        return lax.all_gather(y, "core")

    def shards(pops_in, keep_slot, send_slot, send_dest, neighbours, fluid):
        packed = call(
            pack_kernel, (8, PACK, 128), [(PACK, 512), (PACK, 512)],
            keep_slot, send_slot, send_dest, neighbours, pops_in, fluid, smem=4,
            limit=None,
        )
        planes = lax.all_to_all(packed, "z", 0, 0, tiled=True)
        got = lax.all_gather(planes, "core").reshape(16 * PACK, 128)
        st, nb, xp = call(place_kernel, [(20, ROWS, 128), (ROWS, 128), (6 * ROWS, 128)], [], got)
        xg = both_sides(xp, axes, wide_pairs)
        state = (19, ROWS, 128)
        sent = (5 * ROWS, 128)
        fc, wet, nb3, zp = call(
            start_kernel, [state, (ROWS, 128), (3, ROWS, 128), sent], [state], st, nb, xg
        )
        for step in range(STEPS - 1):
            zg = both_sides(zp, ("z", "core"), z_pairs)
            fc, zp = call(step_kernel, [state, sent], [state], fc, zg, nb3, wet)
        zg = both_sides(zp, ("z", "core"), z_pairs)
        back = call(last_kernel, (8, 32, 128), [state], fc, zg, nb3)
        home = lax.all_to_all(back, "z", 0, 0, tiled=True)
        return call(unpack_kernel, (HELD, 19, 512), [(256, 128)], home)

    placed = (P(axes, None, None), P(axes), P(axes), P(axes), P(axes, None), P(axes, None))
    return jax.shard_map(
        shards, mesh=fine, in_specs=placed, out_specs=P(axes, None, None), check_vma=False
    )
```

```python
import jax
import jax.numpy as jnp
from jax import lax
from jax.experimental import pallas as pl
from jax.experimental.pallas import tpu as pltpu
from jax.sharding import Mesh, PartitionSpec as P

STEPS = 4
HELD = 3
ROWS = 48
PACK = 56
PLANES = 8
INTERPRET = False

VELOCITY = [
    (0, 0, 0),
    (1, 0, 0), (-1, 0, 0), (0, 1, 0), (0, -1, 0), (0, 0, 1), (0, 0, -1),
    (1, 1, 0), (-1, -1, 0), (1, -1, 0), (-1, 1, 0),
    (1, 0, 1), (-1, 0, -1), (1, 0, -1), (-1, 0, 1),
    (0, 1, 1), (0, -1, -1), (0, 1, -1), (0, -1, 1),
]
WEIGHTS = [1.0 / 3.0] + [1.0 / 18.0] * 6 + [1.0 / 36.0] * 12
OPPOSITE = [0, 2, 1, 4, 3, 6, 5, 8, 7, 10, 9, 12, 11, 14, 13, 16, 15, 18, 17]
UP = [i for i in range(19) if VELOCITY[i][2] == 1]
FLAT = [i for i in range(19) if VELOCITY[i][2] == 0]
DOWN = [i for i in range(19) if VELOCITY[i][2] == -1]
NU_ZERO = 0.1
NU_LIMIT = 0.01
LAMBDA_TIME = 10.0
POWER_INDEX = 0.35
OMEGA_ZERO = 1.0 / (3.0 * NU_ZERO + 0.5)
SHEAR_SCALE = 2.1213203435596424
RATE_SCALE = (LAMBDA_TIME * SHEAR_SCALE * OMEGA_ZERO) ** 2
F32 = jnp.float32
BF16 = jnp.bfloat16


def iota(shape, dim):
    return lax.broadcasted_iota(jnp.int32, shape, dim)


def dot(a, b):
    return jnp.dot(a, b, preferred_element_type=F32)


def split(x):
    high = x.astype(BF16)
    rest = x - high.astype(F32)
    middle = rest.astype(BF16)
    low = (rest - middle.astype(F32)).astype(BF16)
    return high, middle, low


def choose(picks, x):
    n = x.shape[1]
    y = dot(picks, jnp.concatenate(split(x), axis=1))
    return y[:, :n] + y[:, n : 2 * n] + y[:, 2 * n :]


def permute_lanes(x, picks):
    m = x.shape[0]
    y = dot(jnp.concatenate(split(x), axis=0), picks)
    return y[:m] + y[m : 2 * m] + y[2 * m :]


def collide(f, fluid):
    def total(indices):
        out = None
        for i in indices:
            out = f[i] if out is None else out + f[i]
        return out

    rho = total(range(19))
    inverse = 1.0 / rho
    u = []
    for a in range(3):
        plus = total([i for i in range(19) if VELOCITY[i][a] == 1])
        minus = total([i for i in range(19) if VELOCITY[i][a] == -1])
        u.append((plus - minus) * inverse)
    base = 1.0 - 1.5 * (u[0] * u[0] + u[1] * u[1] + u[2] * u[2])
    excess = [f[0] - WEIGHTS[0] * rho * base]
    scaled = {}
    for i in range(1, 19, 2):
        c = VELOCITY[i]
        along = None
        for a in range(3):
            if c[a]:
                term = u[a]
                if along is None:
                    along = term if c[a] > 0 else -term
                else:
                    along = along + term if c[a] > 0 else along - term
        if WEIGHTS[i] not in scaled:
            scaled[WEIGHTS[i]] = WEIGHTS[i] * rho
        even = base + 4.5 * along * along
        odd = 3.0 * along
        excess.append(f[i] - scaled[WEIGHTS[i]] * (even + odd))
        excess.append(f[i + 1] - scaled[WEIGHTS[i]] * (even - odd))
    stress = None
    for a in range(3):
        for b in range(a, 3):
            part = None
            for i in range(1, 19):
                sign = VELOCITY[i][a] * VELOCITY[i][b]
                if sign:
                    if part is None:
                        part = excess[i] if sign > 0 else -excess[i]
                    else:
                        part = part + excess[i] if sign > 0 else part - excess[i]
            square = part * part if a == b else 2.0 * (part * part)
            stress = square if stress is None else stress + square
    grown = 1.0 + RATE_SCALE * stress * inverse * inverse
    thinned = jnp.exp(((POWER_INDEX - 1.0) / 2.0) * jnp.log(grown))
    viscosity = NU_LIMIT + (NU_ZERO - NU_LIMIT) * thinned
    rate = 1.0 / (3.0 * viscosity + 0.5)
    wet = fluid == 1.0
    return [jnp.where(wet, f[i] - rate * excess[i], f[OPPOSITE[i]]) for i in range(19)]


def collide_all(f_ref, fluid_ref, fc_ref):
    for g in range(ROWS // 8):
        rows = slice(8 * g, 8 * g + 8)
        done = collide([f_ref[i, rows, :] for i in range(19)], fluid_ref[rows, :])
        for i in range(19):
            fc_ref[i, rows, :] = done[i]


def planes_to_send(fc_ref, zp_ref):
    z = lax.axis_index("z")
    up = ((z + lax.axis_index("core")) % 2) == 0
    for k in range(5):
        @pl.when(up)
        def _():
            zp_ref[ROWS * k : ROWS * (k + 1), :] = fc_ref[UP[k]]

        @pl.when(jnp.logical_not(up))
        def _():
            zp_ref[ROWS * k : ROWS * (k + 1), :] = fc_ref[DOWN[k]]


def pack_kernel(keep, send, dest, nbr, pops, fluid, out, xa, xb):
    xa[...] = jnp.zeros_like(xa)
    xb[...] = jnp.zeros_like(xb)
    for s in range(5):
        slot = jnp.maximum(keep[s] if s < HELD else send[s - HELD], 0)
        for i in range(19):
            rows = slice(10 * s + i // 2, 10 * s + i // 2 + 1)
            (xb if i % 2 else xa)[rows, :] = pops[slot, i : i + 1, :]
    for t in range(HELD):
        xb[10 * t + 9 : 10 * t + 10, :] = fluid[t : t + 1, :].astype(F32)
    k, n = iota((128, 128), 0), iota((128, 128), 1)
    picks = (n == (k % 8) * 16 + k // 8).astype(F32).astype(BF16)
    tiles = [x[:, 128 * q : 128 * q + 128] for x in (xa, xb) for q in range(4)]
    y = permute_lanes(jnp.concatenate(tiles, axis=0), picks)
    lane, row = iota((PACK, 128), 1), iota((PACK, 128), 0)
    values = [keep[t] for t in range(3)] + [dest[j] for j in range(2)]
    values = list(enumerate(values)) + [
        (10 + 18 * t + j, nbr[t, j]) for t in range(3) for j in range(18)
    ]
    line = iota((8, 128), 1)
    table = jnp.zeros((8, 128), jnp.int32)
    for place, value in values:
        table = jnp.where(line == 64 + place, value, table)
    table = jnp.concatenate([table.astype(F32)] * (PACK // 8), axis=0)
    marked = jnp.logical_and(row == 39, lane >= 64)
    for z in range(8):
        acc = table
        for part in range(8):
            piece = y[PACK * part : PACK * part + PACK]
            shift = (16 * part - 16 * z) % 128
            piece = pltpu.roll(piece, shift, 1) if shift else piece
            keep_mask = lane // 16 == part
            if part >= 4:
                keep_mask = jnp.logical_and(keep_mask, row != 39)
            acc = jnp.where(keep_mask, piece, acc)
        out[z] = jnp.where(jnp.logical_or(marked, lane < 128), acc, 0.0)


def place_kernel(got, st, nb, xp):
    tables = got[pl.ds(39, 16, stride=PACK), :]
    row16 = iota((ROWS, 16), 0)
    lane16 = iota((ROWS, 16), 1)
    m16 = row16 // 3
    whose = (m16 % 2) * 8 + m16 // 2
    picks = (lane16 == whose).astype(F32).astype(BF16)
    mine = dot(picks, tables.astype(BF16))
    lane, row = iota((ROWS, 128), 1), iota((ROWS, 128), 0)
    t = row % 3
    kept = jnp.sum(jnp.where(lane == 64 + t, mine, 0.0), axis=1, keepdims=True)
    eye = iota((16, 16), 0) == iota((16, 16), 1)
    lane_t = iota((16, 128), 1)
    found = jnp.full((ROWS, 1), -4096, jnp.int32)
    for j in range(2):
        column = jnp.sum(jnp.where(lane_t == 67 + j, tables, 0.0), axis=1, keepdims=True)
        diagonal = jnp.where(eye, column, 0.0).astype(BF16)
        targets = dot(jnp.ones((ROWS, 16), BF16), diagonal)
        hit = targets == row16.astype(F32)
        where_from = jnp.where(hit, lane16 * PACK + 30 + 10 * j + 4096, 0)
        found = found + jnp.sum(where_from.astype(F32), axis=1, keepdims=True).astype(jnp.int32)
    row1 = iota((ROWS, 1), 0)
    m1 = row1 // 3
    own = ((m1 % 2) * 8 + m1 // 2) * PACK + (row1 % 3) * 10
    source = jnp.where(kept >= 0.0, own, found)
    wide_lane = iota((ROWS, 16 * PACK), 1)
    matrices = [(wide_lane == source + p).astype(F32) for p in range(10)]
    matrices.append((wide_lane == own + 9).astype(F32))
    full = choose(jnp.concatenate(matrices, axis=0).astype(BF16), got[...])
    there = source >= 0
    middle = jnp.logical_and(lane >= 32, lane < 96)
    for i in range(19):
        value = full[ROWS * (i // 2) : ROWS * (i // 2) + ROWS]
        value = pltpu.roll(value, 32 if i % 2 == 0 else 96, 1)
        st[i] = jnp.where(jnp.logical_and(there, middle), value, WEIGHTS[i])
    st[19] = jnp.where(middle, pltpu.roll(full[10 * ROWS : 11 * ROWS], 96, 1), 0.0)
    codes = jnp.zeros((ROWS, 128), F32)
    for k in range(3):
        codes = jnp.where(t == k, pltpu.roll(mine, (128 - 74 - 18 * k) % 128, 1), codes)
    nb[...] = codes
    to_right = ((lax.axis_index("wide") + lax.axis_index("core")) % 2) == 0
    for q in range(5):
        acc = jnp.zeros((ROWS, 128), F32)
        for k in range(4):
            value = st[4 * q + k]
            half = jnp.where(to_right, pltpu.roll(value, 64, 1), pltpu.roll(value, 96, 1))
            half = pltpu.roll(half, 32 * k, 1) if k else half
            acc = jnp.where(lane // 32 == k, half, acc)
        xp[ROWS * q : ROWS * q + ROWS, :] = acc
    xp[ROWS * 5 : ROWS * 6, :] = codes


def start_kernel(st, nb, xg, fc, fluid, nb3, zp, f):
    w = lax.axis_index("wide")
    lane = iota((ROWS, 128), 1)
    left, right = (w + 1) % 2, w % 2
    for i in range(20):
        rows = slice(ROWS * (i // 4), ROWS * (i // 4) + ROWS)
        from_left = xg[left, 0, rows, :]
        from_right = xg[right, 1, rows, :]
        shift = (128 - 32 * (i % 4)) % 128
        from_left = pltpu.roll(from_left, shift, 1) if shift else from_left
        shift = (224 - 32 * (i % 4)) % 128
        from_right = pltpu.roll(from_right, shift, 1) if shift else from_right
        value = jnp.where(lane < 32, from_left, jnp.where(lane < 96, st[i], from_right))
        if i < 19:
            f[i] = value
        else:
            fluid[...] = value
    nb3[0] = xg[left, 0, ROWS * 5 : ROWS * 6, :]
    nb3[1] = nb[...]
    nb3[2] = xg[right, 1, ROWS * 5 : ROWS * 6, :]
    collide_all(f, fluid, fc)
    planes_to_send(fc, zp)


def passing(fc, nb3, segments):
    lane = iota((ROWS, 128), 1)
    column, y = lane // 8, lane % 8
    segment = [column < 4, jnp.logical_and(column >= 4, column < 12), column >= 12]
    row1 = iota((ROWS, 1), 0)
    slots = iota((ROWS, ROWS), 1)
    tables = {g: nb3[g].astype(jnp.int32) for g in segments}

    def source_rows(g, d):
        if d == (0, 0, 0):
            return row1
        j = VELOCITY.index(d) - 1
        return tables[g][:, j : j + 1] - (1 + d[0]) * ROWS

    def move(i, x, at_z):
        cx, cy, cz = VELOCITY[i]
        shift = (8 * cx + cy) % 128
        moved = pltpu.roll(x, shift, 1) if shift else x
        at_y = None
        if cy:
            at_y = y == (0 if cy > 0 else 7)
            moved = jnp.where(at_y, pltpu.roll(x, (8 * cx - 7 * cy) % 128, 1), moved)
        at_x = {}
        if cx > 0:
            at_x = {1: column == 4, 2: column == 12}
            edge = column == 0
        elif cx < 0:
            at_x = {0: column == 3, 1: column == 11}
            edge = column == 15
        parts = []
        for bx in (0, 1) if cx else (0,):
            for by in (0, 1) if cy else (0,):
                if not (bx or by or cz):
                    continue
                for g in segments:
                    if bx and g not in at_x:
                        continue
                    d = (-cx * bx, -cy * by, 0)
                    rows = source_rows(g, d)
                    if cz:
                        rows = jnp.where(at_z, source_rows(g, d[:2] + (-cz,)), rows)
                    mask = at_x[g] if bx else segment[g]
                    if by:
                        mask = jnp.logical_and(mask, at_y)
                    parts.append((mask, rows))
        if not parts:
            return moved
        picks = [(rows == slots).astype(F32) for _, rows in parts]
        taken = choose(jnp.concatenate(picks, axis=0).astype(BF16), moved)
        bounced = fc[OPPOSITE[i]]
        out = moved
        for n, (mask, rows) in enumerate(parts):
            value = jnp.where(rows >= 0, taken[ROWS * n : ROWS * n + ROWS], bounced)
            out = jnp.where(mask, value, out)
        if cx:
            out = jnp.where(edge, bounced, out)
        return out

    return move


def stream(fc, zg, nb3, f):
    z = lax.axis_index("z")
    below, above = (z + 1) % 2, z % 2
    move = passing(fc, nb3, (0, 1, 2))
    for i in range(19):
        if i in UP:
            k = UP.index(i)
            f[i] = move(i, zg[below, 0, ROWS * k : ROWS * (k + 1), :], z == 0)
        elif i in DOWN:
            k = DOWN.index(i)
            f[i] = move(i, zg[above, 1, ROWS * k : ROWS * (k + 1), :], z == PLANES - 1)
        else:
            f[i] = move(i, fc[i], None)


def step_kernel(fc, zg, nb3, fluid, fc_out, zp, f):
    stream(fc, zg, nb3, f)
    collide_all(f, fluid, fc_out)
    planes_to_send(fc_out, zp)


def last_kernel(fc, nb3, out):
    z = lax.axis_index("z")
    first = lax.axis_index("core") == 0
    lane = iota((ROWS, 128), 1)
    move = passing(fc, nb3, (1,))
    left = [move(i, fc[i], None) for i in FLAT]
    left += [move(i, fc[i], z == PLANES - 1) for i in UP] + [None]
    right = [move(i, fc[i], z == 0) for i in DOWN]
    right += [fc[OPPOSITE[i]] for i in UP + DOWN]
    out[:, 40:48, :] = jnp.zeros((PLANES, 8, 128), F32)
    for p in range(15):
        value = pltpu.roll(right[p], 32, 1)
        if left[p] is not None:
            value = jnp.where(lane < 64, pltpu.roll(left[p], 96, 1), value)
        for n in range(PLANES):
            a, b = value[6 * n : 6 * n + 3], value[6 * n + 3 : 6 * n + 6]
            out[n, 3 * p : 3 * p + 3, :] = jnp.where(first, a, b)


def unpack_kernel(got, nbr, out, x):
    lane, row = iota((48, 128), 1), iota((48, 128), 0)
    k, n = iota((128, 128), 0), iota((128, 128), 1)
    picks = (n == (k % 16) * 8 + k // 16).astype(F32).astype(BF16)
    place = iota((HELD, 128), 1)
    here_z, here_y = place // 16, place % 8
    absent = [nbr[:, j : j + 1] < 0 for j in range(18)]
    x[...] = jnp.zeros_like(x)

    def gathered(part):
        acc = None
        for z in range(PLANES):
            shift = (16 * z - 16 * part) % 128
            piece = pltpu.roll(got[z], shift, 1) if shift else got[z]
            acc = piece if acc is None else jnp.where(lane // 16 == z, piece, acc)
        return acc

    for q in range(4):
        a, b = gathered(q), gathered(4 + q)
        a = jnp.where(row >= 27, pltpu.roll(a, 16, 1), a)
        b = jnp.where(row < 15, pltpu.roll(b, 112, 1), b)
        here_x = 2 * q + (place % 16) // 8

        def missing(c):
            spots = []
            for size, here, top in zip(c, (here_x, here_y, here_z), (7, 7, 7)):
                spots.append(None if not size else here == (0 if size > 0 else top))
            found = jnp.zeros((HELD, 128), jnp.bool_)
            for flags in range(1, 8):
                across = [(flags >> s) & 1 for s in range(3)]
                if any(g and spot is None for g, spot in zip(across, spots)):
                    continue
                d = tuple(-size * g for size, g in zip(c, across))
                mask = jnp.broadcast_to(absent[VELOCITY.index(d) - 1], (HELD, 128))
                for g, spot in zip(across, spots):
                    if spot is not None:
                        mask = jnp.logical_and(mask, spot if g else jnp.logical_not(spot))
                found = jnp.logical_or(found, mask)
            return found

        for i in range(19):
            if i in UP:
                j = 3 * UP.index(i)
                bare = b[15 + j : 18 + j]
                value = jnp.where(missing(VELOCITY[i]), bare, a[27 + j : 30 + j])
            elif i in DOWN:
                j = 3 * DOWN.index(i)
                bare = b[30 + j : 33 + j]
                value = jnp.where(missing(VELOCITY[i]), bare, b[j : j + 3])
            else:
                j = 3 * FLAT.index(i)
                value = a[j : j + 3]
            x[64 * q + 3 * i : 64 * q + 3 * i + 3, :] = value
    y = permute_lanes(x[...], picks)
    for q in range(4):
        for i in range(19):
            for t in range(HELD):
                r = 64 * q + 3 * i + t
                out[t, i : i + 1, 128 * q : 128 * q + 128] = y[r : r + 1]


def call(kernel, outs, scratch, *args, smem=0, limit=8 * 1024 * 1024):
    spaces = [pltpu.SMEM] * smem + [pltpu.VMEM] * (len(args) - smem)
    many = isinstance(outs, list)
    shapes = [jax.ShapeDtypeStruct(s, F32) for s in (outs if many else [outs])]
    specs = [pl.BlockSpec(memory_space=pltpu.VMEM) for _ in shapes]
    return pl.pallas_call(
        kernel,
        out_shape=shapes if many else shapes[0],
        in_specs=[pl.BlockSpec(memory_space=s) for s in spaces],
        out_specs=specs if many else specs[0],
        scratch_shapes=[pltpu.VMEM(s, F32) for s in scratch],
        compiler_params=pltpu.CompilerParams(vmem_limit_bytes=limit),
        interpret=INTERPRET,
    )(*args)


def solution(mesh):
    slabs, group = mesh.shape["wide"], mesh.shape["narrow"]
    chips = group // 2
    axes = ("wide", "z", "core")
    fine = Mesh(mesh.devices.reshape(slabs, chips, 2), axes)

    def pairs(count, other, index):
        return [
            [index(a, b, c), index((a + 1) % count, b, c)]
            for c in range(2)
            for a in range(c, count, 2)
            for b in range(other)
        ]

    wide_pairs = pairs(slabs, chips, lambda w, z, c: (w * chips + z) * 2 + c)
    z_pairs = pairs(chips, 1, lambda z, _, c: z * 2 + c)

    def both_sides(x, names, groups):
        y = lax.all_gather(x, names, axis_index_groups=groups)
        return lax.all_gather(y, "core")

    def shards(pops_in, keep_slot, send_slot, send_dest, neighbours, fluid):
        packed = call(
            pack_kernel, (8, PACK, 128), [(PACK, 512), (PACK, 512)],
            keep_slot, send_slot, send_dest, neighbours, pops_in, fluid, smem=4,
            limit=None,
        )
        planes = lax.all_to_all(packed, "z", 0, 0, tiled=True)
        got = lax.all_gather(planes, "core").reshape(16 * PACK, 128)
        st, nb, xp = call(place_kernel, [(20, ROWS, 128), (ROWS, 128), (6 * ROWS, 128)], [], got)
        xg = both_sides(xp, axes, wide_pairs)
        state = (19, ROWS, 128)
        sent = (5 * ROWS, 128)
        fc, wet, nb3, zp = call(
            start_kernel, [state, (ROWS, 128), (3, ROWS, 128), sent], [state], st, nb, xg
        )
        for step in range(STEPS - 1):
            zg = both_sides(zp, ("z", "core"), z_pairs)
            fc, zp = call(step_kernel, [state, sent], [state], fc, zg, nb3, wet)
        back = call(last_kernel, (chips, 48, 128), [], fc, nb3)
        home = lax.all_to_all(back, "z", 0, 0, tiled=True)
        return call(unpack_kernel, (HELD, 19, 512), [(256, 128)], home, neighbours)

    placed = (P(axes, None, None), P(axes), P(axes), P(axes), P(axes, None), P(axes, None))
    return jax.shard_map(
        shards, mesh=fine, in_specs=placed, out_specs=P(axes, None, None), check_vma=False
    )
```

```python
import jax
import jax.numpy as jnp
from jax import lax
from jax.experimental import pallas as pl
from jax.experimental.pallas import tpu as pltpu
from jax.sharding import Mesh, PartitionSpec as P

STEPS = 4
HELD = 3
SLOTS = 48
ROWS = 32
PACK = 56
PLANES = 8
INTERPRET = False

VELOCITY = [
    (0, 0, 0),
    (1, 0, 0), (-1, 0, 0), (0, 1, 0), (0, -1, 0), (0, 0, 1), (0, 0, -1),
    (1, 1, 0), (-1, -1, 0), (1, -1, 0), (-1, 1, 0),
    (1, 0, 1), (-1, 0, -1), (1, 0, -1), (-1, 0, 1),
    (0, 1, 1), (0, -1, -1), (0, 1, -1), (0, -1, 1),
]
WEIGHTS = [1.0 / 3.0] + [1.0 / 18.0] * 6 + [1.0 / 36.0] * 12
OPPOSITE = [0, 2, 1, 4, 3, 6, 5, 8, 7, 10, 9, 12, 11, 14, 13, 16, 15, 18, 17]
UP = [i for i in range(19) if VELOCITY[i][2] == 1]
FLAT = [i for i in range(19) if VELOCITY[i][2] == 0]
DOWN = [i for i in range(19) if VELOCITY[i][2] == -1]
NU_ZERO = 0.1
NU_LIMIT = 0.01
LAMBDA_TIME = 10.0
POWER_INDEX = 0.35
OMEGA_ZERO = 1.0 / (3.0 * NU_ZERO + 0.5)
SHEAR_SCALE = 2.1213203435596424
RATE_SCALE = (LAMBDA_TIME * SHEAR_SCALE * OMEGA_ZERO) ** 2
F32 = jnp.float32
BF16 = jnp.bfloat16


def iota(shape, dim):
    return lax.broadcasted_iota(jnp.int32, shape, dim)


def dot(a, b):
    return jnp.dot(a, b, preferred_element_type=F32)


def split(x):
    high = x.astype(BF16)
    rest = x - high.astype(F32)
    middle = rest.astype(BF16)
    low = (rest - middle.astype(F32)).astype(BF16)
    return high, middle, low


def choose(picks, x):
    n = x.shape[1]
    y = dot(picks, jnp.concatenate(split(x), axis=1))
    return y[:, :n] + y[:, n : 2 * n] + y[:, 2 * n :]


def permute_lanes(x, picks):
    m = x.shape[0]
    y = dot(jnp.concatenate(split(x), axis=0), picks)
    return y[:m] + y[m : 2 * m] + y[2 * m :]


def collide(f, fluid):
    def total(indices):
        out = None
        for i in indices:
            out = f[i] if out is None else out + f[i]
        return out

    rho = total(range(19))
    inverse = 1.0 / rho
    u = []
    for a in range(3):
        plus = total([i for i in range(19) if VELOCITY[i][a] == 1])
        minus = total([i for i in range(19) if VELOCITY[i][a] == -1])
        u.append((plus - minus) * inverse)
    base = 1.0 - 1.5 * (u[0] * u[0] + u[1] * u[1] + u[2] * u[2])
    excess = [f[0] - WEIGHTS[0] * rho * base]
    scaled = {}
    for i in range(1, 19, 2):
        c = VELOCITY[i]
        along = None
        for a in range(3):
            if c[a]:
                term = u[a]
                if along is None:
                    along = term if c[a] > 0 else -term
                else:
                    along = along + term if c[a] > 0 else along - term
        if WEIGHTS[i] not in scaled:
            scaled[WEIGHTS[i]] = WEIGHTS[i] * rho
        even = base + 4.5 * along * along
        odd = 3.0 * along
        excess.append(f[i] - scaled[WEIGHTS[i]] * (even + odd))
        excess.append(f[i + 1] - scaled[WEIGHTS[i]] * (even - odd))
    stress = None
    for a in range(3):
        for b in range(a, 3):
            part = None
            for i in range(1, 19):
                sign = VELOCITY[i][a] * VELOCITY[i][b]
                if sign:
                    if part is None:
                        part = excess[i] if sign > 0 else -excess[i]
                    else:
                        part = part + excess[i] if sign > 0 else part - excess[i]
            square = part * part if a == b else 2.0 * (part * part)
            stress = square if stress is None else stress + square
    grown = 1.0 + RATE_SCALE * stress * inverse * inverse
    thinned = jnp.exp(((POWER_INDEX - 1.0) / 2.0) * jnp.log(grown))
    viscosity = NU_LIMIT + (NU_ZERO - NU_LIMIT) * thinned
    rate = 1.0 / (3.0 * viscosity + 0.5)
    wet = fluid == 1.0
    return [jnp.where(wet, f[i] - rate * excess[i], f[OPPOSITE[i]]) for i in range(19)]


def collide_all(f_ref, fluid_ref, fc_ref):
    for g in range(ROWS // 8):
        rows = slice(8 * g, 8 * g + 8)
        done = collide([f_ref[i, rows, :] for i in range(19)], fluid_ref[rows, :])
        for i in range(19):
            fc_ref[i, rows, :] = done[i]


def planes_to_send(fc_ref, zp_ref):
    z = lax.axis_index("z")
    up = ((z + lax.axis_index("core")) % 2) == 0
    for k in range(5):
        @pl.when(up)
        def _():
            zp_ref[ROWS * k : ROWS * (k + 1), :] = fc_ref[UP[k]]

        @pl.when(jnp.logical_not(up))
        def _():
            zp_ref[ROWS * k : ROWS * (k + 1), :] = fc_ref[DOWN[k]]


def pack_kernel(keep, send, dest, nbr, pops, fluid, out, xa, xb):
    xa[...] = jnp.zeros_like(xa)
    xb[...] = jnp.zeros_like(xb)
    for s in range(5):
        slot = jnp.maximum(keep[s] if s < HELD else send[s - HELD], 0)
        for i in range(19):
            rows = slice(10 * s + i // 2, 10 * s + i // 2 + 1)
            (xb if i % 2 else xa)[rows, :] = pops[slot, i : i + 1, :]
    for t in range(HELD):
        xb[10 * t + 9 : 10 * t + 10, :] = fluid[t : t + 1, :].astype(F32)
    k, n = iota((128, 128), 0), iota((128, 128), 1)
    picks = (n == (k % 8) * 16 + k // 8).astype(F32).astype(BF16)
    tiles = [x[:, 128 * q : 128 * q + 128] for x in (xa, xb) for q in range(4)]
    y = permute_lanes(jnp.concatenate(tiles, axis=0), picks)
    lane, row = iota((PACK, 128), 1), iota((PACK, 128), 0)
    values = [keep[t] for t in range(3)] + [dest[j] for j in range(2)]
    values = list(enumerate(values)) + [
        (10 + 18 * t + j, nbr[t, j]) for t in range(3) for j in range(18)
    ]
    line = iota((8, 128), 1)
    table = jnp.zeros((8, 128), jnp.int32)
    for place, value in values:
        table = jnp.where(line == 64 + place, value, table)
    table = jnp.concatenate([table.astype(F32)] * (PACK // 8), axis=0)
    marked = jnp.logical_and(row == 39, lane >= 64)
    for z in range(8):
        acc = table
        for part in range(8):
            piece = y[PACK * part : PACK * part + PACK]
            shift = (16 * part - 16 * z) % 128
            piece = pltpu.roll(piece, shift, 1) if shift else piece
            keep_mask = lane // 16 == part
            if part >= 4:
                keep_mask = jnp.logical_and(keep_mask, row != 39)
            acc = jnp.where(keep_mask, piece, acc)
        out[z] = jnp.where(jnp.logical_or(marked, lane < 128), acc, 0.0)


def place_kernel(got, st, nb, xp):
    tables = got[pl.ds(39, 16, stride=PACK), :]
    row16 = iota((SLOTS, 16), 0)
    lane16 = iota((SLOTS, 16), 1)
    m16 = row16 // 3
    whose = (m16 % 2) * 8 + m16 // 2
    picks = (lane16 == whose).astype(F32).astype(BF16)
    mine = dot(picks, tables.astype(BF16))
    lane, row = iota((SLOTS, 128), 1), iota((SLOTS, 128), 0)
    t = row % 3
    kept = jnp.sum(jnp.where(lane == 64 + t, mine, 0.0), axis=1, keepdims=True)
    eye = iota((16, 16), 0) == iota((16, 16), 1)
    lane_t = iota((16, 128), 1)
    found = jnp.full((SLOTS, 1), -4096, jnp.int32)
    for j in range(2):
        column = jnp.sum(jnp.where(lane_t == 67 + j, tables, 0.0), axis=1, keepdims=True)
        diagonal = jnp.where(eye, column, 0.0).astype(BF16)
        targets = dot(jnp.ones((SLOTS, 16), BF16), diagonal)
        hit = targets == row16.astype(F32)
        where_from = jnp.where(hit, lane16 * PACK + 30 + 10 * j + 4096, 0)
        found = found + jnp.sum(where_from.astype(F32), axis=1, keepdims=True).astype(jnp.int32)
    row1 = iota((SLOTS, 1), 0)
    m1 = row1 // 3
    own = ((m1 % 2) * 8 + m1 // 2) * PACK + (row1 % 3) * 10
    source = jnp.where(kept >= 0.0, own, found)
    occupied = (source >= 0).astype(F32)
    ones = jnp.ones((ROWS, SLOTS), BF16)

    def ranks(first, width):
        r, slot = iota((SLOTS, width), 0), iota((SLOTS, width), 1) - first
        earlier = dot(ones, jnp.where(r < slot, occupied, 0.0).astype(BF16))
        full = dot(ones, jnp.where(r == slot, occupied, 0.0).astype(BF16))
        return jnp.where(full > 0.5, earlier, -1.0)

    rank = ranks(0, SLOTS)
    picks = (rank == iota((ROWS, SLOTS), 0).astype(F32)).astype(F32).astype(BF16)
    codes = jnp.zeros((SLOTS, 128), F32)
    for k in range(3):
        codes = jnp.where(t == k, pltpu.roll(mine, (128 - 74 - 18 * k) % 128, 1), codes)
    codes = jnp.where(lane == 18, source.astype(F32), codes)
    codes = jnp.where(lane == 19, own.astype(F32), codes)
    codes = choose(picks, codes)
    source = codes[:, 18:19].astype(jnp.int32)
    own = codes[:, 19:20].astype(jnp.int32)
    wide_lane = iota((ROWS, 16 * PACK), 1)
    matrices = [(wide_lane == source + p).astype(F32) for p in range(10)]
    matrices.append((wide_lane == own + 9).astype(F32))
    full = choose(jnp.concatenate(matrices, axis=0).astype(BF16), got[...])
    lane = iota((ROWS, 128), 1)
    middle = jnp.logical_and(lane >= 32, lane < 96)
    for i in range(19):
        value = full[ROWS * (i // 2) : ROWS * (i // 2) + ROWS]
        value = pltpu.roll(value, 32 if i % 2 == 0 else 96, 1)
        st[i] = jnp.where(middle, value, WEIGHTS[i])
    st[19] = jnp.where(middle, pltpu.roll(full[10 * ROWS : 11 * ROWS], 96, 1), 0.0)
    codes = jnp.where(lane < 18, codes, ranks(64, 128))
    nb[...] = codes
    to_right = ((lax.axis_index("wide") + lax.axis_index("core")) % 2) == 0
    for q in range(5):
        acc = jnp.zeros((ROWS, 128), F32)
        for k in range(4):
            value = st[4 * q + k]
            half = jnp.where(to_right, pltpu.roll(value, 64, 1), pltpu.roll(value, 96, 1))
            half = pltpu.roll(half, 32 * k, 1) if k else half
            acc = jnp.where(lane // 32 == k, half, acc)
        xp[ROWS * q : ROWS * q + ROWS, :] = acc
    xp[ROWS * 5 : ROWS * 6, :] = codes


def start_kernel(st, nb, xg, fc, fluid, nb3, zp, f):
    w = lax.axis_index("wide")
    lane = iota((ROWS, 128), 1)
    left, right = (w + 1) % 2, w % 2
    for i in range(20):
        rows = slice(ROWS * (i // 4), ROWS * (i // 4) + ROWS)
        from_left = xg[left, 0, rows, :]
        from_right = xg[right, 1, rows, :]
        shift = (128 - 32 * (i % 4)) % 128
        from_left = pltpu.roll(from_left, shift, 1) if shift else from_left
        shift = (224 - 32 * (i % 4)) % 128
        from_right = pltpu.roll(from_right, shift, 1) if shift else from_right
        value = jnp.where(lane < 32, from_left, jnp.where(lane < 96, st[i], from_right))
        if i < 19:
            f[i] = value
        else:
            fluid[...] = value
    tables = [xg[left, 0, ROWS * 5 : ROWS * 6, :], nb[...], xg[right, 1, ROWS * 5 : ROWS * 6, :]]
    back, ahead = lane < 0, lane < 0
    for j in range(18):
        if VELOCITY[j + 1][0] < 0:
            back = jnp.logical_or(back, lane == j)
        elif VELOCITY[j + 1][0] > 0:
            ahead = jnp.logical_or(ahead, lane == j)
    base = jnp.where(ahead, 2.0 * SLOTS, jnp.where(back, 0.0, 1.0 * SLOTS))
    wanted = [jnp.where(table >= 0.0, table - base, -1.0) for table in tables]
    done = [jnp.full((ROWS, 128), -1.0, F32) for _ in range(3)]
    for slot in range(SLOTS):
        rank = [table[:, 64 + slot : 65 + slot] for table in tables]
        for g in range(3):
            value = jnp.broadcast_to(rank[g], (ROWS, 128))
            value = jnp.where(back, rank[g - 1] if g > 0 else -1.0, value)
            value = jnp.where(ahead, rank[g + 1] if g < 2 else -1.0, value)
            done[g] = jnp.where(wanted[g] == float(slot), value, done[g])
    for g in range(3):
        nb3[g] = jnp.where(lane < 18, done[g], tables[g])
    collide_all(f, fluid, fc)
    planes_to_send(fc, zp)


def passing(fc, nb3, segments):
    lane = iota((ROWS, 128), 1)
    column, y = lane // 8, lane % 8
    segment = [column < 4, jnp.logical_and(column >= 4, column < 12), column >= 12]
    row1 = iota((ROWS, 1), 0)
    slots = iota((ROWS, ROWS), 1)
    tables = {g: nb3[g].astype(jnp.int32) for g in segments}

    def source_rows(g, d):
        if d == (0, 0, 0):
            return row1
        j = VELOCITY.index(d) - 1
        return tables[g][:, j : j + 1]

    def move(i, x, at_z):
        cx, cy, cz = VELOCITY[i]
        shift = (8 * cx + cy) % 128
        moved = pltpu.roll(x, shift, 1) if shift else x
        at_y = None
        if cy:
            at_y = y == (0 if cy > 0 else 7)
            moved = jnp.where(at_y, pltpu.roll(x, (8 * cx - 7 * cy) % 128, 1), moved)
        at_x = {}
        if cx > 0:
            at_x = {1: column == 4, 2: column == 12}
            edge = column == 0
        elif cx < 0:
            at_x = {0: column == 3, 1: column == 11}
            edge = column == 15
        parts = []
        for bx in (0, 1) if cx else (0,):
            for by in (0, 1) if cy else (0,):
                if not (bx or by or cz):
                    continue
                for g in segments:
                    if bx and g not in at_x:
                        continue
                    d = (-cx * bx, -cy * by, 0)
                    rows = source_rows(g, d)
                    if cz:
                        rows = jnp.where(at_z, source_rows(g, d[:2] + (-cz,)), rows)
                    mask = at_x[g] if bx else segment[g]
                    if by:
                        mask = jnp.logical_and(mask, at_y)
                    parts.append((mask, rows))
        if not parts:
            return moved
        picks = [(rows == slots).astype(F32) for _, rows in parts]
        taken = choose(jnp.concatenate(picks, axis=0).astype(BF16), moved)
        bounced = fc[OPPOSITE[i]]
        out = moved
        for n, (mask, rows) in enumerate(parts):
            value = jnp.where(rows >= 0, taken[ROWS * n : ROWS * n + ROWS], bounced)
            out = jnp.where(mask, value, out)
        if cx:
            out = jnp.where(edge, bounced, out)
        return out

    return move


def stream(fc, zg, nb3, f):
    z = lax.axis_index("z")
    below, above = (z + 1) % 2, z % 2
    move = passing(fc, nb3, (0, 1, 2))
    for i in range(19):
        if i in UP:
            k = UP.index(i)
            f[i] = move(i, zg[below, 0, ROWS * k : ROWS * (k + 1), :], z == 0)
        elif i in DOWN:
            k = DOWN.index(i)
            f[i] = move(i, zg[above, 1, ROWS * k : ROWS * (k + 1), :], z == PLANES - 1)
        else:
            f[i] = move(i, fc[i], None)


def step_kernel(fc, zg, nb3, fluid, fc_out, zp, f):
    stream(fc, zg, nb3, f)
    collide_all(f, fluid, fc_out)
    planes_to_send(fc_out, zp)


def last_kernel(fc_in, zg, nb3, fluid, out, f, fc):
    stream(fc_in, zg, nb3, f)
    collide_all(f, fluid, fc)
    z = lax.axis_index("z")
    first = lax.axis_index("core") == 0
    lane = iota((ROWS, 128), 1)
    move = passing(fc, nb3, (1,))
    left = [move(i, fc[i], None) for i in FLAT]
    left += [move(i, fc[i], z == PLANES - 1) for i in UP] + [None]
    right = [move(i, fc[i], z == 0) for i in DOWN]
    right += [fc[OPPOSITE[i]] for i in UP + DOWN]
    left_rest = [WEIGHTS[i] for i in FLAT + UP] + [0.0]
    right_rest = [WEIGHTS[i] for i in DOWN + UP + DOWN]
    values = []
    for p in range(15):
        value = pltpu.roll(right[p], 32, 1)
        if left[p] is not None:
            value = jnp.where(lane < 64, pltpu.roll(left[p], 96, 1), value)
        values.append(value)
    lane, slot = iota((SLOTS, 128), 1), iota((SLOTS, 128), 0)
    rank = jnp.broadcast_to(nb3[1, 0:1, :], (SLOTS, 128))
    rank = jnp.sum(jnp.where(lane == 64 + slot, rank, 0.0), axis=1, keepdims=True)
    picks = rank == iota((SLOTS, ROWS), 1).astype(F32)
    spread = choose(picks.astype(F32).astype(BF16), jnp.concatenate(values, axis=1))
    filled = rank >= 0.0
    out[:, 40:48, :] = jnp.zeros((PLANES, 8, 128), F32)
    for p in range(15):
        rest = jnp.where(lane < 64, left_rest[p], right_rest[p])
        value = jnp.where(filled, spread[:, 128 * p : 128 * p + 128], rest)
        for n in range(PLANES):
            a, b = value[6 * n : 6 * n + 3], value[6 * n + 3 : 6 * n + 6]
            out[n, 3 * p : 3 * p + 3, :] = jnp.where(first, a, b)


def unpack_kernel(got, nbr, out, x):
    lane, row = iota((48, 128), 1), iota((48, 128), 0)
    k, n = iota((128, 128), 0), iota((128, 128), 1)
    picks = (n == (k % 16) * 8 + k // 16).astype(F32).astype(BF16)
    place = iota((HELD, 128), 1)
    here_z, here_y = place // 16, place % 8
    absent = [nbr[:, j : j + 1] < 0 for j in range(18)]
    x[...] = jnp.zeros_like(x)

    def gathered(part):
        acc = None
        for z in range(PLANES):
            shift = (16 * z - 16 * part) % 128
            piece = pltpu.roll(got[z], shift, 1) if shift else got[z]
            acc = piece if acc is None else jnp.where(lane // 16 == z, piece, acc)
        return acc

    for q in range(4):
        a, b = gathered(q), gathered(4 + q)
        a = jnp.where(row >= 27, pltpu.roll(a, 16, 1), a)
        b = jnp.where(row < 15, pltpu.roll(b, 112, 1), b)
        here_x = 2 * q + (place % 16) // 8

        def missing(c):
            spots = []
            for size, here, top in zip(c, (here_x, here_y, here_z), (7, 7, 7)):
                spots.append(None if not size else here == (0 if size > 0 else top))
            found = jnp.zeros((HELD, 128), jnp.bool_)
            for flags in range(1, 8):
                across = [(flags >> s) & 1 for s in range(3)]
                if any(g and spot is None for g, spot in zip(across, spots)):
                    continue
                d = tuple(-size * g for size, g in zip(c, across))
                mask = jnp.broadcast_to(absent[VELOCITY.index(d) - 1], (HELD, 128))
                for g, spot in zip(across, spots):
                    if spot is not None:
                        mask = jnp.logical_and(mask, spot if g else jnp.logical_not(spot))
                found = jnp.logical_or(found, mask)
            return found

        for i in range(19):
            if i in UP:
                j = 3 * UP.index(i)
                bare = b[15 + j : 18 + j]
                value = jnp.where(missing(VELOCITY[i]), bare, a[27 + j : 30 + j])
            elif i in DOWN:
                j = 3 * DOWN.index(i)
                bare = b[30 + j : 33 + j]
                value = jnp.where(missing(VELOCITY[i]), bare, b[j : j + 3])
            else:
                j = 3 * FLAT.index(i)
                value = a[j : j + 3]
            x[64 * q + 3 * i : 64 * q + 3 * i + 3, :] = value
    y = permute_lanes(x[...], picks)
    for q in range(4):
        for i in range(19):
            for t in range(HELD):
                r = 64 * q + 3 * i + t
                out[t, i : i + 1, 128 * q : 128 * q + 128] = y[r : r + 1]


def call(kernel, outs, scratch, *args, smem=0, limit=8 * 1024 * 1024):
    spaces = [pltpu.SMEM] * smem + [pltpu.VMEM] * (len(args) - smem)
    many = isinstance(outs, list)
    shapes = [jax.ShapeDtypeStruct(s, F32) for s in (outs if many else [outs])]
    specs = [pl.BlockSpec(memory_space=pltpu.VMEM) for _ in shapes]
    return pl.pallas_call(
        kernel,
        out_shape=shapes if many else shapes[0],
        in_specs=[pl.BlockSpec(memory_space=s) for s in spaces],
        out_specs=specs if many else specs[0],
        scratch_shapes=[pltpu.VMEM(s, F32) for s in scratch],
        compiler_params=pltpu.CompilerParams(vmem_limit_bytes=limit),
        interpret=INTERPRET,
    )(*args)


def solution(mesh):
    slabs, group = mesh.shape["wide"], mesh.shape["narrow"]
    chips = group // 2
    axes = ("wide", "z", "core")
    fine = Mesh(mesh.devices.reshape(slabs, chips, 2), axes)

    def pairs(count, other, index):
        return [
            [index(a, b, c), index((a + 1) % count, b, c)]
            for c in range(2)
            for a in range(c, count, 2)
            for b in range(other)
        ]

    wide_pairs = pairs(slabs, chips, lambda w, z, c: (w * chips + z) * 2 + c)
    z_pairs = pairs(chips, 1, lambda z, _, c: z * 2 + c)

    def both_sides(x, names, groups):
        y = lax.all_gather(x, names, axis_index_groups=groups)
        return lax.all_gather(y, "core")

    def shards(pops_in, keep_slot, send_slot, send_dest, neighbours, fluid):
        packed = call(
            pack_kernel, (8, PACK, 128), [(PACK, 512), (PACK, 512)],
            keep_slot, send_slot, send_dest, neighbours, pops_in, fluid, smem=4,
            limit=None,
        )
        planes = lax.all_to_all(packed, "z", 0, 0, tiled=True)
        got = lax.all_gather(planes, "core").reshape(16 * PACK, 128)
        st, nb, xp = call(place_kernel, [(20, ROWS, 128), (ROWS, 128), (6 * ROWS, 128)], [], got)
        xg = both_sides(xp, axes, wide_pairs)
        state = (19, ROWS, 128)
        sent = (5 * ROWS, 128)
        fc, wet, nb3, zp = call(
            start_kernel, [state, (ROWS, 128), (3, ROWS, 128), sent], [state], st, nb, xg
        )
        for step in range(STEPS - 2):
            zg = both_sides(zp, ("z", "core"), z_pairs)
            fc, zp = call(step_kernel, [state, sent], [state], fc, zg, nb3, wet)
        zg = both_sides(zp, ("z", "core"), z_pairs)
        back = call(last_kernel, (chips, 48, 128), [state, state], fc, zg, nb3, wet)
        home = lax.all_to_all(back, "z", 0, 0, tiled=True)
        return call(unpack_kernel, (HELD, 19, 512), [(256, 128)], home, neighbours)

    placed = (P(axes, None, None), P(axes), P(axes), P(axes), P(axes, None), P(axes, None))
    return jax.shard_map(
        shards, mesh=fine, in_specs=placed, out_specs=P(axes, None, None), check_vma=False
    )
```

```python
import jax
import jax.numpy as jnp
from jax import lax
from jax.experimental import pallas as pl
from jax.experimental.pallas import tpu as pltpu
from jax.sharding import Mesh, PartitionSpec as P

STEPS = 4
HELD = 3
SLOTS = 48
ROWS = 32
PACK = 88
KIND = 15
TABLE_ROW = 59
ARRAYS = 30
PLANES = 8
INTERPRET = False

VELOCITY = [
    (0, 0, 0),
    (1, 0, 0), (-1, 0, 0), (0, 1, 0), (0, -1, 0), (0, 0, 1), (0, 0, -1),
    (1, 1, 0), (-1, -1, 0), (1, -1, 0), (-1, 1, 0),
    (1, 0, 1), (-1, 0, -1), (1, 0, -1), (-1, 0, 1),
    (0, 1, 1), (0, -1, -1), (0, 1, -1), (0, -1, 1),
]
WEIGHTS = [1.0 / 3.0] + [1.0 / 18.0] * 6 + [1.0 / 36.0] * 12
OPPOSITE = [0, 2, 1, 4, 3, 6, 5, 8, 7, 10, 9, 12, 11, 14, 13, 16, 15, 18, 17]
UP = [i for i in range(19) if VELOCITY[i][2] == 1]
FLAT = [i for i in range(19) if VELOCITY[i][2] == 0]
DOWN = [i for i in range(19) if VELOCITY[i][2] == -1]
NU_ZERO = 0.1
NU_LIMIT = 0.01
LAMBDA_TIME = 10.0
POWER_INDEX = 0.35
OMEGA_ZERO = 1.0 / (3.0 * NU_ZERO + 0.5)
SHEAR_SCALE = 2.1213203435596424
RATE_SCALE = (LAMBDA_TIME * SHEAR_SCALE * OMEGA_ZERO) ** 2
F32 = jnp.float32
BF16 = jnp.bfloat16


def iota(shape, dim):
    return lax.broadcasted_iota(jnp.int32, shape, dim)


def dot(a, b):
    return jnp.dot(a, b, preferred_element_type=F32)


def split(x):
    high = x.astype(BF16)
    rest = x - high.astype(F32)
    middle = rest.astype(BF16)
    low = (rest - middle.astype(F32)).astype(BF16)
    return high, middle, low


def choose(picks, x):
    n = x.shape[1]
    y = dot(picks, jnp.concatenate(split(x), axis=1))
    return y[:, :n] + y[:, n : 2 * n] + y[:, 2 * n :]


def permute_lanes(x, picks):
    m = x.shape[0]
    y = dot(jnp.concatenate(split(x), axis=0), picks)
    return y[:m] + y[m : 2 * m] + y[2 * m :]


def collide(f, fluid):
    def total(indices):
        out = None
        for i in indices:
            out = f[i] if out is None else out + f[i]
        return out

    rho = total(range(19))
    inverse = 1.0 / rho
    u = []
    for a in range(3):
        plus = total([i for i in range(19) if VELOCITY[i][a] == 1])
        minus = total([i for i in range(19) if VELOCITY[i][a] == -1])
        u.append((plus - minus) * inverse)
    base = 1.0 - 1.5 * (u[0] * u[0] + u[1] * u[1] + u[2] * u[2])
    excess = [f[0] - WEIGHTS[0] * rho * base]
    scaled = {}
    for i in range(1, 19, 2):
        c = VELOCITY[i]
        along = None
        for a in range(3):
            if c[a]:
                term = u[a]
                if along is None:
                    along = term if c[a] > 0 else -term
                else:
                    along = along + term if c[a] > 0 else along - term
        if WEIGHTS[i] not in scaled:
            scaled[WEIGHTS[i]] = WEIGHTS[i] * rho
        even = base + 4.5 * along * along
        odd = 3.0 * along
        excess.append(f[i] - scaled[WEIGHTS[i]] * (even + odd))
        excess.append(f[i + 1] - scaled[WEIGHTS[i]] * (even - odd))
    stress = None
    for a in range(3):
        for b in range(a, 3):
            part = None
            for i in range(1, 19):
                sign = VELOCITY[i][a] * VELOCITY[i][b]
                if sign:
                    if part is None:
                        part = excess[i] if sign > 0 else -excess[i]
                    else:
                        part = part + excess[i] if sign > 0 else part - excess[i]
            square = part * part if a == b else 2.0 * (part * part)
            stress = square if stress is None else stress + square
    grown = 1.0 + RATE_SCALE * stress * inverse * inverse
    thinned = jnp.exp(((POWER_INDEX - 1.0) / 2.0) * jnp.log(grown))
    viscosity = NU_LIMIT + (NU_ZERO - NU_LIMIT) * thinned
    rate = 1.0 / (3.0 * viscosity + 0.5)
    wet = fluid == 1.0
    return [jnp.where(wet, f[i] - rate * excess[i], f[OPPOSITE[i]]) for i in range(19)]


def collide_all(f_ref, fluid_ref, fc_ref):
    for g in range(ROWS // 8):
        rows = slice(8 * g, 8 * g + 8)
        done = collide([f_ref[i, rows, :] for i in range(19)], fluid_ref[rows, :])
        for i in range(19):
            fc_ref[i, rows, :] = done[i]


def planes_to_send(fc_ref, zp_ref):
    z = lax.axis_index("z")
    up = ((z + lax.axis_index("core")) % 2) == 0
    for k in range(5):
        @pl.when(up)
        def _():
            zp_ref[ROWS * k : ROWS * (k + 1), :] = fc_ref[UP[k]]

        @pl.when(jnp.logical_not(up))
        def _():
            zp_ref[ROWS * k : ROWS * (k + 1), :] = fc_ref[DOWN[k]]


def pack_kernel(keep, send, dest, nbr, pops, fluid, out, xa, xb, raw):
    xa[...] = jnp.zeros_like(xa)
    xb[...] = jnp.zeros_like(xb)
    raw[...] = jnp.ones_like(raw)
    for s in range(5):
        slot = jnp.maximum(keep[s] if s < HELD else send[s - HELD], 0)
        xa[KIND * s : KIND * s + 15, :] = pops[slot, 0:15, :]
        xb[KIND * s : KIND * s + 4, :] = pops[slot, 15:19, :]
        for i in range(19):
            raw[i, s : s + 1, :] = pops[slot, i : i + 1, :]
    walls = fluid[...].astype(F32)
    for t in range(HELD):
        xb[KIND * t + 14 : KIND * t + 15, :] = walls[t : t + 1]
    xa[85:88, :] = walls
    xb[85:88, :] = walls
    for j in range(2):
        for k in range(5):
            r = 75 + 5 * j + k
            xa[r : r + 1, :] = raw[OPPOSITE[UP[k]], HELD + j : HELD + j + 1, :]
            xb[r : r + 1, :] = raw[OPPOSITE[DOWN[k]], HELD + j : HELD + j + 1, :]
    walls = jnp.concatenate([walls, jnp.ones((8 - HELD, 512), F32)], axis=0)
    slots = jnp.full((8, 128), -1, jnp.int32)
    for s in range(5):
        slot = keep[s] if s < HELD else send[s - HELD]
        slots = jnp.where(iota((8, 128), 0) == s, slot, slots)
    for q in range(4):
        cells = slice(128 * q, 128 * q + 128)
        done = [jnp.where(slots >= 0, raw[i, :, cells], WEIGHTS[i]) for i in range(19)]
        done = collide(done, walls[:, cells])
        for k in range(5):
            for s in range(5):
                r = KIND * s + 4 + k
                xb[r : r + 1, cells] = done[UP[k]][s : s + 1]
                xb[r + 5 : r + 6, cells] = done[DOWN[k]][s : s + 1]
    k, n = iota((128, 128), 0), iota((128, 128), 1)
    picks = (n == (k % 8) * 16 + k // 8).astype(F32).astype(BF16)
    tiles = [x[:, 128 * q : 128 * q + 128] for x in (xa, xb) for q in range(4)]
    y = permute_lanes(jnp.concatenate(tiles, axis=0), picks)
    lane, row = iota((PACK, 128), 1), iota((PACK, 128), 0)
    kind, late = row % KIND, row >= 75
    rising = jnp.logical_and(jnp.logical_and(kind >= 4, kind < 9), jnp.logical_not(late))
    falling = jnp.logical_or(jnp.logical_and(kind >= 9, kind < 14), late)
    parts = []
    for part in range(8):
        piece = y[PACK * part : PACK * part + PACK]
        if part < 4:
            piece = jnp.where(late, pltpu.roll(piece, 16, 1), piece)
        else:
            moved = jnp.where(falling, pltpu.roll(piece, 112, 1), piece)
            piece = jnp.where(rising, pltpu.roll(piece, 16, 1), moved)
        parts.append(piece)
    values = [keep[t] for t in range(3)] + [dest[j] for j in range(2)]
    values = list(enumerate(values)) + [
        (10 + 18 * t + j, nbr[t, j]) for t in range(3) for j in range(18)
    ]
    line = iota((8, 128), 1)
    table = jnp.zeros((8, 128), jnp.int32)
    for place, value in values:
        table = jnp.where(line == 64 + place, value, table)
    table = jnp.concatenate([table.astype(F32)] * (PACK // 8), axis=0)
    marked = jnp.logical_and(row == TABLE_ROW, lane >= 64)
    for z in range(PLANES):
        acc = None
        for part in range(8):
            shift = (16 * part - 16 * z) % 128
            piece = pltpu.roll(parts[part], shift, 1) if shift else parts[part]
            acc = piece if acc is None else jnp.where(lane // 16 == part, piece, acc)
        out[z] = jnp.where(marked, table, acc)


def place_kernel(got, st, nb, xp):
    def of_all(row):
        return got[pl.ds(row, 16, stride=PACK), :]

    tables = of_all(TABLE_ROW)
    row16 = iota((SLOTS, 16), 0)
    lane16 = iota((SLOTS, 16), 1)
    m16 = row16 // 3
    whose = (m16 % 2) * 8 + m16 // 2
    picks = (lane16 == whose).astype(F32).astype(BF16)
    mine = dot(picks, tables.astype(BF16))
    lane, row = iota((SLOTS, 128), 1), iota((SLOTS, 128), 0)
    t = row % 3
    kept = jnp.sum(jnp.where(lane == 64 + t, mine, 0.0), axis=1, keepdims=True)
    eye = iota((16, 16), 0) == iota((16, 16), 1)
    lane_t = iota((16, 128), 1)
    found = jnp.full((SLOTS, 1), -1.0, F32)
    for j in range(2):
        column = jnp.sum(jnp.where(lane_t == 67 + j, tables, 0.0), axis=1, keepdims=True)
        diagonal = jnp.where(eye, column, 0.0).astype(BF16)
        targets = dot(jnp.ones((SLOTS, 16), BF16), diagonal)
        hit = targets == row16.astype(F32)
        where_from = jnp.where(hit, lane16 + 16 * (HELD + j) + 1, 0)
        found = found + jnp.sum(where_from.astype(F32), axis=1, keepdims=True)
    row1 = iota((SLOTS, 1), 0)
    m1 = row1 // 3
    own = ((m1 % 2) * 8 + m1 // 2 + (row1 % 3) * 16).astype(F32)
    source = jnp.where(kept >= 0.0, own, found)
    occupied = (source >= 0.0).astype(F32)
    ones = jnp.ones((ROWS, SLOTS), BF16)

    def ranks(first, width):
        r, slot = iota((SLOTS, width), 0), iota((SLOTS, width), 1) - first
        earlier = dot(ones, jnp.where(r < slot, occupied, 0.0).astype(BF16))
        full = dot(ones, jnp.where(r == slot, occupied, 0.0).astype(BF16))
        return jnp.where(full > 0.5, earlier, -1.0)

    rank = ranks(0, SLOTS)
    picks = (rank == iota((ROWS, SLOTS), 0).astype(F32)).astype(F32).astype(BF16)
    codes = jnp.zeros((SLOTS, 128), F32)
    for k in range(3):
        codes = jnp.where(t == k, pltpu.roll(mine, (128 - 74 - 18 * k) % 128, 1), codes)
    codes = jnp.where(lane == 18, source, codes)
    codes = jnp.where(lane == 19, own, codes)
    codes = choose(picks, codes)
    source, own = codes[:, 18:19], codes[:, 19:20]

    def one_hot(index, width):
        return (iota((ROWS, width), 1).astype(F32) == index).astype(F32).astype(BF16)

    def stacked(first, step, count):
        return jnp.concatenate([of_all(first + step * s) for s in range(count)], axis=0)

    lines = jnp.concatenate([stacked(p, KIND, 5) for p in range(KIND)], axis=1)
    lines = choose(one_hot(source, 80), lines)
    turned = jnp.concatenate([stacked(75 + k, 5, 2) for k in range(5)], axis=1)
    turned = choose(one_hot(source - 48.0, 32), turned)
    walls = jnp.concatenate([stacked(14, KIND, 3), stacked(85, 1, 3)], axis=1)
    walls = choose(one_hot(own, SLOTS), walls)

    def line(n):
        value = lines[:, 128 * (n % KIND) : 128 * (n % KIND) + 128]
        return pltpu.roll(value, 32 if n < KIND else 96, 1)

    for i in range(19):
        st[i] = line(i)
    st[19] = pltpu.roll(walls[:, 0:128], 96, 1)
    moved = source >= 48.0
    for side in range(2):
        wall = pltpu.roll(walls[:, 128:256], 96 if side else 32, 1) != 1.0
        for k in range(5):
            back = pltpu.roll(turned[:, 128 * k : 128 * k + 128], 96 if side else 32, 1)
            arriving = line(19 + 5 * side + k)
            st[20 + 5 * side + k] = jnp.where(jnp.logical_and(moved, wall), back, arriving)
    lane = iota((ROWS, 128), 1)
    codes = jnp.where(lane < 18, codes, ranks(64, 128))
    nb[...] = codes
    to_right = ((lax.axis_index("wide") + lax.axis_index("core")) % 2) == 0
    for q in range(8):
        acc = jnp.zeros((ROWS, 128), F32)
        for k in range(4):
            if 4 * q + k >= ARRAYS:
                continue
            value = st[4 * q + k]
            half = jnp.where(to_right, pltpu.roll(value, 64, 1), pltpu.roll(value, 96, 1))
            half = pltpu.roll(half, 32 * k, 1) if k else half
            acc = jnp.where(lane // 32 == k, half, acc)
        xp[ROWS * q : ROWS * q + ROWS, :] = acc
    xp[ROWS * 8 : ROWS * 9, :] = codes


def start_kernel(st, nb, xg, fc_out, fluid, nb3, zp, f, fc, arriving):
    w = lax.axis_index("wide")
    lane = iota((ROWS, 128), 1)
    left, right = (w + 1) % 2, w % 2
    for i in range(ARRAYS):
        rows = slice(ROWS * (i // 4), ROWS * (i // 4) + ROWS)
        from_left = xg[left, 0, rows, :]
        from_right = xg[right, 1, rows, :]
        shift = (128 - 32 * (i % 4)) % 128
        from_left = pltpu.roll(from_left, shift, 1) if shift else from_left
        shift = (224 - 32 * (i % 4)) % 128
        from_right = pltpu.roll(from_right, shift, 1) if shift else from_right
        value = jnp.where(lane < 32, from_left, jnp.where(lane < 96, st[i], from_right))
        if i < 19:
            f[i] = value
        elif i == 19:
            fluid[...] = value
        else:
            arriving[i - 20] = value
    last = slice(ROWS * 8, ROWS * 9)
    tables = [xg[left, 0, last, :], nb[...], xg[right, 1, last, :]]
    back, ahead = lane < 0, lane < 0
    for j in range(18):
        if VELOCITY[j + 1][0] < 0:
            back = jnp.logical_or(back, lane == j)
        elif VELOCITY[j + 1][0] > 0:
            ahead = jnp.logical_or(ahead, lane == j)
    base = jnp.where(ahead, 2.0 * SLOTS, jnp.where(back, 0.0, 1.0 * SLOTS))
    wanted = [jnp.where(table >= 0.0, table - base, -1.0) for table in tables]
    done = [jnp.full((ROWS, 128), -1.0, F32) for _ in range(3)]
    for slot in range(SLOTS):
        rank = [table[:, 64 + slot : 65 + slot] for table in tables]
        for g in range(3):
            value = jnp.broadcast_to(rank[g], (ROWS, 128))
            value = jnp.where(back, rank[g - 1] if g > 0 else -1.0, value)
            value = jnp.where(ahead, rank[g + 1] if g < 2 else -1.0, value)
            done[g] = jnp.where(wanted[g] == float(slot), value, done[g])
    for g in range(3):
        nb3[g] = jnp.where(lane < 18, done[g], tables[g])
    collide_all(f, fluid, fc)
    stream(fc, lambda k: arriving[k], lambda k: arriving[5 + k], nb3, f)
    collide_all(f, fluid, fc_out)
    planes_to_send(fc_out, zp)


def passing(fc, nb3, segments):
    lane = iota((ROWS, 128), 1)
    column, y = lane // 8, lane % 8
    segment = [column < 4, jnp.logical_and(column >= 4, column < 12), column >= 12]
    row1 = iota((ROWS, 1), 0)
    slots = iota((ROWS, ROWS), 1)
    tables = {g: nb3[g].astype(jnp.int32) for g in segments}

    def source_rows(g, d):
        if d == (0, 0, 0):
            return row1
        j = VELOCITY.index(d) - 1
        return tables[g][:, j : j + 1]

    def move(i, x, at_z):
        cx, cy, cz = VELOCITY[i]
        shift = (8 * cx + cy) % 128
        moved = pltpu.roll(x, shift, 1) if shift else x
        at_y = None
        if cy:
            at_y = y == (0 if cy > 0 else 7)
            moved = jnp.where(at_y, pltpu.roll(x, (8 * cx - 7 * cy) % 128, 1), moved)
        at_x = {}
        if cx > 0:
            at_x = {1: column == 4, 2: column == 12}
            edge = column == 0
        elif cx < 0:
            at_x = {0: column == 3, 1: column == 11}
            edge = column == 15
        parts = []
        for bx in (0, 1) if cx else (0,):
            for by in (0, 1) if cy else (0,):
                if not (bx or by or cz):
                    continue
                for g in segments:
                    if bx and g not in at_x:
                        continue
                    d = (-cx * bx, -cy * by, 0)
                    rows = source_rows(g, d)
                    if cz:
                        rows = jnp.where(at_z, source_rows(g, d[:2] + (-cz,)), rows)
                    mask = at_x[g] if bx else segment[g]
                    if by:
                        mask = jnp.logical_and(mask, at_y)
                    parts.append((mask, rows))
        if not parts:
            return moved
        picks = [(rows == slots).astype(F32) for _, rows in parts]
        taken = choose(jnp.concatenate(picks, axis=0).astype(BF16), moved)
        bounced = fc[OPPOSITE[i]]
        out = moved
        for n, (mask, rows) in enumerate(parts):
            value = jnp.where(rows >= 0, taken[ROWS * n : ROWS * n + ROWS], bounced)
            out = jnp.where(mask, value, out)
        if cx:
            out = jnp.where(edge, bounced, out)
        return out

    return move


def stream(fc, from_below, from_above, nb3, f):
    z = lax.axis_index("z")
    move = passing(fc, nb3, (0, 1, 2))
    for i in range(19):
        if i in UP:
            f[i] = move(i, from_below(UP.index(i)), z == 0)
        elif i in DOWN:
            f[i] = move(i, from_above(DOWN.index(i)), z == PLANES - 1)
        else:
            f[i] = move(i, fc[i], None)


def exchanged(zg):
    z = lax.axis_index("z")
    below, above = (z + 1) % 2, z % 2
    return (
        lambda k: zg[below, 0, ROWS * k : ROWS * (k + 1), :],
        lambda k: zg[above, 1, ROWS * k : ROWS * (k + 1), :],
    )


def step_kernel(fc, zg, nb3, fluid, fc_out, zp, f):
    stream(fc, *exchanged(zg), nb3, f)
    collide_all(f, fluid, fc_out)
    planes_to_send(fc_out, zp)


def last_kernel(fc_in, zg, nb3, fluid, out, f, fc):
    stream(fc_in, *exchanged(zg), nb3, f)
    collide_all(f, fluid, fc)
    z = lax.axis_index("z")
    first = lax.axis_index("core") == 0
    lane = iota((ROWS, 128), 1)
    move = passing(fc, nb3, (1,))
    left = [move(i, fc[i], None) for i in FLAT]
    left += [move(i, fc[i], z == PLANES - 1) for i in UP] + [None]
    right = [move(i, fc[i], z == 0) for i in DOWN]
    right += [fc[OPPOSITE[i]] for i in UP + DOWN]
    left_rest = [WEIGHTS[i] for i in FLAT + UP] + [0.0]
    right_rest = [WEIGHTS[i] for i in DOWN + UP + DOWN]
    values = []
    for p in range(15):
        value = pltpu.roll(right[p], 32, 1)
        if left[p] is not None:
            value = jnp.where(lane < 64, pltpu.roll(left[p], 96, 1), value)
        values.append(value)
    lane, slot = iota((SLOTS, 128), 1), iota((SLOTS, 128), 0)
    rank = jnp.broadcast_to(nb3[1, 0:1, :], (SLOTS, 128))
    rank = jnp.sum(jnp.where(lane == 64 + slot, rank, 0.0), axis=1, keepdims=True)
    picks = rank == iota((SLOTS, ROWS), 1).astype(F32)
    spread = choose(picks.astype(F32).astype(BF16), jnp.concatenate(values, axis=1))
    filled = rank >= 0.0
    out[:, 40:48, :] = jnp.zeros((PLANES, 8, 128), F32)
    for p in range(15):
        rest = jnp.where(lane < 64, left_rest[p], right_rest[p])
        value = jnp.where(filled, spread[:, 128 * p : 128 * p + 128], rest)
        for n in range(PLANES):
            a, b = value[6 * n : 6 * n + 3], value[6 * n + 3 : 6 * n + 6]
            out[n, 3 * p : 3 * p + 3, :] = jnp.where(first, a, b)


def unpack_kernel(got, nbr, out, x):
    lane, row = iota((48, 128), 1), iota((48, 128), 0)
    k, n = iota((128, 128), 0), iota((128, 128), 1)
    picks = (n == (k % 16) * 8 + k // 16).astype(F32).astype(BF16)
    place = iota((HELD, 128), 1)
    here_z, here_y = place // 16, place % 8
    absent = [nbr[:, j : j + 1] < 0 for j in range(18)]
    x[...] = jnp.zeros_like(x)

    def gathered(part):
        acc = None
        for z in range(PLANES):
            shift = (16 * z - 16 * part) % 128
            piece = pltpu.roll(got[z], shift, 1) if shift else got[z]
            acc = piece if acc is None else jnp.where(lane // 16 == z, piece, acc)
        return acc

    for q in range(4):
        a, b = gathered(q), gathered(4 + q)
        a = jnp.where(row >= 27, pltpu.roll(a, 16, 1), a)
        b = jnp.where(row < 15, pltpu.roll(b, 112, 1), b)
        here_x = 2 * q + (place % 16) // 8

        def missing(c):
            spots = []
            for size, here, top in zip(c, (here_x, here_y, here_z), (7, 7, 7)):
                spots.append(None if not size else here == (0 if size > 0 else top))
            found = jnp.zeros((HELD, 128), jnp.bool_)
            for flags in range(1, 8):
                across = [(flags >> s) & 1 for s in range(3)]
                if any(g and spot is None for g, spot in zip(across, spots)):
                    continue
                d = tuple(-size * g for size, g in zip(c, across))
                mask = jnp.broadcast_to(absent[VELOCITY.index(d) - 1], (HELD, 128))
                for g, spot in zip(across, spots):
                    if spot is not None:
                        mask = jnp.logical_and(mask, spot if g else jnp.logical_not(spot))
                found = jnp.logical_or(found, mask)
            return found

        for i in range(19):
            if i in UP:
                j = 3 * UP.index(i)
                bare = b[15 + j : 18 + j]
                value = jnp.where(missing(VELOCITY[i]), bare, a[27 + j : 30 + j])
            elif i in DOWN:
                j = 3 * DOWN.index(i)
                bare = b[30 + j : 33 + j]
                value = jnp.where(missing(VELOCITY[i]), bare, b[j : j + 3])
            else:
                j = 3 * FLAT.index(i)
                value = a[j : j + 3]
            x[64 * q + 3 * i : 64 * q + 3 * i + 3, :] = value
    y = permute_lanes(x[...], picks)
    for q in range(4):
        for i in range(19):
            for t in range(HELD):
                r = 64 * q + 3 * i + t
                out[t, i : i + 1, 128 * q : 128 * q + 128] = y[r : r + 1]


def call(kernel, outs, scratch, *args, smem=0, limit=8 * 1024 * 1024):
    spaces = [pltpu.SMEM] * smem + [pltpu.VMEM] * (len(args) - smem)
    many = isinstance(outs, list)
    shapes = [jax.ShapeDtypeStruct(s, F32) for s in (outs if many else [outs])]
    specs = [pl.BlockSpec(memory_space=pltpu.VMEM) for _ in shapes]
    return pl.pallas_call(
        kernel,
        out_shape=shapes if many else shapes[0],
        in_specs=[pl.BlockSpec(memory_space=s) for s in spaces],
        out_specs=specs if many else specs[0],
        scratch_shapes=[pltpu.VMEM(s, F32) for s in scratch],
        compiler_params=pltpu.CompilerParams(vmem_limit_bytes=limit),
        interpret=INTERPRET,
    )(*args)


def solution(mesh):
    slabs, group = mesh.shape["wide"], mesh.shape["narrow"]
    chips = group // 2
    axes = ("wide", "z", "core")
    fine = Mesh(mesh.devices.reshape(slabs, chips, 2), axes)

    def pairs(count, other, index):
        return [
            [index(a, b, c), index((a + 1) % count, b, c)]
            for c in range(2)
            for a in range(c, count, 2)
            for b in range(other)
        ]

    wide_pairs = pairs(slabs, chips, lambda w, z, c: (w * chips + z) * 2 + c)
    z_pairs = pairs(chips, 1, lambda z, _, c: z * 2 + c)

    def both_sides(x, names, groups):
        y = lax.all_gather(x, names, axis_index_groups=groups)
        return lax.all_gather(y, "core")

    def shards(pops_in, keep_slot, send_slot, send_dest, neighbours, fluid):
        packed = call(
            pack_kernel, (chips, PACK, 128), [(PACK, 512), (PACK, 512), (19, 8, 512)],
            keep_slot, send_slot, send_dest, neighbours, pops_in, fluid, smem=4,
            limit=None,
        )
        planes = lax.all_to_all(packed, "z", 0, 0, tiled=True)
        got = lax.all_gather(planes, "core").reshape(group * PACK, 128)
        st, nb, xp = call(
            place_kernel, [(ARRAYS, ROWS, 128), (ROWS, 128), (9 * ROWS, 128)], [], got
        )
        xg = both_sides(xp, axes, wide_pairs)
        state = (19, ROWS, 128)
        sent = (5 * ROWS, 128)
        fc, wet, nb3, zp = call(
            start_kernel, [state, (ROWS, 128), (3, ROWS, 128), sent],
            [state, state, (10, ROWS, 128)], st, nb, xg,
        )
        for step in range(STEPS - 3):
            zg = both_sides(zp, ("z", "core"), z_pairs)
            fc, zp = call(step_kernel, [state, sent], [state], fc, zg, nb3, wet)
        zg = both_sides(zp, ("z", "core"), z_pairs)
        back = call(last_kernel, (chips, 48, 128), [state, state], fc, zg, nb3, wet)
        home = lax.all_to_all(back, "z", 0, 0, tiled=True)
        return call(unpack_kernel, (HELD, 19, 512), [(256, 128)], home, neighbours)

    placed = (P(axes, None, None), P(axes), P(axes), P(axes), P(axes, None), P(axes, None))
    return jax.shard_map(
        shards, mesh=fine, in_specs=placed, out_specs=P(axes, None, None), check_vma=False
    )
```

```python
import jax
import jax.numpy as jnp
from jax import lax
from jax.experimental import pallas as pl
from jax.experimental.pallas import tpu as pltpu
from jax.sharding import Mesh, PartitionSpec as P

STEPS = 4
HELD = 3
SLOTS = 48
ROWS = 32
PACK = 88
KIND = 15
TABLE_ROW = 59
ARRAYS = 30
PLANES = 8
INTERPRET = False

VELOCITY = [
    (0, 0, 0),
    (1, 0, 0), (-1, 0, 0), (0, 1, 0), (0, -1, 0), (0, 0, 1), (0, 0, -1),
    (1, 1, 0), (-1, -1, 0), (1, -1, 0), (-1, 1, 0),
    (1, 0, 1), (-1, 0, -1), (1, 0, -1), (-1, 0, 1),
    (0, 1, 1), (0, -1, -1), (0, 1, -1), (0, -1, 1),
]
WEIGHTS = [1.0 / 3.0] + [1.0 / 18.0] * 6 + [1.0 / 36.0] * 12
OPPOSITE = [0, 2, 1, 4, 3, 6, 5, 8, 7, 10, 9, 12, 11, 14, 13, 16, 15, 18, 17]
UP = [i for i in range(19) if VELOCITY[i][2] == 1]
FLAT = [i for i in range(19) if VELOCITY[i][2] == 0]
DOWN = [i for i in range(19) if VELOCITY[i][2] == -1]
NU_ZERO = 0.1
NU_LIMIT = 0.01
LAMBDA_TIME = 10.0
POWER_INDEX = 0.35
OMEGA_ZERO = 1.0 / (3.0 * NU_ZERO + 0.5)
SHEAR_SCALE = 2.1213203435596424
RATE_SCALE = (LAMBDA_TIME * SHEAR_SCALE * OMEGA_ZERO) ** 2
F32 = jnp.float32
BF16 = jnp.bfloat16


def iota(shape, dim):
    return lax.broadcasted_iota(jnp.int32, shape, dim)


def dot(a, b):
    return jnp.dot(a, b, preferred_element_type=F32)


def split(x):
    high = x.astype(BF16)
    rest = x - high.astype(F32)
    middle = rest.astype(BF16)
    low = (rest - middle.astype(F32)).astype(BF16)
    return high, middle, low


def choose(picks, x):
    n = x.shape[1]
    y = dot(picks, jnp.concatenate(split(x), axis=1))
    return y[:, :n] + y[:, n : 2 * n] + y[:, 2 * n :]


def permute_lanes(x, picks):
    m = x.shape[0]
    y = dot(jnp.concatenate(split(x), axis=0), picks)
    return y[:m] + y[m : 2 * m] + y[2 * m :]


def collide(f, fluid):
    def total(indices):
        out = None
        for i in indices:
            out = f[i] if out is None else out + f[i]
        return out

    rho = total(range(19))
    inverse = 1.0 / rho
    u = []
    for a in range(3):
        plus = total([i for i in range(19) if VELOCITY[i][a] == 1])
        minus = total([i for i in range(19) if VELOCITY[i][a] == -1])
        u.append((plus - minus) * inverse)
    base = 1.0 - 1.5 * (u[0] * u[0] + u[1] * u[1] + u[2] * u[2])
    excess = [f[0] - WEIGHTS[0] * rho * base]
    scaled = {}
    for i in range(1, 19, 2):
        c = VELOCITY[i]
        along = None
        for a in range(3):
            if c[a]:
                term = u[a]
                if along is None:
                    along = term if c[a] > 0 else -term
                else:
                    along = along + term if c[a] > 0 else along - term
        if WEIGHTS[i] not in scaled:
            scaled[WEIGHTS[i]] = WEIGHTS[i] * rho
        even = base + 4.5 * along * along
        odd = 3.0 * along
        excess.append(f[i] - scaled[WEIGHTS[i]] * (even + odd))
        excess.append(f[i + 1] - scaled[WEIGHTS[i]] * (even - odd))
    stress = None
    for a in range(3):
        for b in range(a, 3):
            part = None
            for i in range(1, 19):
                sign = VELOCITY[i][a] * VELOCITY[i][b]
                if sign:
                    if part is None:
                        part = excess[i] if sign > 0 else -excess[i]
                    else:
                        part = part + excess[i] if sign > 0 else part - excess[i]
            square = part * part if a == b else 2.0 * (part * part)
            stress = square if stress is None else stress + square
    grown = 1.0 + RATE_SCALE * stress * inverse * inverse
    thinned = jnp.exp(((POWER_INDEX - 1.0) / 2.0) * jnp.log(grown))
    viscosity = NU_LIMIT + (NU_ZERO - NU_LIMIT) * thinned
    rate = 1.0 / (3.0 * viscosity + 0.5)
    wet = fluid == 1.0
    return [jnp.where(wet, f[i] - rate * excess[i], f[OPPOSITE[i]]) for i in range(19)]


def collide_all(f_ref, fluid_ref, fc_ref):
    for g in range(ROWS // 8):
        rows = slice(8 * g, 8 * g + 8)
        done = collide([f_ref[i, rows, :] for i in range(19)], fluid_ref[rows, :])
        for i in range(19):
            fc_ref[i, rows, :] = done[i]


def planes_to_send(fc_ref, zp_ref):
    z = lax.axis_index("z")
    up = ((z + lax.axis_index("core")) % 2) == 0
    for k in range(5):
        @pl.when(up)
        def _():
            zp_ref[ROWS * k : ROWS * (k + 1), :] = fc_ref[UP[k]]

        @pl.when(jnp.logical_not(up))
        def _():
            zp_ref[ROWS * k : ROWS * (k + 1), :] = fc_ref[DOWN[k]]


def pack_kernel(keep, send, dest, nbr, pops, fluid, out, xa, xb, raw):
    xa[...] = jnp.zeros_like(xa)
    xb[...] = jnp.zeros_like(xb)
    raw[...] = jnp.ones_like(raw)
    for s in range(5):
        slot = jnp.maximum(keep[s] if s < HELD else send[s - HELD], 0)
        xa[KIND * s : KIND * s + 15, :] = pops[slot, 0:15, :]
        xb[KIND * s : KIND * s + 4, :] = pops[slot, 15:19, :]
        for i in range(19):
            raw[i, s : s + 1, :] = pops[slot, i : i + 1, :]
    walls = fluid[...].astype(F32)
    for t in range(HELD):
        xb[KIND * t + 14 : KIND * t + 15, :] = walls[t : t + 1]
    xa[85:88, :] = walls
    xb[85:88, :] = walls
    for j in range(2):
        for k in range(5):
            r = 75 + 5 * j + k
            xa[r : r + 1, :] = raw[OPPOSITE[UP[k]], HELD + j : HELD + j + 1, :]
            xb[r : r + 1, :] = raw[OPPOSITE[DOWN[k]], HELD + j : HELD + j + 1, :]
    walls = jnp.concatenate([walls, jnp.ones((8 - HELD, 512), F32)], axis=0)
    slots = jnp.full((8, 128), -1, jnp.int32)
    for s in range(5):
        slot = keep[s] if s < HELD else send[s - HELD]
        slots = jnp.where(iota((8, 128), 0) == s, slot, slots)
    for q in range(4):
        cells = slice(128 * q, 128 * q + 128)
        done = [jnp.where(slots >= 0, raw[i, :, cells], WEIGHTS[i]) for i in range(19)]
        done = collide(done, walls[:, cells])
        for k in range(5):
            for s in range(5):
                r = KIND * s + 4 + k
                xb[r : r + 1, cells] = done[UP[k]][s : s + 1]
                xb[r + 5 : r + 6, cells] = done[DOWN[k]][s : s + 1]
    k, n = iota((128, 128), 0), iota((128, 128), 1)
    picks = (n == (k % 8) * 16 + k // 8).astype(F32).astype(BF16)
    tiles = [x[:, 128 * q : 128 * q + 128] for x in (xa, xb) for q in range(4)]
    y = permute_lanes(jnp.concatenate(tiles, axis=0), picks)
    lane, row = iota((PACK, 128), 1), iota((PACK, 128), 0)
    kind, late = row % KIND, row >= 75
    rising = jnp.logical_and(jnp.logical_and(kind >= 4, kind < 9), jnp.logical_not(late))
    falling = jnp.logical_or(jnp.logical_and(kind >= 9, kind < 14), late)
    parts = []
    for part in range(8):
        piece = y[PACK * part : PACK * part + PACK]
        if part < 4:
            piece = jnp.where(late, pltpu.roll(piece, 16, 1), piece)
        else:
            moved = jnp.where(falling, pltpu.roll(piece, 112, 1), piece)
            piece = jnp.where(rising, pltpu.roll(piece, 16, 1), moved)
        parts.append(piece)
    values = [keep[t] for t in range(3)] + [dest[j] for j in range(2)]
    values = list(enumerate(values)) + [
        (10 + 18 * t + j, nbr[t, j]) for t in range(3) for j in range(18)
    ]
    line = iota((8, 128), 1)
    table = jnp.zeros((8, 128), jnp.int32)
    for place, value in values:
        table = jnp.where(line == 64 + place, value, table)
    table = jnp.concatenate([table.astype(F32)] * (PACK // 8), axis=0)
    marked = jnp.logical_and(row == TABLE_ROW, lane >= 64)
    for z in range(PLANES):
        acc = None
        for part in range(8):
            shift = (16 * part - 16 * z) % 128
            piece = pltpu.roll(parts[part], shift, 1) if shift else parts[part]
            acc = piece if acc is None else jnp.where(lane // 16 == part, piece, acc)
        out[z] = jnp.where(marked, table, acc)


def place_kernel(got, st, nb, xp):
    def of_all(row):
        return got[pl.ds(row, 16, stride=PACK), :]

    tables = of_all(TABLE_ROW)
    row16 = iota((SLOTS, 16), 0)
    lane16 = iota((SLOTS, 16), 1)
    m16 = row16 // 3
    whose = (m16 % 2) * 8 + m16 // 2
    picks = (lane16 == whose).astype(F32).astype(BF16)
    mine = dot(picks, tables.astype(BF16))
    lane, row = iota((SLOTS, 128), 1), iota((SLOTS, 128), 0)
    t = row % 3
    kept = jnp.sum(jnp.where(lane == 64 + t, mine, 0.0), axis=1, keepdims=True)
    eye = iota((16, 16), 0) == iota((16, 16), 1)
    lane_t = iota((16, 128), 1)
    found = jnp.full((SLOTS, 1), -1.0, F32)
    for j in range(2):
        column = jnp.sum(jnp.where(lane_t == 67 + j, tables, 0.0), axis=1, keepdims=True)
        diagonal = jnp.where(eye, column, 0.0).astype(BF16)
        targets = dot(jnp.ones((SLOTS, 16), BF16), diagonal)
        hit = targets == row16.astype(F32)
        where_from = jnp.where(hit, lane16 + 16 * (HELD + j) + 1, 0)
        found = found + jnp.sum(where_from.astype(F32), axis=1, keepdims=True)
    row1 = iota((SLOTS, 1), 0)
    m1 = row1 // 3
    own = ((m1 % 2) * 8 + m1 // 2 + (row1 % 3) * 16).astype(F32)
    source = jnp.where(kept >= 0.0, own, found)
    occupied = (source >= 0.0).astype(F32)
    ones = jnp.ones((ROWS, SLOTS), BF16)

    def ranks(first, width):
        r, slot = iota((SLOTS, width), 0), iota((SLOTS, width), 1) - first
        earlier = dot(ones, jnp.where(r < slot, occupied, 0.0).astype(BF16))
        full = dot(ones, jnp.where(r == slot, occupied, 0.0).astype(BF16))
        return jnp.where(full > 0.5, earlier, -1.0)

    rank = ranks(0, SLOTS)
    picks = (rank == iota((ROWS, SLOTS), 0).astype(F32)).astype(F32).astype(BF16)
    codes = jnp.zeros((SLOTS, 128), F32)
    for k in range(3):
        codes = jnp.where(t == k, pltpu.roll(mine, (128 - 74 - 18 * k) % 128, 1), codes)
    codes = jnp.where(lane == 18, source, codes)
    codes = jnp.where(lane == 19, own, codes)
    codes = choose(picks, codes)
    source, own = codes[:, 18:19], codes[:, 19:20]

    def one_hot(index, width):
        return (iota((ROWS, width), 1).astype(F32) == index).astype(F32).astype(BF16)

    def stacked(first, step, count):
        return jnp.concatenate([of_all(first + step * s) for s in range(count)], axis=0)

    lines = jnp.concatenate([stacked(p, KIND, 5) for p in range(KIND)], axis=1)
    lines = choose(one_hot(source, 80), lines)
    turned = jnp.concatenate([stacked(75 + k, 5, 2) for k in range(5)], axis=1)
    turned = choose(one_hot(source - 48.0, 32), turned)
    walls = jnp.concatenate([stacked(14, KIND, 3), stacked(85, 1, 3)], axis=1)
    walls = choose(one_hot(own, SLOTS), walls)

    def line(n):
        value = lines[:, 128 * (n % KIND) : 128 * (n % KIND) + 128]
        return pltpu.roll(value, 32 if n < KIND else 96, 1)

    for i in range(19):
        st[i] = line(i)
    st[19] = pltpu.roll(walls[:, 0:128], 96, 1)
    moved = source >= 48.0
    for side in range(2):
        wall = pltpu.roll(walls[:, 128:256], 96 if side else 32, 1) != 1.0
        for k in range(5):
            back = pltpu.roll(turned[:, 128 * k : 128 * k + 128], 96 if side else 32, 1)
            arriving = line(19 + 5 * side + k)
            st[20 + 5 * side + k] = jnp.where(jnp.logical_and(moved, wall), back, arriving)
    lane = iota((ROWS, 128), 1)
    codes = jnp.where(lane < 18, codes, ranks(64, 128))
    nb[...] = codes
    to_right = ((lax.axis_index("wide") + lax.axis_index("core")) % 2) == 0
    for q in range(8):
        acc = jnp.zeros((ROWS, 128), F32)
        for k in range(4):
            if 4 * q + k >= ARRAYS:
                continue
            value = st[4 * q + k]
            half = jnp.where(to_right, pltpu.roll(value, 64, 1), pltpu.roll(value, 96, 1))
            half = pltpu.roll(half, 32 * k, 1) if k else half
            acc = jnp.where(lane // 32 == k, half, acc)
        xp[ROWS * q : ROWS * q + ROWS, :] = acc
    xp[ROWS * 8 : ROWS * 9, :] = codes


def start_kernel(st, nb, xg, fc_out, fluid, nbt, zp, f, fc, arriving):
    w = lax.axis_index("wide")
    lane = iota((ROWS, 128), 1)
    left, right = (w + 1) % 2, w % 2
    for i in range(ARRAYS):
        rows = slice(ROWS * (i // 4), ROWS * (i // 4) + ROWS)
        from_left = xg[left, 0, rows, :]
        from_right = xg[right, 1, rows, :]
        shift = (128 - 32 * (i % 4)) % 128
        from_left = pltpu.roll(from_left, shift, 1) if shift else from_left
        shift = (224 - 32 * (i % 4)) % 128
        from_right = pltpu.roll(from_right, shift, 1) if shift else from_right
        value = jnp.where(lane < 32, from_left, jnp.where(lane < 96, st[i], from_right))
        if i < 19:
            f[i] = value
        elif i == 19:
            fluid[...] = value
        else:
            arriving[i - 20] = value
    last = slice(ROWS * 8, ROWS * 9)
    tables = [xg[left, 0, last, :], nb[...], xg[right, 1, last, :]]
    codes = jnp.where(lane < 36, pltpu.roll(tables[1], 18, 1), pltpu.roll(tables[2], 36, 1))
    codes = jnp.where(lane < 18, tables[0], codes)
    codes = jnp.where(lane < 54, codes, -1.0)
    side = jnp.zeros((ROWS, 128), jnp.int32)
    for j in range(18):
        if VELOCITY[j + 1][0]:
            side = jnp.where(lane % 18 == j, VELOCITY[j + 1][0], side)
    wanted = jnp.where(codes >= 0.0, codes - ((1 + side) * SLOTS).astype(F32), -1.0)
    slab = (lane // 18 + side)[0:8]
    done = jnp.full((ROWS, 128), -1.0, F32)
    for slot in range(SLOTS):
        value = jnp.full((8, 128), -1.0, F32)
        for g in range(3):
            value = jnp.where(slab == g, tables[g][0:8, 64 + slot : 65 + slot], value)
        value = jnp.concatenate([value] * (ROWS // 8), axis=0)
        done = jnp.where(wanted == float(slot), value, done)
    nbt[...] = jnp.where(lane < 54, done, tables[1])
    collide_all(f, fluid, fc)
    stream(fc, lambda k: arriving[k], lambda k: arriving[5 + k], nbt, f)
    collide_all(f, fluid, fc_out)
    planes_to_send(fc_out, zp)


def passing(fc, nbt, segments):
    lane = iota((ROWS, 128), 1)
    column, y = lane // 8, lane % 8
    segment = [column < 4, jnp.logical_and(column >= 4, column < 12), column >= 12]
    row1 = iota((ROWS, 1), 0)
    slots = iota((ROWS, ROWS), 1)
    table = nbt[...].astype(jnp.int32)

    def source_rows(g, d):
        if d == (0, 0, 0):
            return row1
        j = VELOCITY.index(d) - 1
        return table[:, 18 * g + j : 18 * g + j + 1]

    def move(i, x, at_z):
        cx, cy, cz = VELOCITY[i]
        shift = (8 * cx + cy) % 128
        moved = pltpu.roll(x, shift, 1) if shift else x
        at_y = None
        if cy:
            at_y = y == (0 if cy > 0 else 7)
            moved = jnp.where(at_y, pltpu.roll(x, (8 * cx - 7 * cy) % 128, 1), moved)
        at_x = {}
        if cx > 0:
            at_x = {1: column == 4, 2: column == 12}
            edge = column == 0
        elif cx < 0:
            at_x = {0: column == 3, 1: column == 11}
            edge = column == 15
        parts = []
        for bx in (0, 1) if cx else (0,):
            for by in (0, 1) if cy else (0,):
                if not (bx or by or cz):
                    continue
                for g in segments:
                    if bx and g not in at_x:
                        continue
                    d = (-cx * bx, -cy * by, 0)
                    rows = source_rows(g, d)
                    if cz:
                        rows = jnp.where(at_z, source_rows(g, d[:2] + (-cz,)), rows)
                    mask = at_x[g] if bx else segment[g]
                    if by:
                        mask = jnp.logical_and(mask, at_y)
                    parts.append((mask, rows))
        if not parts:
            return moved
        picks = [(rows == slots).astype(F32) for _, rows in parts]
        taken = choose(jnp.concatenate(picks, axis=0).astype(BF16), moved)
        bounced = fc[OPPOSITE[i]]
        out = moved
        for n, (mask, rows) in enumerate(parts):
            value = jnp.where(rows >= 0, taken[ROWS * n : ROWS * n + ROWS], bounced)
            out = jnp.where(mask, value, out)
        if cx:
            out = jnp.where(edge, bounced, out)
        return out

    return move


def stream(fc, from_below, from_above, nbt, f):
    z = lax.axis_index("z")
    move = passing(fc, nbt, (0, 1, 2))
    for i in range(19):
        if i in UP:
            f[i] = move(i, from_below(UP.index(i)), z == 0)
        elif i in DOWN:
            f[i] = move(i, from_above(DOWN.index(i)), z == PLANES - 1)
        else:
            f[i] = move(i, fc[i], None)


def exchanged(zg):
    z = lax.axis_index("z")
    below, above = (z + 1) % 2, z % 2
    return (
        lambda k: zg[below, 0, ROWS * k : ROWS * (k + 1), :],
        lambda k: zg[above, 1, ROWS * k : ROWS * (k + 1), :],
    )


def step_kernel(fc, zg, nbt, fluid, fc_out, zp, f):
    stream(fc, *exchanged(zg), nbt, f)
    collide_all(f, fluid, fc_out)
    planes_to_send(fc_out, zp)


def last_kernel(fc_in, zg, nbt, fluid, out, f, fc):
    stream(fc_in, *exchanged(zg), nbt, f)
    collide_all(f, fluid, fc)
    z = lax.axis_index("z")
    first = lax.axis_index("core") == 0
    lane = iota((ROWS, 128), 1)
    move = passing(fc, nbt, (1,))
    column, y = lane // 8, lane % 8
    bare = [fc[OPPOSITE[i]] for i in range(19)]
    up = [move(i, fc[i], z == PLANES - 1) for i in UP]
    down = [move(i, fc[i], z == 0) for i in DOWN]
    left = [move(i, fc[i], None) for i in FLAT] + up[:4]
    right = up[4:] + down
    right += [jnp.where(z == 0, bare[UP[k]], bare[DOWN[k]]) for k in range(5)]
    edge = jnp.where(column == 5, pltpu.roll(bare[13], 8, 1), pltpu.roll(bare[12], 120, 1))
    edge = jnp.where(column == 4, bare[11], jnp.where(column == 11, bare[14], edge))
    right.append(edge)
    edge = jnp.where(y == 1, pltpu.roll(bare[17], 1, 1), pltpu.roll(bare[16], 127, 1))
    right.append(jnp.where(y == 0, bare[15], jnp.where(y == 7, bare[18], edge)))
    left_rest = [WEIGHTS[i] for i in FLAT + UP[:4]]
    right_rest = [WEIGHTS[i] for i in UP[4:] + DOWN + UP] + [WEIGHTS[18]] * 2
    values = []
    for p in range(13):
        value = pltpu.roll(right[p], 32, 1)
        values.append(jnp.where(lane < 64, pltpu.roll(left[p], 96, 1), value))
    lane, slot = iota((SLOTS, 128), 1), iota((SLOTS, 128), 0)
    rank = jnp.broadcast_to(nbt[0:1, :], (SLOTS, 128))
    rank = jnp.sum(jnp.where(lane == 64 + slot, rank, 0.0), axis=1, keepdims=True)
    picks = rank == iota((SLOTS, ROWS), 1).astype(F32)
    spread = choose(picks.astype(F32).astype(BF16), jnp.concatenate(values, axis=1))
    filled = rank >= 0.0
    out[:, 32:40, :] = jnp.zeros((PLANES, 8, 128), F32)
    for p in range(13):
        rest = jnp.where(lane < 64, left_rest[p], right_rest[p])
        value = jnp.where(filled, spread[:, 128 * p : 128 * p + 128], rest)
        for n in range(PLANES):
            a, b = value[6 * n : 6 * n + 3], value[6 * n + 3 : 6 * n + 6]
            out[n, 3 * p : 3 * p + 3, :] = jnp.where(first, a, b)


def unpack_kernel(got, nbr, out, x):
    lane, row = iota((40, 128), 1), iota((40, 128), 0)
    k, n = iota((128, 128), 0), iota((128, 128), 1)
    picks = (n == (k % 16) * 8 + k // 16).astype(F32).astype(BF16)
    place = iota((HELD, 128), 1)
    here_z, here_y = place // 16, place % 8
    absent = [nbr[:, j : j + 1] < 0 for j in range(18)]
    x[...] = jnp.zeros_like(x)

    def gathered(part):
        acc = None
        for z in range(PLANES):
            shift = (16 * z - 16 * part) % 128
            piece = pltpu.roll(got[z], shift, 1) if shift else got[z]
            acc = piece if acc is None else jnp.where(lane // 16 == z, piece, acc)
        return acc

    for q in range(4):
        a, b = gathered(q), gathered(4 + q)
        a = jnp.where(row >= 27, pltpu.roll(a, 16, 1), a)
        falling = jnp.logical_and(row >= 3, row < 18)
        b = jnp.where(falling, pltpu.roll(b, 112, 1), jnp.where(row < 3, pltpu.roll(b, 16, 1), b))
        at_x, at_y = b[33:36], b[36:39]
        edges = {11: at_x, 14: at_x, 13: pltpu.roll(at_x, 120, 1), 12: pltpu.roll(at_x, 8, 1)}
        edges |= {15: at_y, 18: at_y, 17: pltpu.roll(at_y, 127, 1), 16: pltpu.roll(at_y, 1, 1)}
        here_x = 2 * q + (place % 16) // 8

        def missing(c):
            spots = []
            for size, here, top in zip(c, (here_x, here_y, here_z), (7, 7, 7)):
                spots.append(None if not size else here == (0 if size > 0 else top))
            found = jnp.zeros((HELD, 128), jnp.bool_)
            for flags in range(1, 8):
                across = [(flags >> s) & 1 for s in range(3)]
                if any(g and spot is None for g, spot in zip(across, spots)):
                    continue
                d = tuple(-size * g for size, g in zip(c, across))
                mask = jnp.broadcast_to(absent[VELOCITY.index(d) - 1], (HELD, 128))
                for g, spot in zip(across, spots):
                    if spot is not None:
                        mask = jnp.logical_and(mask, spot if g else jnp.logical_not(spot))
                found = jnp.logical_or(found, mask)
            return found

        for i in range(19):
            if i in UP or i in DOWN:
                k = (UP if i in UP else DOWN).index(i)
                bare = b[18 + 3 * k : 21 + 3 * k]
                if i in edges:
                    bare = jnp.where(here_z == (0 if i in UP else 7), bare, edges[i])
                j = 3 * k
                if i in DOWN:
                    value = b[3 + j : 6 + j]
                else:
                    value = a[27 + j : 30 + j] if k < 4 else b[0:3]
                value = jnp.where(missing(VELOCITY[i]), bare, value)
            else:
                j = 3 * FLAT.index(i)
                value = a[j : j + 3]
            x[64 * q + 3 * i : 64 * q + 3 * i + 3, :] = value
    y = permute_lanes(x[...], picks)
    for q in range(4):
        for i in range(19):
            for t in range(HELD):
                r = 64 * q + 3 * i + t
                out[t, i : i + 1, 128 * q : 128 * q + 128] = y[r : r + 1]


def call(kernel, outs, scratch, *args, smem=0, limit=8 * 1024 * 1024):
    spaces = [pltpu.SMEM] * smem + [pltpu.VMEM] * (len(args) - smem)
    many = isinstance(outs, list)
    shapes = [jax.ShapeDtypeStruct(s, F32) for s in (outs if many else [outs])]
    specs = [pl.BlockSpec(memory_space=pltpu.VMEM) for _ in shapes]
    return pl.pallas_call(
        kernel,
        out_shape=shapes if many else shapes[0],
        in_specs=[pl.BlockSpec(memory_space=s) for s in spaces],
        out_specs=specs if many else specs[0],
        scratch_shapes=[pltpu.VMEM(s, F32) for s in scratch],
        compiler_params=pltpu.CompilerParams(vmem_limit_bytes=limit),
        interpret=INTERPRET,
    )(*args)


def solution(mesh):
    slabs, group = mesh.shape["wide"], mesh.shape["narrow"]
    chips = group // 2
    axes = ("wide", "z", "core")
    fine = Mesh(mesh.devices.reshape(slabs, chips, 2), axes)

    def pairs(count, other, index):
        return [
            [index(a, b, c), index((a + 1) % count, b, c)]
            for c in range(2)
            for a in range(c, count, 2)
            for b in range(other)
        ]

    wide_pairs = pairs(slabs, chips, lambda w, z, c: (w * chips + z) * 2 + c)
    z_pairs = pairs(chips, 1, lambda z, _, c: z * 2 + c)

    def both_sides(x, names, groups):
        y = lax.all_gather(x, names, axis_index_groups=groups)
        return lax.all_gather(y, "core")

    def shards(pops_in, keep_slot, send_slot, send_dest, neighbours, fluid):
        held = (keep_slot, send_slot, send_dest, neighbours, pops_in, fluid)
        if not INTERPRET:
            held = [pltpu.with_memory_space_constraint(x, pltpu.HBM) for x in held]
        packed = call(
            pack_kernel, (chips, PACK, 128), [(PACK, 512), (PACK, 512), (19, 8, 512)],
            *held, smem=4,
        )
        planes = lax.all_to_all(packed, "z", 0, 0, tiled=True)
        got = lax.all_gather(planes, "core").reshape(group * PACK, 128)
        st, nb, xp = call(
            place_kernel, [(ARRAYS, ROWS, 128), (ROWS, 128), (9 * ROWS, 128)], [], got
        )
        xg = both_sides(xp, axes, wide_pairs)
        state = (19, ROWS, 128)
        sent = (5 * ROWS, 128)
        fc, wet, nbt, zp = call(
            start_kernel, [state, (ROWS, 128), (ROWS, 128), sent],
            [state, state, (10, ROWS, 128)], st, nb, xg,
        )
        for step in range(STEPS - 3):
            zg = both_sides(zp, ("z", "core"), z_pairs)
            fc, zp = call(step_kernel, [state, sent], [state], fc, zg, nbt, wet)
        zg = both_sides(zp, ("z", "core"), z_pairs)
        back = call(last_kernel, (chips, 40, 128), [state, state], fc, zg, nbt, wet)
        home = lax.all_to_all(back, "z", 0, 0, tiled=True)
        return call(unpack_kernel, (HELD, 19, 512), [(256, 128)], home, neighbours)

    placed = (P(axes, None, None), P(axes), P(axes), P(axes), P(axes, None), P(axes, None))
    return jax.shard_map(
        shards, mesh=fine, in_specs=placed, out_specs=P(axes, None, None), check_vma=False
    )
```

```python
import jax
import jax.numpy as jnp
from jax import lax
from jax.experimental import pallas as pl
from jax.experimental.pallas import tpu as pltpu
from jax.sharding import Mesh, PartitionSpec as P

STEPS = 4
HELD = 3
SLOTS = 48
ROWS = 32
PACK = 88
KIND = 15
TABLE_ROW = 59
ARRAYS = 30
PLANES = 8
INTERPRET = False

VELOCITY = [
    (0, 0, 0),
    (1, 0, 0), (-1, 0, 0), (0, 1, 0), (0, -1, 0), (0, 0, 1), (0, 0, -1),
    (1, 1, 0), (-1, -1, 0), (1, -1, 0), (-1, 1, 0),
    (1, 0, 1), (-1, 0, -1), (1, 0, -1), (-1, 0, 1),
    (0, 1, 1), (0, -1, -1), (0, 1, -1), (0, -1, 1),
]
WEIGHTS = [1.0 / 3.0] + [1.0 / 18.0] * 6 + [1.0 / 36.0] * 12
OPPOSITE = [0, 2, 1, 4, 3, 6, 5, 8, 7, 10, 9, 12, 11, 14, 13, 16, 15, 18, 17]
UP = [i for i in range(19) if VELOCITY[i][2] == 1]
FLAT = [i for i in range(19) if VELOCITY[i][2] == 0]
DOWN = [i for i in range(19) if VELOCITY[i][2] == -1]
NU_ZERO = 0.1
NU_LIMIT = 0.01
LAMBDA_TIME = 10.0
POWER_INDEX = 0.35
OMEGA_ZERO = 1.0 / (3.0 * NU_ZERO + 0.5)
SHEAR_SCALE = 2.1213203435596424
RATE_SCALE = (LAMBDA_TIME * SHEAR_SCALE * OMEGA_ZERO) ** 2
F32 = jnp.float32
BF16 = jnp.bfloat16


def iota(shape, dim):
    return lax.broadcasted_iota(jnp.int32, shape, dim)


def dot(a, b):
    return jnp.dot(a, b, preferred_element_type=F32)


def split(x):
    high = x.astype(BF16)
    rest = x - high.astype(F32)
    middle = rest.astype(BF16)
    low = (rest - middle.astype(F32)).astype(BF16)
    return high, middle, low


def choose(picks, x):
    n = x.shape[1]
    y = dot(picks, jnp.concatenate(split(x), axis=1))
    return y[:, :n] + y[:, n : 2 * n] + y[:, 2 * n :]


def permute_lanes(x, picks):
    m = x.shape[0]
    y = dot(jnp.concatenate(split(x), axis=0), picks)
    return y[:m] + y[m : 2 * m] + y[2 * m :]


def regroup(arrays):
    arrays = list(arrays)
    group = iota(arrays[0].shape, 1) // 16
    for s in (1, 2, 4):
        high = (group & s) != 0
        for i in range(8):
            if i & s:
                continue
            a, b = arrays[i], arrays[i | s]
            arrays[i] = jnp.where(high, pltpu.roll(b, 16 * s, 1), a)
            arrays[i | s] = jnp.where(high, b, pltpu.roll(a, 128 - 16 * s, 1))
    return arrays


def collide(f, fluid):
    def total(indices):
        out = None
        for i in indices:
            out = f[i] if out is None else out + f[i]
        return out

    rho = total(range(19))
    inverse = 1.0 / rho
    u = []
    for a in range(3):
        plus = total([i for i in range(19) if VELOCITY[i][a] == 1])
        minus = total([i for i in range(19) if VELOCITY[i][a] == -1])
        u.append((plus - minus) * inverse)
    base = 1.0 - 1.5 * (u[0] * u[0] + u[1] * u[1] + u[2] * u[2])
    excess = [f[0] - WEIGHTS[0] * rho * base]
    scaled = {}
    for i in range(1, 19, 2):
        c = VELOCITY[i]
        along = None
        for a in range(3):
            if c[a]:
                term = u[a]
                if along is None:
                    along = term if c[a] > 0 else -term
                else:
                    along = along + term if c[a] > 0 else along - term
        if WEIGHTS[i] not in scaled:
            scaled[WEIGHTS[i]] = WEIGHTS[i] * rho
        even = base + 4.5 * along * along
        odd = 3.0 * along
        excess.append(f[i] - scaled[WEIGHTS[i]] * (even + odd))
        excess.append(f[i + 1] - scaled[WEIGHTS[i]] * (even - odd))
    stress = None
    for a in range(3):
        for b in range(a, 3):
            part = None
            for i in range(1, 19):
                sign = VELOCITY[i][a] * VELOCITY[i][b]
                if sign:
                    if part is None:
                        part = excess[i] if sign > 0 else -excess[i]
                    else:
                        part = part + excess[i] if sign > 0 else part - excess[i]
            square = part * part if a == b else 2.0 * (part * part)
            stress = square if stress is None else stress + square
    grown = 1.0 + RATE_SCALE * stress * inverse * inverse
    thinned = jnp.exp(((POWER_INDEX - 1.0) / 2.0) * jnp.log(grown))
    viscosity = NU_LIMIT + (NU_ZERO - NU_LIMIT) * thinned
    rate = 1.0 / (3.0 * viscosity + 0.5)
    wet = fluid == 1.0
    return [jnp.where(wet, f[i] - rate * excess[i], f[OPPOSITE[i]]) for i in range(19)]


def collide_all(f_ref, fluid_ref, fc_ref):
    for g in range(ROWS // 8):
        rows = slice(8 * g, 8 * g + 8)
        done = collide([f_ref[i, rows, :] for i in range(19)], fluid_ref[rows, :])
        for i in range(19):
            fc_ref[i, rows, :] = done[i]


def planes_to_send(fc_ref, zp_ref):
    z = lax.axis_index("z")
    up = ((z + lax.axis_index("core")) % 2) == 0
    for k in range(5):
        @pl.when(up)
        def _():
            zp_ref[ROWS * k : ROWS * (k + 1), :] = fc_ref[UP[k]]

        @pl.when(jnp.logical_not(up))
        def _():
            zp_ref[ROWS * k : ROWS * (k + 1), :] = fc_ref[DOWN[k]]


def pack_kernel(keep, send, dest, nbr, pops, fluid, out, xa, xb, raw):
    xa[...] = jnp.zeros_like(xa)
    xb[...] = jnp.zeros_like(xb)
    raw[...] = jnp.ones_like(raw)
    for s in range(5):
        slot = jnp.maximum(keep[s] if s < HELD else send[s - HELD], 0)
        for q in range(4):
            block = pops[slot, :, 128 * q : 128 * q + 128]
            r = PACK * q + KIND * s
            xa[r : r + 15, :] = block[0:15]
            xb[r : r + 4, :] = block[15:19]
            raw[pl.ds(152 * q + s, 19, stride=8), :] = block
    walls = jnp.concatenate([fluid[...].astype(F32), jnp.ones((8 - HELD, 512), F32)], axis=0)
    slots = jnp.full((8, 128), -1, jnp.int32)
    for s in range(5):
        slot = keep[s] if s < HELD else send[s - HELD]
        slots = jnp.where(iota((8, 128), 0) == s, slot, slots)
    for q in range(4):
        wall = walls[:, 128 * q : 128 * q + 128]
        r = PACK * q
        xb[pl.ds(r + 14, HELD, stride=KIND), :] = wall[0:HELD]
        xa[r + 85 : r + 88, :] = wall[0:HELD]
        xb[r + 85 : r + 88, :] = wall[0:HELD]
        own = [raw[152 * q + 8 * i : 152 * q + 8 * i + 8, :] for i in range(19)]
        done = collide([jnp.where(slots >= 0, own[i], WEIGHTS[i]) for i in range(19)], wall)
        for k in range(5):
            xa[pl.ds(r + 75 + k, 2, stride=5), :] = own[OPPOSITE[UP[k]]][HELD : HELD + 2]
            xb[pl.ds(r + 75 + k, 2, stride=5), :] = own[OPPOSITE[DOWN[k]]][HELD : HELD + 2]
            xb[pl.ds(r + 4 + k, 5, stride=KIND), :] = done[UP[k]][0:5]
            xb[pl.ds(r + 9 + k, 5, stride=KIND), :] = done[DOWN[k]][0:5]
    k, n = iota((128, 128), 0), iota((128, 128), 1)
    picks = (n == (k % 8) * 16 + k // 8).astype(F32).astype(BF16)
    y = permute_lanes(jnp.concatenate([xa[...], xb[...]], axis=0), picks)
    lane, row = iota((PACK, 128), 1), iota((PACK, 128), 0)
    kind, late = row % KIND, row >= 75
    rising = jnp.logical_and(jnp.logical_and(kind >= 4, kind < 9), jnp.logical_not(late))
    falling = jnp.logical_or(jnp.logical_and(kind >= 9, kind < 14), late)
    second = lane >= 64
    rising = jnp.logical_or(
        jnp.logical_and(second, rising), jnp.logical_and(late, jnp.logical_not(second))
    )
    falling = jnp.logical_and(second, falling)
    parts = regroup([y[PACK * part : PACK * part + PACK] for part in range(8)])
    values = [keep[t] for t in range(3)] + [dest[j] for j in range(2)]
    values = list(enumerate(values)) + [
        (10 + 18 * t + j, nbr[t, j]) for t in range(3) for j in range(18)
    ]
    line = iota((8, 128), 1)
    table = jnp.zeros((8, 128), jnp.int32)
    for place, value in values:
        table = jnp.where(line == 64 + place, value, table)
    table = jnp.concatenate([table.astype(F32)] * (PACK // 8), axis=0)
    marked = jnp.logical_and(row == TABLE_ROW, lane >= 64)
    for z in range(PLANES):
        value = jnp.where(falling, parts[(z + 1) % PLANES], parts[z])
        value = jnp.where(rising, parts[(z - 1) % PLANES], value)
        out[z] = jnp.where(marked, table, value)


def place_kernel(got, st, nb, xp):
    def of_all(row):
        return got[pl.ds(row, 16, stride=PACK), :]

    tables = of_all(TABLE_ROW)
    row16 = iota((SLOTS, 16), 0)
    lane16 = iota((SLOTS, 16), 1)
    m16 = row16 // 3
    whose = (m16 % 2) * 8 + m16 // 2
    picks = (lane16 == whose).astype(F32).astype(BF16)
    mine = dot(picks, tables.astype(BF16))
    lane, row = iota((SLOTS, 128), 1), iota((SLOTS, 128), 0)
    t = row % 3
    kept = jnp.sum(jnp.where(lane == 64 + t, mine, 0.0), axis=1, keepdims=True)
    eye = iota((16, 16), 0) == iota((16, 16), 1)
    lane_t = iota((16, 128), 1)
    found = jnp.full((SLOTS, 1), -1.0, F32)
    for j in range(2):
        column = jnp.sum(jnp.where(lane_t == 67 + j, tables, 0.0), axis=1, keepdims=True)
        diagonal = jnp.where(eye, column, 0.0).astype(BF16)
        targets = dot(jnp.ones((SLOTS, 16), BF16), diagonal)
        hit = targets == row16.astype(F32)
        where_from = jnp.where(hit, lane16 + 16 * (HELD + j) + 1, 0)
        found = found + jnp.sum(where_from.astype(F32), axis=1, keepdims=True)
    row1 = iota((SLOTS, 1), 0)
    m1 = row1 // 3
    own = ((m1 % 2) * 8 + m1 // 2 + (row1 % 3) * 16).astype(F32)
    source = jnp.where(kept >= 0.0, own, found)
    occupied = (source >= 0.0).astype(F32)
    ones = jnp.ones((ROWS, SLOTS), BF16)

    def ranks(first, width):
        r, slot = iota((SLOTS, width), 0), iota((SLOTS, width), 1) - first
        earlier = dot(ones, jnp.where(r < slot, occupied, 0.0).astype(BF16))
        full = dot(ones, jnp.where(r == slot, occupied, 0.0).astype(BF16))
        return jnp.where(full > 0.5, earlier, -1.0)

    rank = ranks(0, SLOTS)
    picks = (rank == iota((ROWS, SLOTS), 0).astype(F32)).astype(F32).astype(BF16)
    codes = jnp.zeros((SLOTS, 128), F32)
    for k in range(3):
        codes = jnp.where(t == k, pltpu.roll(mine, (128 - 74 - 18 * k) % 128, 1), codes)
    codes = jnp.where(lane == 18, source, codes)
    codes = jnp.where(lane == 19, own, codes)
    codes = choose(picks, codes)
    source, own = codes[:, 18:19], codes[:, 19:20]

    def one_hot(index, width):
        return (iota((ROWS, width), 1).astype(F32) == index).astype(F32).astype(BF16)

    def stacked(first, step, count):
        return jnp.concatenate([of_all(first + step * s) for s in range(count)], axis=0)

    lines = jnp.concatenate([stacked(p, KIND, 5) for p in range(KIND)], axis=1)
    lines = choose(one_hot(source, 80), lines)
    turned = jnp.concatenate([stacked(75 + k, 5, 2) for k in range(5)], axis=1)
    turned = choose(one_hot(source - 48.0, 32), turned)
    walls = jnp.concatenate([stacked(14, KIND, 3), stacked(85, 1, 3)], axis=1)
    walls = choose(one_hot(own, SLOTS), walls)

    def line(n):
        value = lines[:, 128 * (n % KIND) : 128 * (n % KIND) + 128]
        return pltpu.roll(value, 32 if n < KIND else 96, 1)

    for i in range(19):
        st[i] = line(i)
    st[19] = pltpu.roll(walls[:, 0:128], 96, 1)
    moved = source >= 48.0
    for side in range(2):
        wall = pltpu.roll(walls[:, 128:256], 96 if side else 32, 1) != 1.0
        for k in range(5):
            back = pltpu.roll(turned[:, 128 * k : 128 * k + 128], 96 if side else 32, 1)
            arriving = line(19 + 5 * side + k)
            st[20 + 5 * side + k] = jnp.where(jnp.logical_and(moved, wall), back, arriving)
    lane = iota((ROWS, 128), 1)
    codes = jnp.where(lane < 18, codes, ranks(64, 128))
    nb[...] = codes
    to_right = ((lax.axis_index("wide") + lax.axis_index("core")) % 2) == 0
    for q in range(8):
        acc = jnp.zeros((ROWS, 128), F32)
        for k in range(4):
            if 4 * q + k >= ARRAYS:
                continue
            value = st[4 * q + k]
            half = jnp.where(to_right, pltpu.roll(value, 64, 1), pltpu.roll(value, 96, 1))
            half = pltpu.roll(half, 32 * k, 1) if k else half
            acc = jnp.where(lane // 32 == k, half, acc)
        xp[ROWS * q : ROWS * q + ROWS, :] = acc
    xp[ROWS * 8 : ROWS * 9, :] = codes


def start_kernel(st, nb, xg, fc_out, fluid, nbt, zp, f, fc, arriving):
    w = lax.axis_index("wide")
    lane = iota((ROWS, 128), 1)
    left, right = (w + 1) % 2, w % 2
    for i in range(ARRAYS):
        rows = slice(ROWS * (i // 4), ROWS * (i // 4) + ROWS)
        from_left = xg[left, 0, rows, :]
        from_right = xg[right, 1, rows, :]
        shift = (128 - 32 * (i % 4)) % 128
        from_left = pltpu.roll(from_left, shift, 1) if shift else from_left
        shift = (224 - 32 * (i % 4)) % 128
        from_right = pltpu.roll(from_right, shift, 1) if shift else from_right
        value = jnp.where(lane < 32, from_left, jnp.where(lane < 96, st[i], from_right))
        if i < 19:
            f[i] = value
        elif i == 19:
            fluid[...] = value
        else:
            arriving[i - 20] = value
    last = slice(ROWS * 8, ROWS * 9)
    tables = [xg[left, 0, last, :], nb[...], xg[right, 1, last, :]]
    codes = jnp.where(lane < 36, pltpu.roll(tables[1], 18, 1), pltpu.roll(tables[2], 36, 1))
    codes = jnp.where(lane < 18, tables[0], codes)
    codes = jnp.where(lane < 54, codes, -1.0)
    side = jnp.zeros((ROWS, 128), jnp.int32)
    for j in range(18):
        if VELOCITY[j + 1][0]:
            side = jnp.where(lane % 18 == j, VELOCITY[j + 1][0], side)
    wanted = jnp.where(codes >= 0.0, codes - ((1 + side) * SLOTS).astype(F32), -1.0)
    slab = (lane // 18 + side)[0:8]
    done = jnp.full((ROWS, 128), -1.0, F32)
    for slot in range(SLOTS):
        value = jnp.full((8, 128), -1.0, F32)
        for g in range(3):
            value = jnp.where(slab == g, tables[g][0:8, 64 + slot : 65 + slot], value)
        value = jnp.concatenate([value] * (ROWS // 8), axis=0)
        done = jnp.where(wanted == float(slot), value, done)
    nbt[...] = jnp.where(lane < 54, done, tables[1])
    collide_all(f, fluid, fc)
    stream(fc, lambda k: arriving[k], lambda k: arriving[5 + k], nbt, f)
    collide_all(f, fluid, fc_out)
    planes_to_send(fc_out, zp)


def passing(fc, nbt, segments):
    lane = iota((ROWS, 128), 1)
    column, y = lane // 8, lane % 8
    segment = [column < 4, jnp.logical_and(column >= 4, column < 12), column >= 12]
    slots = iota((ROWS, ROWS), 1)
    table = nbt[...].astype(jnp.int32)
    known = {}

    def source_rows(g, d):
        if d == (0, 0, 0):
            return iota((ROWS, 128), 0)
        j = 18 * g + VELOCITY.index(d) - 1
        if j not in known:
            known[j] = jnp.broadcast_to(table[:, j : j + 1], (ROWS, 128))
        return known[j]

    def move(i, x, at_z):
        cx, cy, cz = VELOCITY[i]
        shift = (8 * cx + cy) % 128
        moved = pltpu.roll(x, shift, 1) if shift else x
        at_y = None
        if cy:
            at_y = y == (0 if cy > 0 else 7)
            moved = jnp.where(at_y, pltpu.roll(x, (8 * cx - 7 * cy) % 128, 1), moved)
        at_x = {}
        if cx > 0:
            at_x = {1: column == 4, 2: column == 12}
            edge = column == 0
        elif cx < 0:
            at_x = {0: column == 3, 1: column == 11}
            edge = column == 15
        parts = []
        for bx in (0, 1) if cx else (0,):
            for by in (0, 1) if cy else (0,):
                if not (bx or by or cz):
                    continue
                for g in segments:
                    if bx and g not in at_x:
                        continue
                    d = (-cx * bx, -cy * by, 0)
                    rows = source_rows(g, d)
                    if cz:
                        rows = jnp.where(at_z, source_rows(g, d[:2] + (-cz,)), rows)
                    mask = at_x[g] if bx else segment[g]
                    if by:
                        mask = jnp.logical_and(mask, at_y)
                    parts.append((mask, rows))
        if not parts:
            return moved
        picks = [(rows[:, :ROWS] == slots).astype(F32) for _, rows in parts]
        taken = choose(jnp.concatenate(picks, axis=0).astype(BF16), moved)
        bounced = fc[OPPOSITE[i]]
        out = moved
        for n, (mask, rows) in enumerate(parts):
            value = jnp.where(rows >= 0, taken[ROWS * n : ROWS * n + ROWS], bounced)
            out = jnp.where(mask, value, out)
        if cx:
            out = jnp.where(edge, bounced, out)
        return out

    return move


def stream(fc, from_below, from_above, nbt, f):
    z = lax.axis_index("z")
    move = passing(fc, nbt, (0, 1, 2))
    for i in range(19):
        if i in UP:
            f[i] = move(i, from_below(UP.index(i)), z == 0)
        elif i in DOWN:
            f[i] = move(i, from_above(DOWN.index(i)), z == PLANES - 1)
        else:
            f[i] = move(i, fc[i], None)


def exchanged(zg):
    z = lax.axis_index("z")
    below, above = (z + 1) % 2, z % 2
    return (
        lambda k: zg[below, 0, ROWS * k : ROWS * (k + 1), :],
        lambda k: zg[above, 1, ROWS * k : ROWS * (k + 1), :],
    )


def step_kernel(fc, zg, nbt, fluid, fc_out, zp, f):
    stream(fc, *exchanged(zg), nbt, f)
    collide_all(f, fluid, fc_out)
    planes_to_send(fc_out, zp)


def last_kernel(fc_in, zg, nbt, fluid, out, f, fc):
    stream(fc_in, *exchanged(zg), nbt, f)
    collide_all(f, fluid, fc)
    z = lax.axis_index("z")
    first = lax.axis_index("core") == 0
    lane = iota((ROWS, 128), 1)
    move = passing(fc, nbt, (1,))
    column, y = lane // 8, lane % 8
    bare = [fc[OPPOSITE[i]] for i in range(19)]
    up = [move(i, fc[i], z == PLANES - 1) for i in UP]
    down = [move(i, fc[i], z == 0) for i in DOWN]
    left = [move(i, fc[i], None) for i in FLAT] + up[:4]
    right = up[4:] + down
    right += [jnp.where(z == 0, bare[UP[k]], bare[DOWN[k]]) for k in range(5)]
    edge = jnp.where(column == 5, pltpu.roll(bare[13], 8, 1), pltpu.roll(bare[12], 120, 1))
    edge = jnp.where(column == 4, bare[11], jnp.where(column == 11, bare[14], edge))
    right.append(edge)
    edge = jnp.where(y == 1, pltpu.roll(bare[17], 1, 1), pltpu.roll(bare[16], 127, 1))
    right.append(jnp.where(y == 0, bare[15], jnp.where(y == 7, bare[18], edge)))
    left_rest = [WEIGHTS[i] for i in FLAT + UP[:4]]
    right_rest = [WEIGHTS[i] for i in UP[4:] + DOWN + UP] + [WEIGHTS[18]] * 2
    values = []
    for p in range(13):
        value = pltpu.roll(right[p], 32, 1)
        values.append(jnp.where(lane < 64, pltpu.roll(left[p], 96, 1), value))
    lane, slot = iota((SLOTS, 128), 1), iota((SLOTS, 128), 0)
    rank = jnp.broadcast_to(nbt[0:1, :], (SLOTS, 128))
    rank = jnp.sum(jnp.where(lane == 64 + slot, rank, 0.0), axis=1, keepdims=True)
    picks = rank == iota((SLOTS, ROWS), 1).astype(F32)
    spread = choose(picks.astype(F32).astype(BF16), jnp.concatenate(values, axis=1))
    filled = rank >= 0.0
    out[:, 32:40, :] = jnp.zeros((PLANES, 8, 128), F32)
    for p in range(13):
        rest = jnp.where(lane < 64, left_rest[p], right_rest[p])
        value = jnp.where(filled, spread[:, 128 * p : 128 * p + 128], rest)
        for n in range(PLANES):
            a, b = value[6 * n : 6 * n + 3], value[6 * n + 3 : 6 * n + 6]
            out[n, 3 * p : 3 * p + 3, :] = jnp.where(first, a, b)


def unpack_kernel(got, nbr, out, x, y):
    lane, row = iota((40, 128), 1), iota((40, 128), 0)
    k, n = iota((128, 128), 0), iota((128, 128), 1)
    picks = (n == (k % 16) * 8 + k // 16).astype(F32).astype(BF16)
    place = iota((HELD, 128), 1)
    here_z, here_y = place // 16, place % 8
    absent = [nbr[:, j : j + 1] < 0 for j in range(18)]
    x[...] = jnp.zeros_like(x)

    tiles = regroup([got[z] for z in range(PLANES)])
    for q in range(4):
        a, b = tiles[q], tiles[4 + q]
        a = jnp.where(row >= 27, pltpu.roll(a, 16, 1), a)
        falling = jnp.logical_and(row >= 3, row < 18)
        b = jnp.where(falling, pltpu.roll(b, 112, 1), jnp.where(row < 3, pltpu.roll(b, 16, 1), b))
        at_x, at_y = b[33:36], b[36:39]
        edges = {11: at_x, 14: at_x, 13: pltpu.roll(at_x, 120, 1), 12: pltpu.roll(at_x, 8, 1)}
        edges |= {15: at_y, 18: at_y, 17: pltpu.roll(at_y, 127, 1), 16: pltpu.roll(at_y, 1, 1)}
        here_x = 2 * q + (place % 16) // 8

        def missing(c):
            spots = []
            for size, here, top in zip(c, (here_x, here_y, here_z), (7, 7, 7)):
                spots.append(None if not size else here == (0 if size > 0 else top))
            found = jnp.zeros((HELD, 128), jnp.bool_)
            for flags in range(1, 8):
                across = [(flags >> s) & 1 for s in range(3)]
                if any(g and spot is None for g, spot in zip(across, spots)):
                    continue
                d = tuple(-size * g for size, g in zip(c, across))
                mask = jnp.broadcast_to(absent[VELOCITY.index(d) - 1], (HELD, 128))
                for g, spot in zip(across, spots):
                    if spot is not None:
                        mask = jnp.logical_and(mask, spot if g else jnp.logical_not(spot))
                found = jnp.logical_or(found, mask)
            return found

        for i in range(19):
            if i in UP or i in DOWN:
                k = (UP if i in UP else DOWN).index(i)
                bare = b[18 + 3 * k : 21 + 3 * k]
                if i in edges:
                    bare = jnp.where(here_z == (0 if i in UP else 7), bare, edges[i])
                j = 3 * k
                if i in DOWN:
                    value = b[3 + j : 6 + j]
                else:
                    value = a[27 + j : 30 + j] if k < 4 else b[0:3]
                value = jnp.where(missing(VELOCITY[i]), bare, value)
            else:
                j = 3 * FLAT.index(i)
                value = a[j : j + 3]
            x[64 * q + 3 * i : 64 * q + 3 * i + 3, :] = value
    y[...] = permute_lanes(x[...], picks)
    for q in range(4):
        for t in range(HELD):
            out[t, :, 128 * q : 128 * q + 128] = y[pl.ds(64 * q + t, 19, stride=3), :]


def call(kernel, outs, scratch, *args, smem=0, limit=8 * 1024 * 1024):
    spaces = [pltpu.SMEM] * smem + [pltpu.VMEM] * (len(args) - smem)
    many = isinstance(outs, list)
    shapes = [jax.ShapeDtypeStruct(s, F32) for s in (outs if many else [outs])]
    specs = [pl.BlockSpec(memory_space=pltpu.VMEM) for _ in shapes]
    return pl.pallas_call(
        kernel,
        out_shape=shapes if many else shapes[0],
        in_specs=[pl.BlockSpec(memory_space=s) for s in spaces],
        out_specs=specs if many else specs[0],
        scratch_shapes=[pltpu.VMEM(s, F32) for s in scratch],
        compiler_params=pltpu.CompilerParams(vmem_limit_bytes=limit),
        interpret=INTERPRET,
    )(*args)


def solution(mesh):
    slabs, group = mesh.shape["wide"], mesh.shape["narrow"]
    chips = group // 2
    axes = ("wide", "z", "core")
    fine = Mesh(mesh.devices.reshape(slabs, chips, 2), axes)

    def pairs(count, other, index):
        return [
            [index(a, b, c), index((a + 1) % count, b, c)]
            for c in range(2)
            for a in range(c, count, 2)
            for b in range(other)
        ]

    wide_pairs = pairs(slabs, chips, lambda w, z, c: (w * chips + z) * 2 + c)
    z_pairs = pairs(chips, 1, lambda z, _, c: z * 2 + c)

    def both_sides(x, names, groups):
        y = lax.all_gather(x, names, axis_index_groups=groups)
        return lax.all_gather(y, "core")

    def shards(pops_in, keep_slot, send_slot, send_dest, neighbours, fluid):
        held = (keep_slot, send_slot, send_dest, neighbours, pops_in, fluid)
        if not INTERPRET:
            held = [pltpu.with_memory_space_constraint(x, pltpu.HBM) for x in held]
        packed = call(
            pack_kernel, (chips, PACK, 128), [(4 * PACK, 128), (4 * PACK, 128), (4 * 152, 128)],
            *held, smem=4,
        )
        planes = lax.all_to_all(packed, "z", 0, 0, tiled=True)
        got = lax.all_gather(planes, "core").reshape(group * PACK, 128)
        st, nb, xp = call(
            place_kernel, [(ARRAYS, ROWS, 128), (ROWS, 128), (9 * ROWS, 128)], [], got
        )
        xg = both_sides(xp, axes, wide_pairs)
        state = (19, ROWS, 128)
        sent = (5 * ROWS, 128)
        fc, wet, nbt, zp = call(
            start_kernel, [state, (ROWS, 128), (ROWS, 128), sent],
            [state, state, (10, ROWS, 128)], st, nb, xg,
        )
        for step in range(STEPS - 3):
            zg = both_sides(zp, ("z", "core"), z_pairs)
            fc, zp = call(step_kernel, [state, sent], [state], fc, zg, nbt, wet)
        zg = both_sides(zp, ("z", "core"), z_pairs)
        back = call(last_kernel, (chips, 40, 128), [state, state], fc, zg, nbt, wet)
        home = lax.all_to_all(back, "z", 0, 0, tiled=True)
        return call(unpack_kernel, (HELD, 19, 512), [(256, 128)] * 2, home, neighbours)

    placed = (P(axes, None, None), P(axes), P(axes), P(axes), P(axes, None), P(axes, None))
    return jax.shard_map(
        shards, mesh=fine, in_specs=placed, out_specs=P(axes, None, None), check_vma=False
    )
```

```python
import jax
import jax.numpy as jnp
from jax import lax
from jax.experimental import pallas as pl
from jax.experimental.pallas import tpu as pltpu
from jax.sharding import Mesh, PartitionSpec as P

STEPS = 4
HELD = 3
SLOTS = 48
ROWS = 32
PACK = 88
KIND = 15
TABLE_ROW = 59
ARRAYS = 30
PLANES = 8
INTERPRET = False

VELOCITY = [
    (0, 0, 0),
    (1, 0, 0), (-1, 0, 0), (0, 1, 0), (0, -1, 0), (0, 0, 1), (0, 0, -1),
    (1, 1, 0), (-1, -1, 0), (1, -1, 0), (-1, 1, 0),
    (1, 0, 1), (-1, 0, -1), (1, 0, -1), (-1, 0, 1),
    (0, 1, 1), (0, -1, -1), (0, 1, -1), (0, -1, 1),
]
WEIGHTS = [1.0 / 3.0] + [1.0 / 18.0] * 6 + [1.0 / 36.0] * 12
OPPOSITE = [0, 2, 1, 4, 3, 6, 5, 8, 7, 10, 9, 12, 11, 14, 13, 16, 15, 18, 17]
UP = [i for i in range(19) if VELOCITY[i][2] == 1]
FLAT = [i for i in range(19) if VELOCITY[i][2] == 0]
DOWN = [i for i in range(19) if VELOCITY[i][2] == -1]
NU_ZERO = 0.1
NU_LIMIT = 0.01
LAMBDA_TIME = 10.0
POWER_INDEX = 0.35
OMEGA_ZERO = 1.0 / (3.0 * NU_ZERO + 0.5)
SHEAR_SCALE = 2.1213203435596424
RATE_SCALE = (LAMBDA_TIME * SHEAR_SCALE * OMEGA_ZERO) ** 2
F32 = jnp.float32
BF16 = jnp.bfloat16


def iota(shape, dim):
    return lax.broadcasted_iota(jnp.int32, shape, dim)


def dot(a, b):
    return jnp.dot(a, b, preferred_element_type=F32)


def split(x):
    high = x.astype(BF16)
    rest = x - high.astype(F32)
    middle = rest.astype(BF16)
    low = (rest - middle.astype(F32)).astype(BF16)
    return high, middle, low


def choose(picks, x):
    n = x.shape[1]
    y = dot(picks, jnp.concatenate(split(x), axis=1))
    return y[:, :n] + y[:, n : 2 * n] + y[:, 2 * n :]


def permute_lanes(x, picks):
    m = x.shape[0]
    y = dot(jnp.concatenate(split(x), axis=0), picks)
    return y[:m] + y[m : 2 * m] + y[2 * m :]


def regroup(arrays):
    arrays = list(arrays)
    group = iota(arrays[0].shape, 1) // 16
    for s in (1, 2, 4):
        high = (group & s) != 0
        for i in range(8):
            if i & s:
                continue
            a, b = arrays[i], arrays[i | s]
            arrays[i] = jnp.where(high, pltpu.roll(b, 16 * s, 1), a)
            arrays[i | s] = jnp.where(high, b, pltpu.roll(a, 128 - 16 * s, 1))
    return arrays


def collide(f, fluid):
    def total(indices):
        out = None
        for i in indices:
            out = f[i] if out is None else out + f[i]
        return out

    rho = total(range(19))
    inverse = 1.0 / rho
    u = []
    for a in range(3):
        plus = total([i for i in range(19) if VELOCITY[i][a] == 1])
        minus = total([i for i in range(19) if VELOCITY[i][a] == -1])
        u.append((plus - minus) * inverse)
    base = 1.0 - 1.5 * (u[0] * u[0] + u[1] * u[1] + u[2] * u[2])
    excess = [f[0] - WEIGHTS[0] * rho * base]
    scaled = {}
    for i in range(1, 19, 2):
        c = VELOCITY[i]
        along = None
        for a in range(3):
            if c[a]:
                term = u[a]
                if along is None:
                    along = term if c[a] > 0 else -term
                else:
                    along = along + term if c[a] > 0 else along - term
        if WEIGHTS[i] not in scaled:
            scaled[WEIGHTS[i]] = WEIGHTS[i] * rho
        even = base + 4.5 * along * along
        odd = 3.0 * along
        excess.append(f[i] - scaled[WEIGHTS[i]] * (even + odd))
        excess.append(f[i + 1] - scaled[WEIGHTS[i]] * (even - odd))
    stress = None
    for a in range(3):
        for b in range(a, 3):
            part = None
            for i in range(1, 19):
                sign = VELOCITY[i][a] * VELOCITY[i][b]
                if sign:
                    if part is None:
                        part = excess[i] if sign > 0 else -excess[i]
                    else:
                        part = part + excess[i] if sign > 0 else part - excess[i]
            square = part * part if a == b else 2.0 * (part * part)
            stress = square if stress is None else stress + square
    grown = 1.0 + RATE_SCALE * stress * inverse * inverse
    thinned = jnp.exp(((POWER_INDEX - 1.0) / 2.0) * jnp.log(grown))
    viscosity = NU_LIMIT + (NU_ZERO - NU_LIMIT) * thinned
    rate = 1.0 / (3.0 * viscosity + 0.5)
    wet = fluid == 1.0
    return [jnp.where(wet, f[i] - rate * excess[i], f[OPPOSITE[i]]) for i in range(19)]


def collide_all(f_ref, fluid_ref, fc_ref):
    for g in range(ROWS // 8):
        rows = slice(8 * g, 8 * g + 8)
        done = collide([f_ref[i, rows, :] for i in range(19)], fluid_ref[rows, :])
        for i in range(19):
            fc_ref[i, rows, :] = done[i]


def planes_to_send(fc_ref, zp_ref):
    z = lax.axis_index("z")
    up = ((z + lax.axis_index("core")) % 2) == 0
    for k in range(5):
        @pl.when(up)
        def _():
            zp_ref[ROWS * k : ROWS * (k + 1), :] = fc_ref[UP[k]]

        @pl.when(jnp.logical_not(up))
        def _():
            zp_ref[ROWS * k : ROWS * (k + 1), :] = fc_ref[DOWN[k]]


def pack_kernel(keep, send, dest, nbr, pops, fluid, out, xa, xb, raw):
    xa[...] = jnp.zeros_like(xa)
    xb[...] = jnp.zeros_like(xb)
    raw[...] = jnp.ones_like(raw)
    for s in range(5):
        slot = jnp.maximum(keep[s] if s < HELD else send[s - HELD], 0)
        for q in range(4):
            block = pops[slot, :, 128 * q : 128 * q + 128]
            r = PACK * q + KIND * s
            xa[r : r + 15, :] = block[0:15]
            xb[r : r + 4, :] = block[15:19]
            raw[pl.ds(152 * q + s, 19, stride=8), :] = block
    walls = jnp.concatenate([fluid[...].astype(F32), jnp.ones((8 - HELD, 512), F32)], axis=0)
    slots = jnp.full((8, 128), -1, jnp.int32)
    for s in range(5):
        slot = keep[s] if s < HELD else send[s - HELD]
        slots = jnp.where(iota((8, 128), 0) == s, slot, slots)
    for q in range(4):
        wall = walls[:, 128 * q : 128 * q + 128]
        r = PACK * q
        xb[pl.ds(r + 14, HELD, stride=KIND), :] = wall[0:HELD]
        xa[r + 85 : r + 88, :] = wall[0:HELD]
        xb[r + 85 : r + 88, :] = wall[0:HELD]
        own = [raw[152 * q + 8 * i : 152 * q + 8 * i + 8, :] for i in range(19)]
        done = collide([jnp.where(slots >= 0, own[i], WEIGHTS[i]) for i in range(19)], wall)
        for k in range(5):
            xa[pl.ds(r + 75 + k, 2, stride=5), :] = own[OPPOSITE[UP[k]]][HELD : HELD + 2]
            xb[pl.ds(r + 75 + k, 2, stride=5), :] = own[OPPOSITE[DOWN[k]]][HELD : HELD + 2]
            xb[pl.ds(r + 4 + k, 5, stride=KIND), :] = done[UP[k]][0:5]
            xb[pl.ds(r + 9 + k, 5, stride=KIND), :] = done[DOWN[k]][0:5]
    k, n = iota((128, 128), 0), iota((128, 128), 1)
    picks = (n == (k % 8) * 16 + k // 8).astype(F32).astype(BF16)
    y = permute_lanes(jnp.concatenate([xa[0 : 4 * PACK, :], xb[0 : 4 * PACK, :]], axis=0), picks)
    lane, row = iota((PACK, 128), 1), iota((PACK, 128), 0)
    kind, late = row % KIND, row >= 75
    rising = jnp.logical_and(jnp.logical_and(kind >= 4, kind < 9), jnp.logical_not(late))
    falling = jnp.logical_or(jnp.logical_and(kind >= 9, kind < 14), late)
    second = lane >= 64
    rising = jnp.logical_or(
        jnp.logical_and(second, rising), jnp.logical_and(late, jnp.logical_not(second))
    )
    falling = jnp.logical_and(second, falling)
    parts = regroup([y[PACK * part : PACK * part + PACK] for part in range(8)])
    values = [keep[t] for t in range(3)] + [dest[j] for j in range(2)]
    values = list(enumerate(values)) + [
        (10 + 18 * t + j, nbr[t, j]) for t in range(3) for j in range(18)
    ]
    line = iota((8, 128), 1)
    table = jnp.zeros((8, 128), jnp.int32)
    for place, value in values:
        table = jnp.where(line == 64 + place, value, table)
    table = jnp.concatenate([table.astype(F32)] * (PACK // 8), axis=0)
    marked = jnp.logical_and(row == TABLE_ROW, lane >= 64)
    for z in range(PLANES):
        value = jnp.where(falling, parts[(z + 1) % PLANES], parts[z])
        value = jnp.where(rising, parts[(z - 1) % PLANES], value)
        out[z] = jnp.where(marked, table, value)


def place_kernel(got, st, nb, xp):
    def of_all(row):
        return got[pl.ds(row, 16, stride=PACK), :]

    tables = of_all(TABLE_ROW)
    row16 = iota((SLOTS, 16), 0)
    lane16 = iota((SLOTS, 16), 1)
    m16 = row16 // 3
    whose = (m16 % 2) * 8 + m16 // 2
    picks = (lane16 == whose).astype(F32).astype(BF16)
    mine = dot(picks, tables.astype(BF16))
    lane, row = iota((SLOTS, 128), 1), iota((SLOTS, 128), 0)
    t = row % 3
    kept = jnp.sum(jnp.where(lane == 64 + t, mine, 0.0), axis=1, keepdims=True)
    eye = iota((16, 16), 0) == iota((16, 16), 1)
    lane_t = iota((16, 128), 1)
    found = jnp.full((SLOTS, 1), -1.0, F32)
    for j in range(2):
        column = jnp.sum(jnp.where(lane_t == 67 + j, tables, 0.0), axis=1, keepdims=True)
        diagonal = jnp.where(eye, column, 0.0).astype(BF16)
        targets = dot(jnp.ones((SLOTS, 16), BF16), diagonal)
        hit = targets == row16.astype(F32)
        where_from = jnp.where(hit, lane16 + 16 * (HELD + j) + 1, 0)
        found = found + jnp.sum(where_from.astype(F32), axis=1, keepdims=True)
    row1 = iota((SLOTS, 1), 0)
    m1 = row1 // 3
    own = ((m1 % 2) * 8 + m1 // 2 + (row1 % 3) * 16).astype(F32)
    source = jnp.where(kept >= 0.0, own, found)
    occupied = (source >= 0.0).astype(F32)
    ones = jnp.ones((ROWS, SLOTS), BF16)

    def ranks(first, width):
        r, slot = iota((SLOTS, width), 0), iota((SLOTS, width), 1) - first
        earlier = dot(ones, jnp.where(r < slot, occupied, 0.0).astype(BF16))
        full = dot(ones, jnp.where(r == slot, occupied, 0.0).astype(BF16))
        return jnp.where(full > 0.5, earlier, -1.0)

    rank = ranks(0, SLOTS)
    picks = (rank == iota((ROWS, SLOTS), 0).astype(F32)).astype(F32).astype(BF16)
    codes = jnp.zeros((SLOTS, 128), F32)
    for k in range(3):
        codes = jnp.where(t == k, pltpu.roll(mine, (128 - 74 - 18 * k) % 128, 1), codes)
    codes = jnp.where(lane == 18, source, codes)
    codes = jnp.where(lane == 19, own, codes)
    codes = choose(picks, codes)
    source, own = codes[:, 18:19], codes[:, 19:20]

    def one_hot(index, width):
        return (iota((ROWS, width), 1).astype(F32) == index).astype(F32).astype(BF16)

    def stacked(first, step, count):
        return jnp.concatenate([of_all(first + step * s) for s in range(count)], axis=0)

    lines = jnp.concatenate([stacked(p, KIND, 5) for p in range(KIND)], axis=1)
    lines = choose(one_hot(source, 80), lines)
    turned = jnp.concatenate([stacked(75 + k, 5, 2) for k in range(5)], axis=1)
    turned = choose(one_hot(source - 48.0, 32), turned)
    walls = jnp.concatenate([stacked(14, KIND, 3), stacked(85, 1, 3)], axis=1)
    walls = choose(one_hot(own, SLOTS), walls)

    def line(n):
        value = lines[:, 128 * (n % KIND) : 128 * (n % KIND) + 128]
        return pltpu.roll(value, 32 if n < KIND else 96, 1)

    for i in range(19):
        st[i] = line(i)
    st[19] = pltpu.roll(walls[:, 0:128], 96, 1)
    moved = source >= 48.0
    for side in range(2):
        wall = pltpu.roll(walls[:, 128:256], 96 if side else 32, 1) != 1.0
        for k in range(5):
            back = pltpu.roll(turned[:, 128 * k : 128 * k + 128], 96 if side else 32, 1)
            arriving = line(19 + 5 * side + k)
            st[20 + 5 * side + k] = jnp.where(jnp.logical_and(moved, wall), back, arriving)
    lane = iota((ROWS, 128), 1)
    codes = jnp.where(lane < 18, codes, ranks(64, 128))
    nb[...] = codes
    to_right = ((lax.axis_index("wide") + lax.axis_index("core")) % 2) == 0
    for q in range(8):
        acc = jnp.zeros((ROWS, 128), F32)
        for k in range(4):
            if 4 * q + k >= ARRAYS:
                continue
            value = st[4 * q + k]
            half = jnp.where(to_right, pltpu.roll(value, 64, 1), pltpu.roll(value, 96, 1))
            half = pltpu.roll(half, 32 * k, 1) if k else half
            acc = jnp.where(lane // 32 == k, half, acc)
        xp[ROWS * q : ROWS * q + ROWS, :] = acc
    xp[ROWS * 8 : ROWS * 9, :] = codes


def start_kernel(st, nb, xg, fc_out, fluid, nbt, zp, f, fc, arriving):
    w = lax.axis_index("wide")
    lane = iota((ROWS, 128), 1)
    left, right = (w + 1) % 2, w % 2
    for i in range(ARRAYS):
        rows = slice(ROWS * (i // 4), ROWS * (i // 4) + ROWS)
        from_left = xg[left, 0, rows, :]
        from_right = xg[right, 1, rows, :]
        shift = (128 - 32 * (i % 4)) % 128
        from_left = pltpu.roll(from_left, shift, 1) if shift else from_left
        shift = (224 - 32 * (i % 4)) % 128
        from_right = pltpu.roll(from_right, shift, 1) if shift else from_right
        value = jnp.where(lane < 32, from_left, jnp.where(lane < 96, st[i], from_right))
        if i < 19:
            f[i] = value
        elif i == 19:
            fluid[...] = value
        else:
            arriving[i - 20] = value
    last = slice(ROWS * 8, ROWS * 9)
    tables = [xg[left, 0, last, :], nb[...], xg[right, 1, last, :]]
    codes = jnp.where(lane < 36, pltpu.roll(tables[1], 18, 1), pltpu.roll(tables[2], 36, 1))
    codes = jnp.where(lane < 18, tables[0], codes)
    codes = jnp.where(lane < 54, codes, -1.0)
    side = jnp.zeros((ROWS, 128), jnp.int32)
    for j in range(18):
        if VELOCITY[j + 1][0]:
            side = jnp.where(lane % 18 == j, VELOCITY[j + 1][0], side)
    wanted = jnp.where(codes >= 0.0, codes - ((1 + side) * SLOTS).astype(F32), -1.0)
    slab = (lane // 18 + side)[0:8]
    done = jnp.full((ROWS, 128), -1.0, F32)
    for slot in range(SLOTS):
        value = jnp.full((8, 128), -1.0, F32)
        for g in range(3):
            value = jnp.where(slab == g, tables[g][0:8, 64 + slot : 65 + slot], value)
        value = jnp.concatenate([value] * (ROWS // 8), axis=0)
        done = jnp.where(wanted == float(slot), value, done)
    nbt[...] = jnp.where(lane < 54, done, tables[1])
    collide_all(f, fluid, fc)
    stream(fc, lambda k: arriving[k], lambda k: arriving[5 + k], nbt, f)
    collide_all(f, fluid, fc_out)
    planes_to_send(fc_out, zp)


def passing(fc, nbt, segments):
    lane = iota((ROWS, 128), 1)
    column, y = lane // 8, lane % 8
    segment = [column < 4, jnp.logical_and(column >= 4, column < 12), column >= 12]
    slots = iota((ROWS, ROWS), 1)
    table = nbt[...].astype(jnp.int32)
    known = {}

    def source_rows(g, d):
        if d == (0, 0, 0):
            return iota((ROWS, 128), 0)
        j = 18 * g + VELOCITY.index(d) - 1
        if j not in known:
            known[j] = jnp.broadcast_to(table[:, j : j + 1], (ROWS, 128))
        return known[j]

    def move(i, x, at_z):
        cx, cy, cz = VELOCITY[i]
        shift = (8 * cx + cy) % 128
        moved = pltpu.roll(x, shift, 1) if shift else x
        at_y = None
        if cy:
            at_y = y == (0 if cy > 0 else 7)
            moved = jnp.where(at_y, pltpu.roll(x, (8 * cx - 7 * cy) % 128, 1), moved)
        at_x = {}
        if cx > 0:
            at_x = {1: column == 4, 2: column == 12}
            edge = column == 0
        elif cx < 0:
            at_x = {0: column == 3, 1: column == 11}
            edge = column == 15
        parts = []
        for bx in (0, 1) if cx else (0,):
            for by in (0, 1) if cy else (0,):
                if not (bx or by or cz):
                    continue
                for g in segments:
                    if bx and g not in at_x:
                        continue
                    d = (-cx * bx, -cy * by, 0)
                    rows = source_rows(g, d)
                    if cz:
                        rows = jnp.where(at_z, source_rows(g, d[:2] + (-cz,)), rows)
                    mask = at_x[g] if bx else segment[g]
                    if by:
                        mask = jnp.logical_and(mask, at_y)
                    parts.append((mask, rows))
        if not parts:
            return moved
        picks = [(rows[:, :ROWS] == slots).astype(F32) for _, rows in parts]
        taken = choose(jnp.concatenate(picks, axis=0).astype(BF16), moved)
        bounced = fc[OPPOSITE[i]]
        out = moved
        for n, (mask, rows) in enumerate(parts):
            value = jnp.where(rows >= 0, taken[ROWS * n : ROWS * n + ROWS], bounced)
            out = jnp.where(mask, value, out)
        if cx:
            out = jnp.where(edge, bounced, out)
        return out

    return move


def stream(fc, from_below, from_above, nbt, f):
    z = lax.axis_index("z")
    move = passing(fc, nbt, (0, 1, 2))
    for i in range(19):
        if i in UP:
            f[i] = move(i, from_below(UP.index(i)), z == 0)
        elif i in DOWN:
            f[i] = move(i, from_above(DOWN.index(i)), z == PLANES - 1)
        else:
            f[i] = move(i, fc[i], None)


def exchanged(zg):
    z = lax.axis_index("z")
    below, above = (z + 1) % 2, z % 2
    return (
        lambda k: zg[below, 0, ROWS * k : ROWS * (k + 1), :],
        lambda k: zg[above, 1, ROWS * k : ROWS * (k + 1), :],
    )


def step_kernel(fc, zg, nbt, fluid, fc_out, zp, f):
    stream(fc, *exchanged(zg), nbt, f)
    collide_all(f, fluid, fc_out)
    planes_to_send(fc_out, zp)


def last_kernel(fc_in, zg, nbt, fluid, out, f, fc):
    stream(fc_in, *exchanged(zg), nbt, f)
    collide_all(f, fluid, fc)
    z = lax.axis_index("z")
    first = lax.axis_index("core") == 0
    lane = iota((ROWS, 128), 1)
    move = passing(fc, nbt, (1,))
    column, y = lane // 8, lane % 8
    bare = [fc[OPPOSITE[i]] for i in range(19)]
    up = [move(i, fc[i], z == PLANES - 1) for i in UP]
    down = [move(i, fc[i], z == 0) for i in DOWN]
    left = [move(i, fc[i], None) for i in FLAT] + up[:4]
    right = up[4:] + down
    right += [jnp.where(z == 0, bare[UP[k]], bare[DOWN[k]]) for k in range(5)]
    edge = jnp.where(column == 5, pltpu.roll(bare[13], 8, 1), pltpu.roll(bare[12], 120, 1))
    edge = jnp.where(column == 4, bare[11], jnp.where(column == 11, bare[14], edge))
    right.append(edge)
    edge = jnp.where(y == 1, pltpu.roll(bare[17], 1, 1), pltpu.roll(bare[16], 127, 1))
    right.append(jnp.where(y == 0, bare[15], jnp.where(y == 7, bare[18], edge)))
    left_rest = [WEIGHTS[i] for i in FLAT + UP[:4]]
    right_rest = [WEIGHTS[i] for i in UP[4:] + DOWN + UP] + [WEIGHTS[18]] * 2
    values = []
    for p in range(13):
        value = pltpu.roll(right[p], 32, 1)
        values.append(jnp.where(lane < 64, pltpu.roll(left[p], 96, 1), value))
    lane, slot = iota((SLOTS, 128), 1), iota((SLOTS, 128), 0)
    rank = jnp.broadcast_to(nbt[0:1, :], (SLOTS, 128))
    rank = jnp.sum(jnp.where(lane == 64 + slot, rank, 0.0), axis=1, keepdims=True)
    picks = rank == iota((SLOTS, ROWS), 1).astype(F32)
    spread = choose(picks.astype(F32).astype(BF16), jnp.concatenate(values, axis=1))
    filled = rank >= 0.0
    out[:, 32:40, :] = jnp.zeros((PLANES, 8, 128), F32)
    for p in range(13):
        rest = jnp.where(lane < 64, left_rest[p], right_rest[p])
        value = jnp.where(filled, spread[:, 128 * p : 128 * p + 128], rest)
        for n in range(PLANES):
            a, b = value[6 * n : 6 * n + 3], value[6 * n + 3 : 6 * n + 6]
            out[n, 3 * p : 3 * p + 3, :] = jnp.where(first, a, b)


def unpack_kernel(got, nbr, out, x, y):
    lane, row = iota((40, 128), 1), iota((40, 128), 0)
    k, n = iota((128, 128), 0), iota((128, 128), 1)
    picks = (n == (k % 16) * 8 + k // 16).astype(F32).astype(BF16)
    place = iota((HELD, 128), 1)
    here_z, here_y = place // 16, place % 8
    absent = [nbr[:, j : j + 1] < 0 for j in range(18)]
    x[...] = jnp.zeros_like(x)

    tiles = regroup([got[z] for z in range(PLANES)])
    for q in range(4):
        a, b = tiles[q], tiles[4 + q]
        a = jnp.where(row >= 27, pltpu.roll(a, 16, 1), a)
        falling = jnp.logical_and(row >= 3, row < 18)
        b = jnp.where(falling, pltpu.roll(b, 112, 1), jnp.where(row < 3, pltpu.roll(b, 16, 1), b))
        at_x, at_y = b[33:36], b[36:39]
        edges = {11: at_x, 14: at_x, 13: pltpu.roll(at_x, 120, 1), 12: pltpu.roll(at_x, 8, 1)}
        edges |= {15: at_y, 18: at_y, 17: pltpu.roll(at_y, 127, 1), 16: pltpu.roll(at_y, 1, 1)}
        here_x = 2 * q + (place % 16) // 8

        def missing(c):
            spots = []
            for size, here, top in zip(c, (here_x, here_y, here_z), (7, 7, 7)):
                spots.append(None if not size else here == (0 if size > 0 else top))
            found = jnp.zeros((HELD, 128), jnp.bool_)
            for flags in range(1, 8):
                across = [(flags >> s) & 1 for s in range(3)]
                if any(g and spot is None for g, spot in zip(across, spots)):
                    continue
                d = tuple(-size * g for size, g in zip(c, across))
                mask = jnp.broadcast_to(absent[VELOCITY.index(d) - 1], (HELD, 128))
                for g, spot in zip(across, spots):
                    if spot is not None:
                        mask = jnp.logical_and(mask, spot if g else jnp.logical_not(spot))
                found = jnp.logical_or(found, mask)
            return found

        for i in range(19):
            if i in UP or i in DOWN:
                k = (UP if i in UP else DOWN).index(i)
                bare = b[18 + 3 * k : 21 + 3 * k]
                if i in edges:
                    bare = jnp.where(here_z == (0 if i in UP else 7), bare, edges[i])
                j = 3 * k
                if i in DOWN:
                    value = b[3 + j : 6 + j]
                else:
                    value = a[27 + j : 30 + j] if k < 4 else b[0:3]
                value = jnp.where(missing(VELOCITY[i]), bare, value)
            else:
                j = 3 * FLAT.index(i)
                value = a[j : j + 3]
            x[64 * q + 3 * i : 64 * q + 3 * i + 3, :] = value
    y[0:256, :] = permute_lanes(x[...], picks)
    y[256:272, :] = jnp.zeros((16, 128), F32)
    for q in range(4):
        for t in range(HELD):
            out[t, :, 128 * q : 128 * q + 128] = y[pl.ds(64 * q + t, 19, stride=3), :]


def call(kernel, outs, scratch, *args, smem=0, limit=8 * 1024 * 1024):
    spaces = [pltpu.SMEM] * smem + [pltpu.VMEM] * (len(args) - smem)
    many = isinstance(outs, list)
    shapes = [jax.ShapeDtypeStruct(s, F32) for s in (outs if many else [outs])]
    specs = [pl.BlockSpec(memory_space=pltpu.VMEM) for _ in shapes]
    return pl.pallas_call(
        kernel,
        out_shape=shapes if many else shapes[0],
        in_specs=[pl.BlockSpec(memory_space=s) for s in spaces],
        out_specs=specs if many else specs[0],
        scratch_shapes=[pltpu.VMEM(s, F32) for s in scratch],
        compiler_params=pltpu.CompilerParams(vmem_limit_bytes=limit),
        interpret=INTERPRET,
    )(*args)


def solution(mesh):
    slabs, group = mesh.shape["wide"], mesh.shape["narrow"]
    chips = group // 2
    axes = ("wide", "z", "core")
    fine = Mesh(mesh.devices.reshape(slabs, chips, 2), axes)

    def pairs(count, other, index):
        return [
            [index(a, b, c), index((a + 1) % count, b, c)]
            for c in range(2)
            for a in range(c, count, 2)
            for b in range(other)
        ]

    wide_pairs = pairs(slabs, chips, lambda w, z, c: (w * chips + z) * 2 + c)
    z_pairs = pairs(chips, 1, lambda z, _, c: z * 2 + c)

    def both_sides(x, names, groups):
        y = lax.all_gather(x, names, axis_index_groups=groups)
        return lax.all_gather(y, "core")

    def shards(pops_in, keep_slot, send_slot, send_dest, neighbours, fluid):
        held = (keep_slot, send_slot, send_dest, neighbours, pops_in, fluid)
        if not INTERPRET:
            held = [pltpu.with_memory_space_constraint(x, pltpu.HBM) for x in held]
        packed = call(
            pack_kernel, (chips, PACK, 128), [(4 * PACK + 40, 128), (4 * PACK + 40, 128), (4 * 152 + 48, 128)],
            *held, smem=4,
        )
        planes = lax.all_to_all(packed, "z", 0, 0, tiled=True)
        got = lax.all_gather(planes, "core").reshape(group * PACK, 128)
        st, nb, xp = call(
            place_kernel, [(ARRAYS, ROWS, 128), (ROWS, 128), (9 * ROWS, 128)], [], got
        )
        xg = both_sides(xp, axes, wide_pairs)
        state = (19, ROWS, 128)
        sent = (5 * ROWS, 128)
        fc, wet, nbt, zp = call(
            start_kernel, [state, (ROWS, 128), (ROWS, 128), sent],
            [state, state, (10, ROWS, 128)], st, nb, xg,
        )
        for step in range(STEPS - 3):
            zg = both_sides(zp, ("z", "core"), z_pairs)
            fc, zp = call(step_kernel, [state, sent], [state], fc, zg, nbt, wet)
        zg = both_sides(zp, ("z", "core"), z_pairs)
        back = call(last_kernel, (chips, 40, 128), [state, state], fc, zg, nbt, wet)
        home = lax.all_to_all(back, "z", 0, 0, tiled=True)
        return call(unpack_kernel, (HELD, 19, 512), [(256, 128), (272, 128)], home, neighbours)

    placed = (P(axes, None, None), P(axes), P(axes), P(axes), P(axes, None), P(axes, None))
    return jax.shard_map(
        shards, mesh=fine, in_specs=placed, out_specs=P(axes, None, None), check_vma=False
    )
```

```python
import jax
import jax.numpy as jnp
from jax import lax
from jax.experimental import pallas as pl
from jax.experimental.pallas import tpu as pltpu
from jax.sharding import Mesh, PartitionSpec as P

STEPS = 4
HELD = 3
SLOTS = 48
ROWS = 32
PACK = 88
KIND = 15
TABLE_ROW = 59
ARRAYS = 30
PLANES = 8
INTERPRET = False

VELOCITY = [
    (0, 0, 0),
    (1, 0, 0), (-1, 0, 0), (0, 1, 0), (0, -1, 0), (0, 0, 1), (0, 0, -1),
    (1, 1, 0), (-1, -1, 0), (1, -1, 0), (-1, 1, 0),
    (1, 0, 1), (-1, 0, -1), (1, 0, -1), (-1, 0, 1),
    (0, 1, 1), (0, -1, -1), (0, 1, -1), (0, -1, 1),
]
WEIGHTS = [1.0 / 3.0] + [1.0 / 18.0] * 6 + [1.0 / 36.0] * 12
OPPOSITE = [0, 2, 1, 4, 3, 6, 5, 8, 7, 10, 9, 12, 11, 14, 13, 16, 15, 18, 17]
UP = [i for i in range(19) if VELOCITY[i][2] == 1]
FLAT = [i for i in range(19) if VELOCITY[i][2] == 0]
DOWN = [i for i in range(19) if VELOCITY[i][2] == -1]
NU_ZERO = 0.1
NU_LIMIT = 0.01
LAMBDA_TIME = 10.0
POWER_INDEX = 0.35
OMEGA_ZERO = 1.0 / (3.0 * NU_ZERO + 0.5)
SHEAR_SCALE = 2.1213203435596424
RATE_SCALE = (LAMBDA_TIME * SHEAR_SCALE * OMEGA_ZERO) ** 2
F32 = jnp.float32
BF16 = jnp.bfloat16


def iota(shape, dim):
    return lax.broadcasted_iota(jnp.int32, shape, dim)


def dot(a, b):
    return jnp.dot(a, b, preferred_element_type=F32)


def split(x):
    high = x.astype(BF16)
    rest = x - high.astype(F32)
    middle = rest.astype(BF16)
    low = (rest - middle.astype(F32)).astype(BF16)
    return high, middle, low


def choose(picks, x):
    n = x.shape[1]
    y = dot(picks, jnp.concatenate(split(x), axis=1))
    return y[:, :n] + y[:, n : 2 * n] + y[:, 2 * n :]


def permute_lanes(x, picks):
    m = x.shape[0]
    y = dot(jnp.concatenate(split(x), axis=0), picks)
    return y[:m] + y[m : 2 * m] + y[2 * m :]


def regroup(arrays):
    arrays = list(arrays)
    group = iota(arrays[0].shape, 1) // 16
    for s in (1, 2, 4):
        high = (group & s) != 0
        for i in range(8):
            if i & s:
                continue
            a, b = arrays[i], arrays[i | s]
            arrays[i] = jnp.where(high, pltpu.roll(b, 16 * s, 1), a)
            arrays[i | s] = jnp.where(high, b, pltpu.roll(a, 128 - 16 * s, 1))
    return arrays


def collide(f, fluid):
    def total(indices):
        out = None
        for i in indices:
            out = f[i] if out is None else out + f[i]
        return out

    rho = total(range(19))
    inverse = 1.0 / rho
    u = []
    for a in range(3):
        plus = total([i for i in range(19) if VELOCITY[i][a] == 1])
        minus = total([i for i in range(19) if VELOCITY[i][a] == -1])
        u.append((plus - minus) * inverse)
    base = 1.0 - 1.5 * (u[0] * u[0] + u[1] * u[1] + u[2] * u[2])
    excess = [f[0] - WEIGHTS[0] * rho * base]
    scaled = {}
    for i in range(1, 19, 2):
        c = VELOCITY[i]
        along = None
        for a in range(3):
            if c[a]:
                term = u[a]
                if along is None:
                    along = term if c[a] > 0 else -term
                else:
                    along = along + term if c[a] > 0 else along - term
        if WEIGHTS[i] not in scaled:
            scaled[WEIGHTS[i]] = WEIGHTS[i] * rho
        even = base + 4.5 * along * along
        odd = 3.0 * along
        excess.append(f[i] - scaled[WEIGHTS[i]] * (even + odd))
        excess.append(f[i + 1] - scaled[WEIGHTS[i]] * (even - odd))
    stress = None
    for a in range(3):
        for b in range(a, 3):
            part = None
            for i in range(1, 19):
                sign = VELOCITY[i][a] * VELOCITY[i][b]
                if sign:
                    if part is None:
                        part = excess[i] if sign > 0 else -excess[i]
                    else:
                        part = part + excess[i] if sign > 0 else part - excess[i]
            square = part * part if a == b else 2.0 * (part * part)
            stress = square if stress is None else stress + square
    grown = 1.0 + RATE_SCALE * stress * inverse * inverse
    thinned = jnp.exp(((POWER_INDEX - 1.0) / 2.0) * jnp.log(grown))
    viscosity = NU_LIMIT + (NU_ZERO - NU_LIMIT) * thinned
    rate = 1.0 / (3.0 * viscosity + 0.5)
    wet = fluid == 1.0
    return [jnp.where(wet, f[i] - rate * excess[i], f[OPPOSITE[i]]) for i in range(19)]


def collide_all(f_ref, fluid_ref, fc_ref):
    for g in range(ROWS // 8):
        rows = slice(8 * g, 8 * g + 8)
        done = collide([f_ref[i, rows, :] for i in range(19)], fluid_ref[rows, :])
        for i in range(19):
            fc_ref[i, rows, :] = done[i]


def planes_to_send(fc_ref, zp_ref):
    z = lax.axis_index("z")
    up = ((z + lax.axis_index("core")) % 2) == 0
    for k in range(5):
        @pl.when(up)
        def _():
            zp_ref[ROWS * k : ROWS * (k + 1), :] = fc_ref[UP[k]]

        @pl.when(jnp.logical_not(up))
        def _():
            zp_ref[ROWS * k : ROWS * (k + 1), :] = fc_ref[DOWN[k]]


def pack_kernel(keep, send, dest, nbr, pops, fluid, out, xa, xb, raw):
    xa[...] = jnp.zeros_like(xa)
    xb[...] = jnp.zeros_like(xb)
    raw[...] = jnp.ones_like(raw)
    for s in range(5):
        slot = jnp.maximum(keep[s] if s < HELD else send[s - HELD], 0)
        for q in range(4):
            block = pops[slot, :, 128 * q : 128 * q + 128]
            r = PACK * q + KIND * s
            xa[r : r + 15, :] = block[0:15]
            xb[r : r + 4, :] = block[15:19]
            raw[pl.ds(152 * q + s, 19, stride=8), :] = block
    walls = jnp.concatenate([fluid[...].astype(F32), jnp.ones((8 - HELD, 512), F32)], axis=0)
    slots = jnp.full((8, 128), -1, jnp.int32)
    for s in range(5):
        slot = keep[s] if s < HELD else send[s - HELD]
        slots = jnp.where(iota((8, 128), 0) == s, slot, slots)
    for q in range(4):
        wall = walls[:, 128 * q : 128 * q + 128]
        r = PACK * q
        xb[pl.ds(r + 14, HELD, stride=KIND), :] = wall[0:HELD]
        xa[r + 85 : r + 88, :] = wall[0:HELD]
        xb[r + 85 : r + 88, :] = wall[0:HELD]
        own = [raw[152 * q + 8 * i : 152 * q + 8 * i + 8, :] for i in range(19)]
        done = collide([jnp.where(slots >= 0, own[i], WEIGHTS[i]) for i in range(19)], wall)
        for k in range(5):
            xa[pl.ds(r + 75 + k, 2, stride=5), :] = own[OPPOSITE[UP[k]]][HELD : HELD + 2]
            xb[pl.ds(r + 75 + k, 2, stride=5), :] = own[OPPOSITE[DOWN[k]]][HELD : HELD + 2]
            xb[pl.ds(r + 4 + k, 5, stride=KIND), :] = done[UP[k]][0:5]
            xb[pl.ds(r + 9 + k, 5, stride=KIND), :] = done[DOWN[k]][0:5]
    k, n = iota((128, 128), 0), iota((128, 128), 1)
    picks = (n == (k % 8) * 16 + k // 8).astype(F32).astype(BF16)
    y = permute_lanes(jnp.concatenate([xa[0 : 4 * PACK, :], xb[0 : 4 * PACK, :]], axis=0), picks)
    lane, row = iota((PACK, 128), 1), iota((PACK, 128), 0)
    kind, late = row % KIND, row >= 75
    rising = jnp.logical_and(jnp.logical_and(kind >= 4, kind < 9), jnp.logical_not(late))
    falling = jnp.logical_or(jnp.logical_and(kind >= 9, kind < 14), late)
    second = lane >= 64
    rising = jnp.logical_or(
        jnp.logical_and(second, rising), jnp.logical_and(late, jnp.logical_not(second))
    )
    falling = jnp.logical_and(second, falling)
    parts = regroup([y[PACK * part : PACK * part + PACK] for part in range(8)])
    values = [keep[t] for t in range(3)] + [dest[j] for j in range(2)]
    values = list(enumerate(values)) + [
        (10 + 18 * t + j, nbr[t, j]) for t in range(3) for j in range(18)
    ]
    line = iota((8, 128), 1)
    table = jnp.zeros((8, 128), jnp.int32)
    for place, value in values:
        table = jnp.where(line == 64 + place, value, table)
    table = jnp.concatenate([table.astype(F32)] * (PACK // 8), axis=0)
    marked = jnp.logical_and(row == TABLE_ROW, lane >= 64)
    for z in range(PLANES):
        value = jnp.where(falling, parts[(z + 1) % PLANES], parts[z])
        value = jnp.where(rising, parts[(z - 1) % PLANES], value)
        out[z] = jnp.where(marked, table, value)


def place_kernel(got, st, nb, xp):
    def of_all(row):
        return got[pl.ds(row, 16, stride=PACK), :]

    tables = of_all(TABLE_ROW)
    row16 = iota((SLOTS, 16), 0)
    lane16 = iota((SLOTS, 16), 1)
    m16 = row16 // 3
    whose = (m16 % 2) * 8 + m16 // 2
    picks = (lane16 == whose).astype(F32).astype(BF16)
    mine = dot(picks, tables.astype(BF16))
    lane, row = iota((SLOTS, 128), 1), iota((SLOTS, 128), 0)
    t = row % 3
    kept = jnp.sum(jnp.where(lane == 64 + t, mine, 0.0), axis=1, keepdims=True)
    eye = iota((16, 16), 0) == iota((16, 16), 1)
    lane_t = iota((16, 128), 1)
    found = jnp.full((SLOTS, 1), -1.0, F32)
    for j in range(2):
        column = jnp.sum(jnp.where(lane_t == 67 + j, tables, 0.0), axis=1, keepdims=True)
        diagonal = jnp.where(eye, column, 0.0).astype(BF16)
        targets = dot(jnp.ones((SLOTS, 16), BF16), diagonal)
        hit = targets == row16.astype(F32)
        where_from = jnp.where(hit, lane16 + 16 * (HELD + j) + 1, 0)
        found = found + jnp.sum(where_from.astype(F32), axis=1, keepdims=True)
    row1 = iota((SLOTS, 1), 0)
    m1 = row1 // 3
    own = ((m1 % 2) * 8 + m1 // 2 + (row1 % 3) * 16).astype(F32)
    source = jnp.where(kept >= 0.0, own, found)
    occupied = (source >= 0.0).astype(F32)
    ones = jnp.ones((ROWS, SLOTS), BF16)

    def ranks(first, width):
        r, slot = iota((SLOTS, width), 0), iota((SLOTS, width), 1) - first
        earlier = dot(ones, jnp.where(r < slot, occupied, 0.0).astype(BF16))
        full = dot(ones, jnp.where(r == slot, occupied, 0.0).astype(BF16))
        return jnp.where(full > 0.5, earlier, -1.0)

    rank = ranks(0, SLOTS)
    picks = (rank == iota((ROWS, SLOTS), 0).astype(F32)).astype(F32).astype(BF16)
    codes = jnp.zeros((SLOTS, 128), F32)
    for k in range(3):
        codes = jnp.where(t == k, pltpu.roll(mine, (128 - 74 - 18 * k) % 128, 1), codes)
    codes = jnp.where(lane == 18, source, codes)
    codes = jnp.where(lane == 19, own, codes)
    codes = choose(picks, codes)
    source, own = codes[:, 18:19], codes[:, 19:20]

    def one_hot(index, width):
        return (iota((ROWS, width), 1).astype(F32) == index).astype(F32).astype(BF16)

    def stacked(first, step, count):
        return jnp.concatenate([of_all(first + step * s) for s in range(count)], axis=0)

    lines = jnp.concatenate([stacked(p, KIND, 5) for p in range(KIND)], axis=1)
    lines = choose(one_hot(source, 80), lines)
    turned = jnp.concatenate([stacked(75 + k, 5, 2) for k in range(5)], axis=1)
    turned = choose(one_hot(source - 48.0, 32), turned)
    walls = jnp.concatenate([stacked(14, KIND, 3), stacked(85, 1, 3)], axis=1)
    walls = choose(one_hot(own, SLOTS), walls)

    def line(n):
        value = lines[:, 128 * (n % KIND) : 128 * (n % KIND) + 128]
        return pltpu.roll(value, 32 if n < KIND else 96, 1)

    for i in range(19):
        st[i] = line(i)
    st[19] = pltpu.roll(walls[:, 0:128], 96, 1)
    moved = source >= 48.0
    for side in range(2):
        wall = pltpu.roll(walls[:, 128:256], 96 if side else 32, 1) != 1.0
        for k in range(5):
            back = pltpu.roll(turned[:, 128 * k : 128 * k + 128], 96 if side else 32, 1)
            arriving = line(19 + 5 * side + k)
            st[20 + 5 * side + k] = jnp.where(jnp.logical_and(moved, wall), back, arriving)
    lane = iota((ROWS, 128), 1)
    codes = jnp.where(lane < 18, codes, ranks(64, 128))
    nb[...] = codes
    to_right = ((lax.axis_index("wide") + lax.axis_index("core")) % 2) == 0
    for q in range(8):
        halves = []
        for first in (64, 32):
            acc = jnp.zeros((ROWS, 128), F32)
            for k in range(min(4, ARRAYS - 4 * q)):
                shift = (32 * k - first) % 128
                value = st[4 * q + k]
                value = pltpu.roll(value, shift, 1) if shift else value
                acc = jnp.where(lane // 32 == k, value, acc)
            halves.append(acc)
        xp[ROWS * q : ROWS * q + ROWS, :] = jnp.where(to_right, halves[0], halves[1])
    xp[ROWS * 8 : ROWS * 9, :] = codes


def start_kernel(st, nb, xg, fc_out, fluid, nbt, zp, f, fc, arriving):
    w = lax.axis_index("wide")
    lane = iota((ROWS, 128), 1)
    left, right = (w + 1) % 2, w % 2
    for i in range(ARRAYS):
        rows = slice(ROWS * (i // 4), ROWS * (i // 4) + ROWS)
        from_left = xg[left, 0, rows, :]
        from_right = xg[right, 1, rows, :]
        shift = (128 - 32 * (i % 4)) % 128
        from_left = pltpu.roll(from_left, shift, 1) if shift else from_left
        shift = (224 - 32 * (i % 4)) % 128
        from_right = pltpu.roll(from_right, shift, 1) if shift else from_right
        value = jnp.where(lane < 32, from_left, jnp.where(lane < 96, st[i], from_right))
        if i < 19:
            f[i] = value
        elif i == 19:
            fluid[...] = value
        else:
            arriving[i - 20] = value
    last = slice(ROWS * 8, ROWS * 9)
    tables = [xg[left, 0, last, :], nb[...], xg[right, 1, last, :]]
    codes = jnp.where(lane < 36, pltpu.roll(tables[1], 18, 1), pltpu.roll(tables[2], 36, 1))
    codes = jnp.where(lane < 18, tables[0], codes)
    codes = jnp.where(lane < 54, codes, -1.0)
    side = jnp.zeros((ROWS, 128), jnp.int32)
    for j in range(18):
        if VELOCITY[j + 1][0]:
            side = jnp.where(lane % 18 == j, VELOCITY[j + 1][0], side)
    wanted = jnp.where(codes >= 0.0, codes - ((1 + side) * SLOTS).astype(F32), -1.0)
    slab = (lane // 18 + side)[0:8]
    done = jnp.full((ROWS, 128), -1.0, F32)
    for slot in range(SLOTS):
        value = jnp.full((8, 128), -1.0, F32)
        for g in range(3):
            value = jnp.where(slab == g, tables[g][0:8, 64 + slot : 65 + slot], value)
        value = jnp.concatenate([value] * (ROWS // 8), axis=0)
        done = jnp.where(wanted == float(slot), value, done)
    nbt[...] = jnp.where(lane < 54, done, tables[1])
    collide_all(f, fluid, fc)
    stream(fc, lambda k: arriving[k], lambda k: arriving[5 + k], nbt, f)
    collide_all(f, fluid, fc_out)
    planes_to_send(fc_out, zp)


def passing(fc, nbt, segments):
    lane = iota((ROWS, 128), 1)
    column, y = lane // 8, lane % 8
    segment = [column < 4, jnp.logical_and(column >= 4, column < 12), column >= 12]
    slots = iota((ROWS, ROWS), 1)
    table = nbt[...].astype(jnp.int32)
    known = {}

    def source_rows(g, d):
        if d == (0, 0, 0):
            return iota((ROWS, 128), 0)
        j = 18 * g + VELOCITY.index(d) - 1
        if j not in known:
            known[j] = jnp.broadcast_to(table[:, j : j + 1], (ROWS, 128))
        return known[j]

    def move(i, x, at_z):
        cx, cy, cz = VELOCITY[i]
        shift = (8 * cx + cy) % 128
        moved = pltpu.roll(x, shift, 1) if shift else x
        at_y = None
        if cy:
            at_y = y == (0 if cy > 0 else 7)
            moved = jnp.where(at_y, pltpu.roll(x, (8 * cx - 7 * cy) % 128, 1), moved)
        at_x = {}
        if cx > 0:
            at_x = {1: column == 4, 2: column == 12}
            edge = column == 0
        elif cx < 0:
            at_x = {0: column == 3, 1: column == 11}
            edge = column == 15
        parts = []
        for bx in (0, 1) if cx else (0,):
            for by in (0, 1) if cy else (0,):
                if not (bx or by or cz):
                    continue
                for g in segments:
                    if bx and g not in at_x:
                        continue
                    d = (-cx * bx, -cy * by, 0)
                    rows = source_rows(g, d)
                    if cz:
                        rows = jnp.where(at_z, source_rows(g, d[:2] + (-cz,)), rows)
                    mask = at_x[g] if bx else segment[g]
                    if by:
                        mask = jnp.logical_and(mask, at_y)
                    parts.append((mask, rows))
        if not parts:
            return moved
        picks = [(rows[:, :ROWS] == slots).astype(F32) for _, rows in parts]
        taken = choose(jnp.concatenate(picks, axis=0).astype(BF16), moved)
        bounced = fc[OPPOSITE[i]]
        out = moved
        for n, (mask, rows) in enumerate(parts):
            value = jnp.where(rows >= 0, taken[ROWS * n : ROWS * n + ROWS], bounced)
            out = jnp.where(mask, value, out)
        if cx:
            out = jnp.where(edge, bounced, out)
        return out

    return move


def stream(fc, from_below, from_above, nbt, f):
    z = lax.axis_index("z")
    move = passing(fc, nbt, (0, 1, 2))
    for i in range(19):
        if i in UP:
            f[i] = move(i, from_below(UP.index(i)), z == 0)
        elif i in DOWN:
            f[i] = move(i, from_above(DOWN.index(i)), z == PLANES - 1)
        else:
            f[i] = move(i, fc[i], None)


def exchanged(zg):
    z = lax.axis_index("z")
    below, above = (z + 1) % 2, z % 2
    return (
        lambda k: zg[below, 0, ROWS * k : ROWS * (k + 1), :],
        lambda k: zg[above, 1, ROWS * k : ROWS * (k + 1), :],
    )


def step_kernel(fc, zg, nbt, fluid, fc_out, zp, f):
    stream(fc, *exchanged(zg), nbt, f)
    collide_all(f, fluid, fc_out)
    planes_to_send(fc_out, zp)


def last_kernel(fc_in, zg, nbt, fluid, out, f, fc):
    stream(fc_in, *exchanged(zg), nbt, f)
    collide_all(f, fluid, fc)
    z = lax.axis_index("z")
    first = lax.axis_index("core") == 0
    lane = iota((ROWS, 128), 1)
    move = passing(fc, nbt, (1,))
    column, y = lane // 8, lane % 8
    bare = [fc[OPPOSITE[i]] for i in range(19)]
    up = [move(i, fc[i], z == PLANES - 1) for i in UP]
    down = [move(i, fc[i], z == 0) for i in DOWN]
    left = [move(i, fc[i], None) for i in FLAT] + up[:4]
    right = up[4:] + down
    right += [jnp.where(z == 0, bare[UP[k]], bare[DOWN[k]]) for k in range(5)]
    edge = jnp.where(column == 5, pltpu.roll(bare[13], 8, 1), pltpu.roll(bare[12], 120, 1))
    edge = jnp.where(column == 4, bare[11], jnp.where(column == 11, bare[14], edge))
    right.append(edge)
    edge = jnp.where(y == 1, pltpu.roll(bare[17], 1, 1), pltpu.roll(bare[16], 127, 1))
    right.append(jnp.where(y == 0, bare[15], jnp.where(y == 7, bare[18], edge)))
    left_rest = [WEIGHTS[i] for i in FLAT + UP[:4]]
    right_rest = [WEIGHTS[i] for i in UP[4:] + DOWN + UP] + [WEIGHTS[18]] * 2
    values = []
    for p in range(13):
        value = pltpu.roll(right[p], 32, 1)
        values.append(jnp.where(lane < 64, pltpu.roll(left[p], 96, 1), value))
    lane, slot = iota((SLOTS, 128), 1), iota((SLOTS, 128), 0)
    rank = jnp.broadcast_to(nbt[0:1, :], (SLOTS, 128))
    rank = jnp.sum(jnp.where(lane == 64 + slot, rank, 0.0), axis=1, keepdims=True)
    picks = rank == iota((SLOTS, ROWS), 1).astype(F32)
    spread = choose(picks.astype(F32).astype(BF16), jnp.concatenate(values, axis=1))
    filled = rank >= 0.0
    out[:, 32:40, :] = jnp.zeros((PLANES, 8, 128), F32)
    for p in range(13):
        rest = jnp.where(lane < 64, left_rest[p], right_rest[p])
        value = jnp.where(filled, spread[:, 128 * p : 128 * p + 128], rest)
        for n in range(PLANES):
            a, b = value[6 * n : 6 * n + 3], value[6 * n + 3 : 6 * n + 6]
            out[n, 3 * p : 3 * p + 3, :] = jnp.where(first, a, b)


def unpack_kernel(got, nbr, out, x, y):
    lane, row = iota((40, 128), 1), iota((40, 128), 0)
    k, n = iota((128, 128), 0), iota((128, 128), 1)
    picks = (n == (k % 16) * 8 + k // 16).astype(F32).astype(BF16)
    place = iota((HELD, 128), 1)
    here_z, here_y = place // 16, place % 8
    absent = [nbr[:, j : j + 1] < 0 for j in range(18)]
    x[...] = jnp.zeros_like(x)

    tiles = regroup([got[z] for z in range(PLANES)])
    for q in range(4):
        a, b = tiles[q], tiles[4 + q]
        a = jnp.where(row >= 27, pltpu.roll(a, 16, 1), a)
        falling = jnp.logical_and(row >= 3, row < 18)
        b = jnp.where(falling, pltpu.roll(b, 112, 1), jnp.where(row < 3, pltpu.roll(b, 16, 1), b))
        at_x, at_y = b[33:36], b[36:39]
        edges = {11: at_x, 14: at_x, 13: pltpu.roll(at_x, 120, 1), 12: pltpu.roll(at_x, 8, 1)}
        edges |= {15: at_y, 18: at_y, 17: pltpu.roll(at_y, 127, 1), 16: pltpu.roll(at_y, 1, 1)}
        here_x = 2 * q + (place % 16) // 8

        def missing(c):
            spots = []
            for size, here, top in zip(c, (here_x, here_y, here_z), (7, 7, 7)):
                spots.append(None if not size else here == (0 if size > 0 else top))
            found = jnp.zeros((HELD, 128), jnp.bool_)
            for flags in range(1, 8):
                across = [(flags >> s) & 1 for s in range(3)]
                if any(g and spot is None for g, spot in zip(across, spots)):
                    continue
                d = tuple(-size * g for size, g in zip(c, across))
                mask = jnp.broadcast_to(absent[VELOCITY.index(d) - 1], (HELD, 128))
                for g, spot in zip(across, spots):
                    if spot is not None:
                        mask = jnp.logical_and(mask, spot if g else jnp.logical_not(spot))
                found = jnp.logical_or(found, mask)
            return found

        for i in range(19):
            if i in UP or i in DOWN:
                k = (UP if i in UP else DOWN).index(i)
                bare = b[18 + 3 * k : 21 + 3 * k]
                if i in edges:
                    bare = jnp.where(here_z == (0 if i in UP else 7), bare, edges[i])
                j = 3 * k
                if i in DOWN:
                    value = b[3 + j : 6 + j]
                else:
                    value = a[27 + j : 30 + j] if k < 4 else b[0:3]
                value = jnp.where(missing(VELOCITY[i]), bare, value)
            else:
                j = 3 * FLAT.index(i)
                value = a[j : j + 3]
            x[64 * q + 3 * i : 64 * q + 3 * i + 3, :] = value
    y[0:256, :] = permute_lanes(x[...], picks)
    y[256:272, :] = jnp.zeros((16, 128), F32)
    for q in range(4):
        for t in range(HELD):
            out[t, :, 128 * q : 128 * q + 128] = y[pl.ds(64 * q + t, 19, stride=3), :]


def call(kernel, outs, scratch, *args, smem=0, limit=8 * 1024 * 1024):
    spaces = [pltpu.SMEM] * smem + [pltpu.VMEM] * (len(args) - smem)
    many = isinstance(outs, list)
    shapes = [jax.ShapeDtypeStruct(s, F32) for s in (outs if many else [outs])]
    specs = [pl.BlockSpec(memory_space=pltpu.VMEM) for _ in shapes]
    return pl.pallas_call(
        kernel,
        out_shape=shapes if many else shapes[0],
        in_specs=[pl.BlockSpec(memory_space=s) for s in spaces],
        out_specs=specs if many else specs[0],
        scratch_shapes=[pltpu.VMEM(s, F32) for s in scratch],
        compiler_params=pltpu.CompilerParams(vmem_limit_bytes=limit),
        interpret=INTERPRET,
    )(*args)


def solution(mesh):
    slabs, group = mesh.shape["wide"], mesh.shape["narrow"]
    chips = group // 2
    axes = ("wide", "z", "core")
    fine = Mesh(mesh.devices.reshape(slabs, chips, 2), axes)

    def pairs(count, other, index):
        return [
            [index(a, b, c), index((a + 1) % count, b, c)]
            for c in range(2)
            for a in range(c, count, 2)
            for b in range(other)
        ]

    wide_pairs = pairs(slabs, chips, lambda w, z, c: (w * chips + z) * 2 + c)
    z_pairs = pairs(chips, 1, lambda z, _, c: z * 2 + c)

    def both_sides(x, names, groups):
        y = lax.all_gather(x, names, axis_index_groups=groups)
        return lax.all_gather(y, "core")

    def shards(pops_in, keep_slot, send_slot, send_dest, neighbours, fluid):
        held = (keep_slot, send_slot, send_dest, neighbours, pops_in, fluid)
        if not INTERPRET:
            held = [pltpu.with_memory_space_constraint(x, pltpu.HBM) for x in held]
        packed = call(
            pack_kernel, (chips, PACK, 128), [(4 * PACK + 40, 128), (4 * PACK + 40, 128), (4 * 152 + 48, 128)],
            *held, smem=4,
        )
        planes = lax.all_to_all(packed, "z", 0, 0, tiled=True)
        got = lax.all_gather(planes, "core").reshape(group * PACK, 128)
        st, nb, xp = call(
            place_kernel, [(ARRAYS, ROWS, 128), (ROWS, 128), (9 * ROWS, 128)], [], got
        )
        xg = both_sides(xp, axes, wide_pairs)
        state = (19, ROWS, 128)
        sent = (5 * ROWS, 128)
        fc, wet, nbt, zp = call(
            start_kernel, [state, (ROWS, 128), (ROWS, 128), sent],
            [state, state, (10, ROWS, 128)], st, nb, xg,
        )
        for step in range(STEPS - 3):
            zg = both_sides(zp, ("z", "core"), z_pairs)
            fc, zp = call(step_kernel, [state, sent], [state], fc, zg, nbt, wet)
        zg = both_sides(zp, ("z", "core"), z_pairs)
        back = call(last_kernel, (chips, 40, 128), [state, state], fc, zg, nbt, wet)
        home = lax.all_to_all(back, "z", 0, 0, tiled=True)
        return call(unpack_kernel, (HELD, 19, 512), [(256, 128), (272, 128)], home, neighbours)

    placed = (P(axes, None, None), P(axes), P(axes), P(axes), P(axes, None), P(axes, None))
    return jax.shard_map(
        shards, mesh=fine, in_specs=placed, out_specs=P(axes, None, None), check_vma=False
    )
```
